32 devices in a mesh: wide: 8 (over z, y), narrow: 4 (over x, core).
Axes of the slice: x: 2, y: 2, z: 4, core: 2. Of those that a mesh axis runs over, the one named last changes fastest.
Arguments:
- tokens: bfloat16 [32, 256, 1024], P(('wide', 'narrow')), may hold values from -6 to 6
- doc_ids: int32 [32, 256], P(('wide', 'narrow')), may hold values from 0 to 7, never falling along the last dimension, each value on 1 to 128 neighbouring positions
- attn_gain: float32 [1024], P(('wide', 'narrow')), may hold values from 0.5 to 1.5
- mixer_in: float32 [1024, 6144], P(('wide', 'narrow')), may hold values from -0.1875 to 0.1875
- mixer_small: float32 [1024, 24], P(('wide', 'narrow')), may hold values from -0.375 to 0.375
- conv_weight: float32 [5120, 4], P(('wide', 'narrow')), may hold values from -3 to 3
- decay_log: float32 [8], replicated, may hold values from -4 to 1
- decay_bias: float32 [8], replicated, may hold values from -4 to 0
- out_gain: float32 [128], replicated, may hold values from 0.5 to 1.5
- mixer_out: float32 [1024, 1024], P(None, ('wide', 'narrow')), may hold values from -0.375 to 0.375
- ffn_gain: float32 [1024], P(('wide', 'narrow')), may hold values from 0.5 to 1.5
- ffn_in: float32 [1024, 5632], P(('wide', 'narrow')), may hold values from -0.1875 to 0.1875
- ffn_out: float32 [2816, 1024], P(None, ('wide', 'narrow')), may hold values from -0.21875 to 0.21875
- out_grad: bfloat16 [32, 256, 1024], P(('wide', 'narrow')), may hold values from -6 to 6
Outputs:
- outputs: bfloat16 [32, 256, 1024], P(('wide', 'narrow'))
- input_grad: bfloat16 [32, 256, 1024], P(('wide', 'narrow'))
- attn_gain_grad: float32 [1024], P(('wide', 'narrow'))
- mixer_in_grad: float32 [1024, 6144], P(('wide', 'narrow'))
- mixer_small_grad: float32 [1024, 24], P(('wide', 'narrow'))
- conv_grad: float32 [5120, 4], P(('wide', 'narrow'))
- decay_log_grad: float32 [8], replicated
- decay_bias_grad: float32 [8], replicated
- out_gain_grad: float32 [128], replicated
- mixer_out_grad: float32 [1024, 1024], P(None, ('wide', 'narrow'))
- ffn_gain_grad: float32 [1024], P(('wide', 'narrow'))
- ffn_in_grad: float32 [1024, 5632], P(('wide', 'narrow'))
- ffn_out_grad: float32 [2816, 1024], P(None, ('wide', 'narrow'))
The draws below stay inside these ranges and needn't reach their ends.
Inputs may be any that keep to these rules, and one draw needn't show every extreme that they name: `doc_ids`: along each row the numbers never fall; equal numbers form one document of at most 128 positions, and some document of each draw has exactly that many.
All inputs are finite; a program needn't handle non-finite values.
Results may differ from the reference program's by a relative error of at most 0.01.
The reference program's roundings to bfloat16 on the way count: a program that leaves them out, or rounds other values in their place, can miss the bound.
Values may be sent and summed in bfloat16 or wider, within the bound.
A program may use at most 256 MiB of HBM per device.

```python
import math
import jax
import jax.numpy as jnp
import numpy as np
from jax import lax

D = 1024
H = 8
DH = 128
FF = 2816
KCONV = 4
GROUP = 64
DOCS = 8
SEQ_LEN = 256
ROWS = 32
INNER = 1024
CH = 5120
IN_COLS = 6144
SMALL_COLS = 24


def steps_of(own_key, dims, cuts, smallest, largest):
    loudness, own = 1.0, jax.random.fold_in(own_key, 6)
    for dim, blocks in cuts:
        heights = jnp.exp(jax.random.uniform(jax.random.fold_in(own, dim), (blocks,), jnp.float32, smallest / len(cuts), largest / len(cuts)))
        loudness = loudness * jnp.repeat(heights, dims[dim] // blocks).reshape([-1 if axis == dim else 1 for axis in range(len(dims))])
    return loudness


def split_up(number_of, total, reach, skew):
    portions = [(1 << 20) // math.isqrt(standing ** skew) + 1 for standing in range(2, number_of + 1)]
    spare, counts = total - reach - (number_of - 1), [1] * (number_of - 1)
    while spare > 0:
        candidates = [i for i in range(number_of - 1) if counts[i] < reach]
        whole, remaining = sum([portions[i] for i in candidates]), spare
        for i in candidates:
            addition = min(reach - counts[i], max(1, remaining * portions[i] // whole), spare)
            counts[i] = counts[i] + addition
            spare = spare - addition
    return np.array([reach] + counts)


def ragged_sizes(own_key, amount, total, bound, skew):
    if amount == 2:
        one = jax.random.randint(own_key, (), max(1, total - bound), min(bound, total - 1) + 1)
        return jnp.stack([one, total - one])
    tallies = jnp.asarray(split_up(amount, total, bound, skew), jnp.int32)
    pairs = (amount - 1) // 2
    giver, receiver = tallies[1:1 + 2 * pairs:2], tallies[2:2 + 2 * pairs:2]
    room = jnp.minimum(giver - 1, bound - receiver)
    shifted = jax.random.randint(jax.random.fold_in(own_key, 1), (pairs,), 0, 1 << 20) % (room + 1)
    tallies = tallies.at[1:1 + 2 * pairs:2].set(giver - shifted).at[2:2 + 2 * pairs:2].set(receiver + shifted)
    return tallies[jax.random.permutation(jax.random.fold_in(own_key, 2), amount)]


def noise(stream_key, extent, scale, most, cuts=(), kind=jnp.bfloat16):
    array = jax.random.normal(stream_key, extent, jnp.float32) * scale
    if len(cuts) > 0:
        array = steps_of(stream_key, extent, cuts, -0.22, 0.18) * array
    return jnp.clip(array, min=-most, max=most).astype(kind)


def setup_inputs(seed: int = 0) -> dict:
    seeds = jax.random.split(jax.random.key(seed), 15)
    return {
        "tokens": noise(seeds[0], (ROWS, SEQ_LEN, D), 1.0, 6.0, ((0, 32),)),
        "doc_ids": jax.vmap(lambda own: jnp.searchsorted(jnp.cumsum(ragged_sizes(own, DOCS, SEQ_LEN, SEQ_LEN // 2, 2)), jnp.arange(SEQ_LEN), side="right"))(jax.random.split(seeds[1], ROWS)).reshape((ROWS, SEQ_LEN)).astype(jnp.int32),
        "attn_gain": jnp.clip(1.0 + 0.1 * jax.random.normal(seeds[2], (D,), jnp.float32), 0.5, 1.5),
        "mixer_in": noise(seeds[3], (D, IN_COLS), D ** -0.5, 0.1875, ((0, 32),), jnp.float32),
        "mixer_small": noise(seeds[4], (D, SMALL_COLS), (D // 4) ** -0.5, 0.375, ((0, 32),), jnp.float32),
        "conv_weight": noise(seeds[5], (CH, KCONV), KCONV ** -0.5, 3.0, ((0, 32),), jnp.float32),
        "decay_log": jnp.clip(jax.random.uniform(seeds[6], (H,), jnp.float32, -4.0, 1.0), -4.0, 1.0),
        "decay_bias": jnp.clip(jax.random.uniform(seeds[7], (H,), jnp.float32, -4.0, 0.0), -4.0, 0.0),
        "out_gain": jnp.clip(1.0 + 0.1 * jax.random.normal(seeds[8], (DH,), jnp.float32), 0.5, 1.5),
        "mixer_out": noise(seeds[9], (INNER, D), (INNER // 4) ** -0.5, 0.375, ((1, 32),), jnp.float32),
        "ffn_gain": jnp.clip(1.0 + 0.1 * jax.random.normal(seeds[10], (D,), jnp.float32), 0.5, 1.5),
        "ffn_in": noise(seeds[11], (D, 2 * FF), D ** -0.5, 0.1875, ((0, 32),), jnp.float32),
        "ffn_out": noise(seeds[12], (FF, D), (FF // 4) ** -0.5, 0.21875, ((1, 32),), jnp.float32),
        "out_grad": noise(seeds[13], (ROWS, SEQ_LEN, D), 1.0, 6.0, ((0, 32),)),
    }


norm_eps = 1e-06
highest = lax.Precision.HIGHEST

@jax.custom_vjp
def low(v):
    return lax.optimization_barrier(v.astype(jnp.bfloat16)).astype(jnp.float32)

@jax.custom_vjp
def low_back(v):
    return v

def low_keep(v):
    return (low(v), None)

def low_pass(kept, grad):
    return (grad,)

def back_keep(v):
    return (v, None)

def back_low(kept, grad):
    return (low(grad),)
low.defvjp(low_keep, low_pass)
low_back.defvjp(back_keep, back_low)

def rms_scale(inputs, gain_row):
    return inputs * lax.rsqrt(lax.optimization_barrier(jnp.mean(inputs * inputs, axis=-1, keepdims=True)) + norm_eps) * gain_row

def unit_rows(inputs):
    return inputs * lax.rsqrt(lax.optimization_barrier(jnp.sum(inputs * inputs, axis=-1, keepdims=True)) + norm_eps)

def group_step(carried, pieces):
    states, prev_doc = carried
    key_rows, values, queries, beta_rows, decays, doc_rows = pieces
    length = doc_rows.shape[0]
    cumulative = jnp.cumsum(decays, axis=1)
    row_index = lax.broadcasted_iota(jnp.int32, (length, length), 0)
    col_index = lax.broadcasted_iota(jnp.int32, (length, length), 1)
    same_doc = doc_rows[:, None] == doc_rows[None, :]
    causal = same_doc & (row_index >= col_index)
    strict = same_doc & (row_index > col_index)
    spread = cumulative[:, :, None] - cumulative[:, None, :]
    weights = jnp.where(causal, jnp.exp(jnp.where(causal, spread, 0.0)), 0.0)
    entering = jnp.where((doc_rows == prev_doc)[None, :], jnp.exp(cumulative), 0.0)
    key_key = jnp.einsum('hid,hjd->hij', key_rows, key_rows, precision=highest)
    lower_part = jnp.where(strict, beta_rows[:, :, None] * weights * key_key, 0.0)
    system = lower_part + jnp.eye(length, dtype=jnp.float32)
    key_state = jnp.einsum('hid,hde->hie', key_rows, states, precision=highest)
    target = beta_rows[:, :, None] * (values - entering[:, :, None] * key_state)
    updates = lax.linalg.triangular_solve(system, target, left_side=True, lower=True)
    query_key = jnp.einsum('hid,hjd->hij', queries, key_rows, precision=highest)
    query_state = jnp.einsum('hid,hde->hie', queries, states, precision=highest)
    outputs = entering[:, :, None] * query_state + jnp.einsum('hij,hje->hie', weights * query_key, updates, precision=highest)
    last_doc = doc_rows[length - 1]
    final_decay = cumulative[:, length - 1]
    tail_weight = jnp.where((doc_rows == last_doc)[None, :], jnp.exp(final_decay[:, None] - cumulative), 0.0)
    kept_decay = jnp.where(prev_doc == last_doc, jnp.exp(final_decay), 0.0)
    states = kept_decay[:, None, None] * states + jnp.einsum('hjd,hje->hde', key_rows * tail_weight[:, :, None], updates, precision=highest)
    return ((states, last_doc), outputs)

def arrange(source, blocks):
    shaped = source.reshape((blocks, GROUP) + source.shape[1:])
    return jnp.moveaxis(shaped, 1, 2)

def recurrence(queries, key_rows, values, beta_rows, decays, doc_ids):
    length, head_count, head_width = queries.shape
    step_count = key_rows.shape[1]
    sub_count = length * step_count
    blocks = sub_count // GROUP
    sub_keys = key_rows.reshape(sub_count, head_count, head_width)
    sub_values = values.reshape(sub_count, head_count, head_width)
    sub_queries = jnp.broadcast_to(queries[:, None], (length, step_count, head_count, head_width)).reshape(sub_count, head_count, head_width)
    sub_betas = beta_rows.reshape(sub_count, head_count)
    sub_decays = jnp.concatenate([decays[:, None], jnp.zeros((length, step_count - 1, head_count), jnp.float32)], axis=1).reshape(sub_count, head_count)
    sub_docs = jnp.broadcast_to(doc_ids[:, None], (length, step_count)).reshape(blocks, GROUP)
    pieces = (arrange(sub_keys, blocks), arrange(sub_values, blocks), arrange(sub_queries, blocks), arrange(sub_betas, blocks), arrange(sub_decays, blocks), sub_docs)
    initial = (jnp.zeros((head_count, head_width, head_width), jnp.float32), jnp.full((), -1, jnp.int32))
    carried, outputs = lax.scan(jax.checkpoint(group_step), initial, pieces)
    outputs = jnp.moveaxis(outputs, 1, 2).reshape(length, step_count, head_count, head_width)
    return outputs[:, step_count - 1]

def short_conv(mixed_rows, weight, doc_ids):
    length = mixed_rows.shape[0]
    tap_count = weight.shape[1]
    padded = jnp.concatenate([jnp.zeros((tap_count - 1, mixed_rows.shape[1]), jnp.float32), mixed_rows], axis=0)
    padded_docs = jnp.concatenate([jnp.full((tap_count - 1,), -1, jnp.int32), doc_ids])
    summed = jnp.zeros_like(mixed_rows)
    for offset in range(tap_count):
        window = padded[offset:offset + length]
        inside = (padded_docs[offset:offset + length] == doc_ids)[:, None]
        summed = summed + jnp.where(inside, window, 0.0) * weight[:, offset]
    return summed

def mixer_core(projected, gate_logits, doc_ids, conv_weight, decay_log, decay_bias, out_gain):
    row_count = projected.shape[0]
    head_count = decay_log.shape[0]
    head_width = out_gain.shape[0]
    inner_width = head_count * head_width
    step_count = (gate_logits.shape[1] - head_count) // head_count
    conv_cols = conv_weight.shape[0]
    mixed_rows = jax.nn.silu(short_conv(projected[:, :conv_cols], conv_weight, doc_ids))
    queries = unit_rows(mixed_rows[:, :inner_width].reshape(row_count, head_count, head_width)) * head_width ** (-0.5)
    key_end = inner_width + step_count * inner_width
    key_rows = unit_rows(mixed_rows[:, inner_width:key_end].reshape(row_count, step_count, head_count, head_width))
    values = mixed_rows[:, key_end:].reshape(row_count, step_count, head_count, head_width)
    beta_rows = jax.nn.sigmoid(gate_logits[:, :step_count * head_count]).reshape(row_count, step_count, head_count)
    decays = -jnp.exp(decay_log) * jax.nn.softplus(gate_logits[:, step_count * head_count:] + decay_bias)
    outputs = recurrence(queries, key_rows, values, beta_rows, decays, doc_ids)
    gate_rows = projected[:, conv_cols:].reshape(row_count, head_count, head_width)
    normed = rms_scale(outputs, out_gain) * jax.nn.silu(gate_rows)
    return normed.reshape(row_count, inner_width)

def row_forward(inputs, doc_ids, attn_gain, mixer_in, mixer_small, conv_weight, decay_log, decay_bias, out_gain, mixer_out, ffn_gain, ffn_in, ffn_out):
    normed = low(rms_scale(inputs, low(attn_gain)))
    projected = low_back(jnp.dot(normed, low(mixer_in), precision=highest))
    gate_logits = low_back(jnp.dot(normed, low(mixer_small), precision=highest))
    mixed = low(mixer_core(projected, gate_logits, doc_ids, low(conv_weight), decay_log, decay_bias, out_gain))
    middle = inputs + low_back(jnp.dot(mixed, low(mixer_out), precision=highest))
    ffn_rows = low(rms_scale(middle, low(ffn_gain)))
    gate_up = low_back(jnp.dot(ffn_rows, low(ffn_in), precision=highest))
    hidden = low(jax.nn.silu(gate_up[:, :FF]) * gate_up[:, FF:])
    return middle + low_back(jnp.dot(hidden, low(ffn_out), precision=highest))

def reference(tokens, doc_ids, attn_gain, mixer_in, mixer_small, conv_weight, decay_log, decay_bias, out_gain, mixer_out, ffn_gain, ffn_in, ffn_out, out_grad):
    params = (attn_gain, mixer_in, mixer_small, conv_weight, decay_log, decay_bias, out_gain, mixer_out, ffn_gain, ffn_in, ffn_out)

    def one_row(sums, pieces):
        row_tokens, row_docs, row_grad = pieces

        def forward(row_inputs, *weights):
            return row_forward(row_inputs, row_docs, *weights)
        result, pullback = jax.vjp(forward, row_tokens.astype(jnp.float32), *params)
        grads = pullback(row_grad.astype(jnp.float32))
        sums = tuple((partial_sum + term for partial_sum, term in zip(sums, grads[1:])))
        return (sums, (result.astype(jnp.bfloat16), grads[0].astype(jnp.bfloat16)))
    zeros = tuple((jnp.zeros(weight.shape, jnp.float32) for weight in params))
    sums, (outputs, input_grad) = lax.scan(one_row, zeros, (tokens, doc_ids, out_grad))
    return (outputs, input_grad, sums[0], sums[1], sums[2], sums[3], sums[4], sums[5], sums[6], sums[7], sums[8], sums[9], sums[10])
```

```python
import functools
import jax
import jax.numpy as jnp
from jax import lax
from jax.experimental import pallas as pl
from jax.experimental.pallas import tpu as pltpu
from jax.sharding import PartitionSpec as P

norm_eps = 1e-06
low = jnp.bfloat16
f32 = jnp.float32
AXES = ("wide", "narrow")


def dims(left, right, left_dim, right_dim):
    return lax.dot_general(
        left, right, (((left_dim,), (right_dim,)), ((), ())), preferred_element_type=f32
    )


def one(left, right, left_dim=1, right_dim=0):
    return dims(left.astype(low), right.astype(low), left_dim, right_dim)


def parts(value):
    high = value.astype(low)
    return high, (value - high.astype(f32)).astype(low)


def three(left, right, left_dim=1, right_dim=0):
    left_high, left_rest = left if isinstance(left, tuple) else parts(left)
    right_high, right_rest = right if isinstance(right, tuple) else parts(right)
    return (
        dims(left_high, right_high, left_dim, right_dim)
        + dims(left_high, right_rest, left_dim, right_dim)
        + dims(left_rest, right_high, left_dim, right_dim)
    )


def sigmoid(value):
    return 1.0 / (1.0 + jnp.exp(-value))


def later(value, distance):
    return pltpu.roll(value, distance % value.shape[0], 0)


def short_conv(rows, taps, inside):
    summed = rows * taps[3:4]
    for distance in (1, 2, 3):
        summed = summed + later(rows, distance) * inside[distance - 1] * taps[3 - distance : 4 - distance]
    return summed


def short_conv_back(grad, rows, taps, inside):
    back = grad * taps[3:4]
    tap_grads = [jnp.sum(grad * rows, axis=0, keepdims=True)]
    for distance in (1, 2, 3):
        masked = grad * inside[distance - 1]
        back = back + later(masked, -distance) * taps[3 - distance : 4 - distance]
        tap_grads.append(jnp.sum(masked * later(rows, distance), axis=0, keepdims=True))
    return back, jnp.concatenate(tap_grads[::-1], axis=0)


def unit(rows):
    scale = lax.rsqrt(jnp.sum(rows * rows, axis=1, keepdims=True) + norm_eps)
    return rows * scale, scale


def unit_back(normed, scale, grad):
    return scale * (grad - normed * jnp.sum(grad * normed, axis=1, keepdims=True))


def iotas(count):
    return (
        lax.broadcasted_iota(jnp.int32, (count, count), 0),
        lax.broadcasted_iota(jnp.int32, (count, count), 1),
    )


def decay_matrix(rate_col, rate_row, doc_col, doc_row):
    row, col = iotas(rate_col.shape[0])
    same = doc_col == doc_row
    causal = same & (row >= col)
    sum_col = jnp.sum(jnp.where(causal, rate_row, 0.0), axis=1, keepdims=True)
    sum_row = jnp.sum(jnp.where(same & (row <= col), rate_col, 0.0), axis=0, keepdims=True)
    spread = jnp.where(row > col, jnp.minimum(sum_col - sum_row, 0.0), 0.0)
    return jnp.where(causal, jnp.exp(spread), 0.0), causal


def quad(a, b, c, d):
    return jnp.concatenate(
        [jnp.concatenate([a, b], axis=1), jnp.concatenate([c, d], axis=1)], axis=0
    )


PAIRS = ((0, 0), (1, 0), (1, 1))


def decay_tiles(decay):
    half = decay.shape[0] // 2
    row, col = iotas(half)
    keys, queries = {}, {}
    for i, j in PAIRS:
        tile = decay[i * half : (i + 1) * half, j * half : (j + 1) * half]
        strict = jnp.where(row > col, tile, 0.0) if i == j else tile
        keys[i, j] = quad(strict, strict, tile, strict if i == j else tile)
        queries[i, j] = jnp.concatenate([tile, tile], axis=1)
    return keys, queries


def tiles(first, second):
    half = first.shape[0] // 2
    return [
        jnp.concatenate([first[:half], second[:half]], axis=0),
        jnp.concatenate([first[half:], second[half:]], axis=0),
    ]


def untiled(pair):
    half = pair[0].shape[0] // 2
    return (
        jnp.concatenate([pair[0][:half], pair[1][:half]], axis=0),
        jnp.concatenate([pair[0][half:], pair[1][half:]], axis=0),
    )


def inverses(systems):
    count = systems[0].shape[0]
    half = count // 2
    row, col = iotas(count)
    row_token, col_token = row & (half - 1), col & (half - 1)
    apart = jnp.where(row_token > col_token, row_token ^ col_token, 0)
    eye = jnp.where(row == col, 1.0, 0.0)
    solved = [eye - jnp.where(row_token == col_token, system, 0.0) for system in systems]
    lows = [system.astype(low) for system in systems]
    size = 1
    while size < half:
        inside = jnp.where((apart >= size) & (apart < 2 * size), 1.0, 0.0).astype(low)
        rounded = [value.astype(low) for value in solved]
        products = [dims(entry * inside, value, 1, 0) for entry, value in zip(lows, rounded)]
        solved = [
            value - dims(kept, product.astype(low), 1, 0)
            for value, kept, product in zip(solved, rounded, products)
        ]
        size *= 2
    refined = []
    for system, value, kept in zip(systems, solved, (parts(value) for value in solved)):
        left = eye - value - three(system, kept)
        refined.append(value + dims(kept[0], left.astype(low), 1, 0))
    return refined


def mixer_values(pieces, taps, beta, rate_col, doc_col, inside, rate_row, doc_row):
    convolved = [short_conv(piece, tap, inside) for piece, tap in zip(pieces, taps)]
    slopes = [sigmoid(value) for value in convolved]
    active = [value * slope for value, slope in zip(convolved, slopes)]
    decay, causal = decay_matrix(rate_col, rate_row, doc_col, doc_row)
    return convolved, slopes, active, decay


def lane_of(shape):
    return lax.broadcasted_iota(jnp.int32, shape, 1)


def pick(values, lane):
    return jnp.sum(jnp.where(lane_of(values.shape) == lane, values, 0.0), axis=1, keepdims=True)


def as_row(col):
    row, column = iotas(col.shape[0])
    return jnp.sum(jnp.where(row == column, col, 0.0), axis=0, keepdims=True)


def head_scalars(head, heads, logits, rates, marks):
    first = sigmoid(pick(logits, head))
    second = sigmoid(pick(logits, heads + head))
    speed = -jnp.exp(pick(rates[0:1], 2 * heads + head))
    soft = pick(logits, 2 * heads + head) + pick(rates[1:2], 2 * heads + head)
    rate = speed * (jnp.maximum(soft, 0.0) + jnp.log1p(jnp.exp(-jnp.abs(soft))))
    doc = marks[:, 0:1]
    inside = [marks[:, 1:2], marks[:, 2:3], marks[:, 3:4]]
    return first, second, speed, soft, rate, doc, inside


def rms_scale(inputs):
    return lax.rsqrt(jnp.mean(inputs * inputs, axis=1, keepdims=True) + norm_eps)


def forward_head(pieces, taps, scalars, doc_row, gain):
    first_beta, second_beta, _, _, rate, doc, inside = scalars
    beta = tiles(first_beta, second_beta)
    _, _, active, decay = mixer_values(
        pieces[:5], taps, beta, rate, doc, inside, as_row(rate), doc_row
    )
    half = decay.shape[0] // 2
    width = active[0].shape[1]
    query = unit(active[0])[0] * width ** (-0.5)
    key = tiles(unit(active[1])[0], unit(active[2])[0])
    value = tiles(active[3], active[4])
    key_decay, query_decay = decay_tiles(decay)
    system = {
        (i, j): beta[i] * key_decay[i, j] * three(key[i], key[j], 1, 1) for i, j in PAIRS
    }
    inverse = [parts(entry) for entry in inverses([system[0, 0], system[1, 1]])]
    first = three(inverse[0], beta[0] * value[0])
    second = three(inverse[1], beta[1] * value[1] - three(system[1, 0], first))
    queries = [query[:half], query[half:]]
    reads = {(i, j): query_decay[i, j] * three(queries[i], key[j], 1, 1) for i, j in PAIRS}
    out = jnp.concatenate(
        [three(reads[0, 0], first), three(reads[1, 0], first) + three(reads[1, 1], second)], axis=0
    )
    gate = pieces[5]
    mixed = out * rms_scale(out) * gain * (gate * sigmoid(gate))
    return mixed.astype(low), inverse, [first, second], out


def forward_kernel(sizes, streams, count, calls, heads, *refs):
    refs = list(refs)
    token_ref, gain_row_ref, in_ref, small_ref, tap_ref = [refs.pop(0) for _ in range(5)]
    mark_ref, doc_ref, rate_ref, gain_ref = [refs.pop(0) for _ in range(4)]
    shards = [refs.pop(0) for _ in range(count)]
    mixed_ref, piece_ref, inverse_ref, update_ref, out_ref, logit_ref, normed_ref = [
        refs.pop(0) for _ in range(7)
    ]
    fulls = [refs.pop(0) for _ in range(count)]
    head = pl.program_id(0)
    if count:
        tick, finish = gather_steps(sizes, streams, shards, fulls, refs)
        for step, place_at in enumerate(calls):
            if place_at < heads:
                pl.when(head == place_at)(functools.partial(tick, step))

    @pl.when(head == 0)
    def _():
        inputs = token_ref[...].astype(f32)
        normed = (inputs * rms_scale(inputs) * gain_row_ref[...]).astype(low)
        normed_ref[...] = normed
        logit_ref[...] = dims(normed, small_ref[...], 1, 0)

    width = gain_ref.shape[1]
    projected = dims(normed_ref[...], in_ref[...], 1, 0)
    piece_ref[0] = projected
    pieces = [projected[:, group * width : (group + 1) * width] for group in range(6)]
    taps = [tap_ref[:, group * width : (group + 1) * width] for group in range(5)]
    scalars = head_scalars(head, heads, logit_ref[...], rate_ref[...], mark_ref[...])
    mixed, inverse, update, out = forward_head(pieces, taps, scalars, doc_ref[0:1], gain_ref[...])
    mixed_ref[...] = mixed
    for tile in (0, 1):
        inverse_ref[0, 2 * tile] = inverse[tile][0]
        inverse_ref[0, 2 * tile + 1] = inverse[tile][1]
        update_ref[0, tile] = update[tile]
    out_ref[...] = out
    if count:

        @pl.when(head == heads - 1)
        def _():
            for step, place_at in enumerate(calls):
                if place_at >= heads:
                    tick(step)
            finish()


def backward_head(pieces, taps, scalars, doc_row, gain, grad, inverse, update, out):
    first_beta, second_beta, speed, soft, rate, doc, inside = scalars
    beta = tiles(first_beta, second_beta)
    convolved, slopes, active, decay = mixer_values(
        pieces[:5], taps, beta, rate, doc, inside, as_row(rate), doc_row
    )
    count = decay.shape[0]
    half = count // 2
    width = active[0].shape[1]
    root = width ** (-0.5)
    gate = pieces[5]
    scale = rms_scale(out)
    normed = out * scale
    gate_slope = sigmoid(gate)
    opened = gate * gate_slope
    normed_grad = grad * opened * gain
    gain_grad = jnp.sum(grad * opened * normed, axis=0, keepdims=True)
    gate_grad = grad * normed * gain * (gate_slope * (1.0 + gate * (1.0 - gate_slope)))
    out_grad = scale * (normed_grad - normed * jnp.mean(normed_grad * normed, axis=1, keepdims=True))

    query_unit, query_scale = unit(active[0])
    key_first, first_scale = unit(active[1])
    key_second, second_scale = unit(active[2])
    query = query_unit * root
    key = tiles(key_first, key_second)
    value = tiles(active[3], active[4])
    key_decay, query_decay = decay_tiles(decay)
    key_parts = [parts(entry) for entry in key]
    query_parts = [parts(query[:half]), parts(query[half:])]
    key_low = [entry[0] for entry in key_parts]
    query_low = [entry[0] for entry in query_parts]
    update = [parts(entry) for entry in update]
    gram = {(i, j): three(key_parts[i], key_parts[j], 1, 1) for i, j in PAIRS}
    cross = {(i, j): three(query_parts[i], key_parts[j], 1, 1) for i, j in PAIRS}
    reads = {(i, j): parts(query_decay[i, j] * cross[i, j]) for i, j in PAIRS}
    outs = [parts(out_grad[:half]), parts(out_grad[half:])]
    read_grad = {(i, j): three(outs[i], update[j], 1, 1) for i, j in PAIRS}
    first_grad = three(reads[0, 0], outs[0], 0, 0) + three(reads[1, 0], outs[1], 0, 0)
    second_grad = three(reads[1, 1], outs[1], 0, 0)
    target_second = three(inverse[1], second_grad, 0, 0)
    link = beta[1] * key_decay[1, 0] * gram[1, 0]
    target_first = three(inverse[0], first_grad - three(link, target_second, 0, 0), 0, 0)
    target = [target_first, target_second]
    target_parts = [parts(entry) for entry in target]
    beta_grad = [jnp.sum(target[i] * value[i], axis=1, keepdims=True) for i in (0, 1)]
    value_grad = [beta[i] * target[i] for i in (0, 1)]
    key_grad = [None, None]
    query_grad = [None, None]
    energy = {}

    def add(total, term):
        return term if total is None else total + term

    for i, j in PAIRS:
        weighted = -three(target_parts[i], update[j], 1, 1) * key_decay[i, j]
        product = weighted * gram[i, j]
        beta_grad[i] = beta_grad[i] + jnp.sum(product, axis=1, keepdims=True)
        gram_grad = (beta[i] * weighted).astype(low)
        key_energy = beta[i] * product
        key_grad[i] = add(key_grad[i], dims(gram_grad, key_low[j], 1, 0))
        key_grad[j] = add(key_grad[j], dims(gram_grad, key_low[i], 0, 0))
        cross_grad = read_grad[i, j] * query_decay[i, j]
        query_energy = cross_grad * cross[i, j]
        cross_low = cross_grad.astype(low)
        query_grad[i] = add(query_grad[i], dims(cross_low, key_low[j], 1, 0))
        key_grad[j] = add(key_grad[j], dims(cross_low, query_low[i], 0, 0))
        energy[i, j] = (
            key_energy[:half, :half]
            + key_energy[:half, half:]
            + key_energy[half:, :half]
            + key_energy[half:, half:]
            + query_energy[:, :half]
            + query_energy[:, half:]
        )
    whole = quad(energy[0, 0], jnp.zeros((half, half), f32), energy[1, 0], energy[1, 1])
    sum_grad = as_row(jnp.sum(whole, axis=1, keepdims=True)) - jnp.sum(whole, axis=0, keepdims=True)
    row, col = iotas(count)
    rate_grad = jnp.sum(
        jnp.where((doc == doc_row) & (col >= row), sum_grad, 0.0), axis=1, keepdims=True
    )
    first_beta_grad, second_beta_grad = untiled(beta_grad)
    soft_grad = rate_grad * speed * sigmoid(soft)
    log_grad = jnp.sum(rate_grad * rate, axis=0, keepdims=True)
    bias_grad = jnp.sum(soft_grad, axis=0, keepdims=True)
    logit_grads = [
        first_beta_grad * first_beta * (1.0 - first_beta),
        second_beta_grad * second_beta * (1.0 - second_beta),
        soft_grad,
    ]
    first_key_grad, second_key_grad = untiled(key_grad)
    first_value_grad, second_value_grad = untiled(value_grad)
    active_grads = [
        unit_back(query_unit, query_scale, jnp.concatenate(query_grad, axis=0) * root),
        unit_back(key_first, first_scale, first_key_grad),
        unit_back(key_second, second_scale, second_key_grad),
        first_value_grad,
        second_value_grad,
    ]
    piece_grads, tap_grads = [], []
    for group in range(5):
        slope = slopes[group]
        conv_grad = active_grads[group] * (slope * (1.0 + convolved[group] * (1.0 - slope)))
        back, tap_grad = short_conv_back(conv_grad, pieces[group], taps[group], inside)
        piece_grads.append(back.astype(low))
        tap_grads.append(tap_grad)
    piece_grads.append(gate_grad.astype(low))
    return piece_grads, tap_grads, logit_grads, log_grad, bias_grad, gain_grad


def backward_kernel(sizes, streams, count, calls, heads, *refs):
    refs = list(refs)
    token_ref, gain_row_ref, in_ref, small_ref, tap_ref = [refs.pop(0) for _ in range(5)]
    mark_ref, doc_ref, rate_ref, gain_ref = [refs.pop(0) for _ in range(4)]
    grad_ref, piece_ref, inverse_ref, update_ref, out_ref, logit_ref, normed_ref, middle_ref = [
        refs.pop(0) for _ in range(8)
    ]
    terms = [refs.pop(0) for _ in range(count)]
    in_grad_ref, tap_grad_ref, small_grad_ref, sums_ref, gain_grad_ref, token_grad_ref = [
        refs.pop(0) for _ in range(6)
    ]
    sums = [refs.pop(0) for _ in range(count)]
    logit_grad_ref, normed_grad_ref = refs.pop(0), refs.pop(0)
    head = pl.program_id(0)
    if count:
        tick, finish = scatter_steps(sizes, streams, terms, sums, refs)
        for step, place_at in enumerate(calls):
            if place_at < heads:
                pl.when(head == place_at)(functools.partial(tick, step))

    @pl.when(head == 0)
    def _():
        logit_grad_ref[...] = jnp.zeros_like(logit_grad_ref)
        normed_grad_ref[...] = jnp.zeros_like(normed_grad_ref)
        sums_ref[...] = jnp.zeros_like(sums_ref)

    width = gain_ref.shape[1]
    pieces = [piece_ref[0, :, group * width : (group + 1) * width] for group in range(6)]
    taps = [tap_ref[:, group * width : (group + 1) * width] for group in range(5)]
    scalars = head_scalars(head, heads, logit_ref[...], rate_ref[...], mark_ref[...])
    piece_grads, tap_grads, logit_grads, log_grad, bias_grad, gain_grad = backward_head(
        pieces,
        taps,
        scalars,
        doc_ref[0:1],
        gain_ref[...],
        grad_ref[...],
        [(inverse_ref[0, 0], inverse_ref[0, 1]), (inverse_ref[0, 2], inverse_ref[0, 3])],
        [update_ref[0, 0], update_ref[0, 1]],
        out_ref[...],
    )
    for group in range(5):
        tap_grad_ref[:, group * width : (group + 1) * width] = tap_grads[group]
    projected_grad = jnp.concatenate(piece_grads, axis=1)
    in_grad_ref[...] = dims(normed_ref[...], projected_grad, 0, 0).astype(low)
    normed_grad_ref[...] += dims(projected_grad, in_ref[...], 1, 1)
    lane = lane_of(logit_grad_ref.shape)
    spread = jnp.zeros(logit_grad_ref.shape, f32)
    for index, entry in enumerate(logit_grads):
        spread = spread + jnp.where(lane == index * heads + head, entry, 0.0)
    logit_grad_ref[...] += spread
    line = lane_of((1, width))
    sums_ref[0:1] += jnp.where(line == head, log_grad, 0.0)
    sums_ref[1:2] += jnp.where(line == head, bias_grad, 0.0)
    sums_ref[2:3] += gain_grad

    @pl.when(head == heads - 1)
    def _():
        logit_low = logit_grad_ref[...].astype(low)
        small_grad_ref[...] = dims(normed_ref[...], logit_low, 0, 0).astype(low)
        grad = normed_grad_ref[...] + dims(logit_low, small_ref[...], 1, 1)
        inputs = token_ref[...].astype(f32)
        scale = rms_scale(inputs)
        normed = inputs * scale
        gain_grad_ref[...] = jnp.sum(grad * normed, axis=0, keepdims=True)
        weighted = grad * gain_row_ref[...]
        back = scale * (weighted - normed * jnp.mean(weighted * normed, axis=1, keepdims=True))
        token_grad_ref[...] = (middle_ref[...] + back).astype(low)
        if count:
            for step, place_at in enumerate(calls):
                if place_at >= heads:
                    tick(step)
            finish()


def whole_spec(shape):
    return pl.BlockSpec(shape, lambda h: (0,) * len(shape))


def head_spec(*shape):
    return pl.BlockSpec((1,) + shape, lambda h: (h,) + (0,) * len(shape))


def col_spec(rows, width):
    return pl.BlockSpec((rows, width), lambda h: (0, h))


HBM = pl.BlockSpec(memory_space=pltpu.HBM)
VMEM_LIMIT = 62 << 20


def shared_specs(seq_len, model_width, width):
    return [
        whole_spec((seq_len, model_width)),
        whole_spec((1, model_width)),
        col_spec(model_width, 6 * width),
        whole_spec((model_width, 128)),
        col_spec(4, 5 * width),
        whole_spec((seq_len, 8)),
        whole_spec((8, seq_len)),
        whole_spec((8, 128)),
        whole_spec((1, width)),
    ]


def saved_specs(seq_len, model_width, width):
    return [
        head_spec(seq_len, 6 * width),
        head_spec(4, seq_len, seq_len),
        head_spec(2, seq_len, width),
        col_spec(seq_len, width),
        whole_spec((seq_len, 128)),
        whole_spec((seq_len, model_width)),
    ]


def mixer_forward(sizes, streams, calls, shared, shards, heads, call):
    seq_len, model_width = shared[0].shape
    width = shared[-1].shape[1]
    count = len(shards)
    scratch, extra = [], {}
    if count:
        total = slots(sizes, streams)
        extra = dict(collective_id=call, has_side_effects=True)
        scratch = [
            pltpu.SemaphoreType.DMA((total,)),
            pltpu.SemaphoreType.DMA((total,)),
            pltpu.SemaphoreType.DMA((count,)),
        ]
        shape = tuple(sizes[dim] for dim in "zyxc")
    outs = pl.pallas_call(
        functools.partial(forward_kernel, sizes, streams, count, calls, heads),
        grid=(heads,),
        in_specs=shared_specs(seq_len, model_width, width) + [HBM] * count,
        out_specs=[col_spec(seq_len, width)] + saved_specs(seq_len, model_width, width) + [HBM] * count,
        out_shape=[
            jax.ShapeDtypeStruct((seq_len, heads * width), low),
            jax.ShapeDtypeStruct((heads, seq_len, 6 * width), f32),
            jax.ShapeDtypeStruct((heads, 4, seq_len, seq_len), low),
            jax.ShapeDtypeStruct((heads, 2, seq_len, width), f32),
            jax.ShapeDtypeStruct((seq_len, heads * width), f32),
            jax.ShapeDtypeStruct((seq_len, 128), f32),
            jax.ShapeDtypeStruct((seq_len, model_width), low),
        ]
        + [jax.ShapeDtypeStruct(shape + shard.shape, shard.dtype) for shard in shards],
        scratch_shapes=scratch,
        compiler_params=pltpu.CompilerParams(vmem_limit_bytes=VMEM_LIMIT, **extra),
        name="mixer_forward",
    )(*shared, *shards)
    return outs[0], outs[1:7], [out.reshape((-1, out.shape[-1])) for out in outs[7:]]


def mixer_backward(sizes, streams, calls, shared, grad, saved, middle_grad, terms, heads, call):
    seq_len, model_width = shared[0].shape
    width = shared[-1].shape[1]
    count = len(terms)
    scratch = [pltpu.VMEM((seq_len, 128), f32), pltpu.VMEM((seq_len, model_width), f32)]
    extra, blocks = {}, []
    if count:
        extra = dict(collective_id=call, has_side_effects=True)
        blocks, buffers = scatter_setup(sizes, streams, terms)
        scratch = scratch + buffers
    outs = pl.pallas_call(
        functools.partial(backward_kernel, sizes, streams, count, calls, heads),
        grid=(heads,),
        in_specs=shared_specs(seq_len, model_width, width)
        + [col_spec(seq_len, width)]
        + saved_specs(seq_len, model_width, width)
        + [whole_spec((seq_len, model_width))]
        + [HBM] * count,
        out_specs=[
            col_spec(model_width, 6 * width),
            col_spec(4, 5 * width),
            whole_spec((model_width, 128)),
            whole_spec((8, width)),
            whole_spec((1, model_width)),
            whole_spec((seq_len, model_width)),
        ]
        + [whole_spec((block.shape[4], block.shape[5])) for block in blocks],
        out_shape=[
            jax.ShapeDtypeStruct((model_width, heads * 6 * width), low),
            jax.ShapeDtypeStruct((4, heads * 5 * width), f32),
            jax.ShapeDtypeStruct((model_width, 128), low),
            jax.ShapeDtypeStruct((8, width), f32),
            jax.ShapeDtypeStruct((1, model_width), f32),
            jax.ShapeDtypeStruct((seq_len, model_width), low),
        ]
        + [jax.ShapeDtypeStruct((block.shape[4], block.shape[5]), f32) for block in blocks],
        scratch_shapes=scratch,
        compiler_params=pltpu.CompilerParams(vmem_limit_bytes=VMEM_LIMIT, **extra),
        name="mixer_backward",
    )(*shared, grad, *saved, middle_grad, *blocks)
    return outs[:6], outs[6:]


def rms_parts(inputs):
    scale = lax.rsqrt(jnp.mean(inputs * inputs, axis=-1, keepdims=True) + norm_eps)
    return inputs * scale, scale


def rms_back(normed, scale, gain_row, grad):
    weighted = grad * gain_row
    return (
        scale * (weighted - normed * jnp.mean(weighted * normed, axis=-1, keepdims=True)),
        jnp.sum(grad * normed, axis=0),
    )


def gathered(shard):
    return lax.all_gather(shard, AXES, axis=0, tiled=True)


def scattered(whole):
    return lax.psum_scatter(whole, AXES, scatter_dimension=0, tiled=True)


MESH = pl.DeviceIdType.MESH


def grid_of(wide, narrow):
    pair = 2 if narrow % 2 == 0 else 1
    half = 2 if wide % 2 == 0 else 1
    return {"z": wide // half, "y": half, "x": narrow // pair, "c": pair}


def place(sizes):
    wide, narrow = lax.axis_index("wide"), lax.axis_index("narrow")
    return {
        "z": wide // sizes["y"],
        "y": lax.rem(wide, sizes["y"]),
        "x": narrow // sizes["c"],
        "c": lax.rem(narrow, sizes["c"]),
    }


def device(sizes, at):
    return (at["z"] * sizes["y"] + at["y"], at["x"] * sizes["c"] + at["c"])


def moved(sizes, at, dim, step):
    other = dict(at)
    other[dim] = lax.rem(at[dim] + step, sizes[dim])
    return other


def meet(sizes, me):
    barrier = pltpu.get_barrier_semaphore()
    count = 0
    for dim in "zyxc":
        for step in range(1, sizes[dim]):
            pl.semaphore_signal(
                barrier,
                inc=1,
                device_id=device(sizes, moved(sizes, me, dim, step)),
                device_id_type=MESH,
            )
            count += 1
    pl.semaphore_wait(barrier, count)


def slots(sizes, streams):
    return sum(sizes[dim] - 1 for stream in streams for dim in stream[3])


def cut(array, cols, chunks, share, orders, first_lag, per_lag):
    units = cols // 128
    streams, start = [], 0
    edges = []
    for chunk in range(chunks):
        edges += [(chunk + share) / chunks, (chunk + 1) / chunks]
    for index, edge in enumerate(edges):
        stop = round(edge * units)
        if stop > start:
            lag = first_lag + (index // 2) // per_lag
            streams.append((array, start * 128, (stop - start) * 128, orders[index % 2], lag))
        start = stop
    return streams


def agenda(streams):
    last = max(stream[4] for stream in streams) + 5
    return [
        [
            (index, phase)
            for phase in (4, 3, 2, 1, 0)
            for index, stream in enumerate(streams)
            if step - stream[4] == phase
        ]
        for step in range(last)
    ]


def slot_table(sizes, streams):
    table, used = {}, 0
    for index, stream in enumerate(streams):
        for phase in range(4):
            table[index, phase] = used
            used += sizes[stream[3][phase]] - 1
    return table


def gather_steps(sizes, streams, shards, fulls, sems):
    send_sem, recv_sem, local_sem = sems
    table = slot_table(sizes, streams)
    plan = agenda(streams)

    def local(me):
        return [
            pltpu.make_async_copy(
                shard, full.at[me["z"], me["y"], me["x"], me["c"]], local_sem.at[index]
            )
            for index, (shard, full) in enumerate(zip(shards, fulls))
        ]

    def copies(me, index, phase):
        array, col, width, order, lag = streams[index]
        dim = order[phase]
        block = tuple(slice(None) if d in order[:phase] else me[d] for d in "zyxc")
        target = fulls[array].at[block + (slice(None), pl.ds(col, width))]
        source = shards[array].at[:, pl.ds(col, width)] if phase == 0 else target
        return [
            pltpu.make_async_remote_copy(
                src_ref=source,
                dst_ref=target,
                send_sem=send_sem.at[table[index, phase] + hop - 1],
                recv_sem=recv_sem.at[table[index, phase] + hop - 1],
                device_id=device(sizes, moved(sizes, me, dim, hop)),
                device_id_type=MESH,
            )
            for hop in range(1, sizes[dim])
        ]

    def tick(step):
        me = place(sizes)
        if step == 0:
            for copy in local(me):
                copy.start()
            meet(sizes, me)
        if step == 1:
            for copy in local(me):
                copy.wait()
        for index, phase in plan[step]:
            if phase > 0:
                for copy in copies(me, index, phase - 1):
                    copy.wait_recv()
            if phase < 4:
                for copy in copies(me, index, phase):
                    copy.start()

    def finish():
        me = place(sizes)
        for index in range(len(streams)):
            for phase in range(4):
                for copy in copies(me, index, phase):
                    copy.wait_send()

    return tick, finish


def gather_kernel(sizes, streams, count, *refs):
    tick, finish = gather_steps(
        sizes, streams, refs[:count], refs[count : 2 * count], refs[2 * count :]
    )
    for step in range(len(agenda(streams))):
        tick(step)
    finish()


def gather(sizes, streams, shards, call):
    count = len(shards)
    total = slots(sizes, streams)
    shape = tuple(sizes[dim] for dim in "zyxc")
    outs = pl.pallas_call(
        functools.partial(gather_kernel, sizes, streams, count),
        out_shape=[jax.ShapeDtypeStruct(shape + shard.shape, shard.dtype) for shard in shards],
        in_specs=[HBM] * count,
        out_specs=[HBM] * count,
        scratch_shapes=[
            pltpu.SemaphoreType.DMA((total,)),
            pltpu.SemaphoreType.DMA((total,)),
            pltpu.SemaphoreType.DMA((count,)),
        ],
        compiler_params=pltpu.CompilerParams(collective_id=call, has_side_effects=True),
        name="weights_gather",
    )(*shards)
    return [out.reshape((-1, out.shape[-1])) for out in outs]


def scatter_setup(sizes, streams, terms):
    shape = tuple(sizes[dim] for dim in "zyxc")
    devices = shape[0] * shape[1] * shape[2] * shape[3]
    blocks = [
        term.reshape(shape + (term.shape[0] // devices, term.shape[1])) for term in terms
    ]
    total = slots(sizes, streams)
    buffers = [
        pltpu.SemaphoreType.DMA((total,)),
        pltpu.SemaphoreType.DMA((total,)),
        pltpu.SemaphoreType.DMA((len(streams),)),
    ]
    for array, col, width, order, lag in streams:
        tail = (blocks[array].shape[4], width)
        buffers.append(pltpu.VMEM(shape[:3] + tail, low))
        for phase in range(4):
            kept = tuple(sizes[dim] for dim in "zyx" if dim not in order[: phase + 1])
            buffers.append(pltpu.VMEM((sizes[order[phase]] - 1,) + kept + tail, low))
    return blocks, buffers


def scatter_steps(sizes, streams, terms, sums, refs):
    send_sem, recv_sem, local_sem = refs[:3]
    held = [refs[3 + 5 * index] for index in range(len(streams))]
    got = {
        (index, phase): refs[4 + 5 * index + phase]
        for index in range(len(streams))
        for phase in range(4)
    }
    table = slot_table(sizes, streams)
    plan = agenda(streams)

    def load(me, index):
        array, col, width, order, lag = streams[index]
        return pltpu.make_async_copy(
            terms[array].at[:, :, :, me["c"], :, pl.ds(col, width)], held[index], local_sem.at[index]
        )

    def copies(me, index, phase):
        array, col, width, order, lag = streams[index]
        dim = order[phase]
        found = []
        for hop in range(1, sizes[dim]):
            to = moved(sizes, me, dim, hop)
            if phase == 0:
                source = terms[array].at[:, :, :, to["c"], :, pl.ds(col, width)]
            else:
                block = tuple(
                    me[d] if d in order[:phase] else (to[d] if d == dim else slice(None))
                    for d in "zyx"
                )
                source = held[index].at[block]
            found.append(
                pltpu.make_async_remote_copy(
                    src_ref=source,
                    dst_ref=got[index, phase].at[hop - 1],
                    send_sem=send_sem.at[table[index, phase] + hop - 1],
                    recv_sem=recv_sem.at[table[index, phase] + hop - 1],
                    device_id=device(sizes, to),
                    device_id_type=MESH,
                )
            )
        return found

    def combine(me, index, phase):
        array, col, width, order, lag = streams[index]
        kept = [d for d in "zyx" if d not in order[: phase + 1]]
        total = 1
        for d in kept:
            total *= sizes[d]

        def body(flat, carry):
            at, rest = dict(me), flat
            for d in reversed(kept):
                at[d] = lax.rem(rest, sizes[d])
                rest = rest // sizes[d]
            where = tuple(at[d] for d in "zyx")
            inner = tuple(at[d] for d in kept)
            value = held[index][where]
            others = [got[index, phase][(hop,) + inner] for hop in range(sizes[order[phase]] - 1)]
            if phase == 3 or len(others) > 1:
                value = value.astype(f32)
                for other in others:
                    value = value + other.astype(f32)
            else:
                value = value + others[0]
            if phase == 3:
                sums[array][:, pl.ds(col, width)] = value
            else:
                held[index][where] = value.astype(low)
            return carry

        if total == 1:
            body(0, 0)
        else:
            lax.fori_loop(0, total, body, 0)

    def tick(step):
        me = place(sizes)
        if step == 0:
            for index in range(len(streams)):
                load(me, index).start()
            meet(sizes, me)
        for index, phase in plan[step]:
            if phase > 0:
                for copy in copies(me, index, phase - 1):
                    copy.wait_recv()
                if phase == 1:
                    load(me, index).wait()
                combine(me, index, phase - 1)
            if phase < 4:
                for copy in copies(me, index, phase):
                    copy.start()

    def finish():
        me = place(sizes)
        for index in range(len(streams)):
            for phase in range(4):
                for copy in copies(me, index, phase):
                    copy.wait_send()

    return tick, finish


def small_buffers(sizes, shape):
    return [pltpu.VMEM((2,) + shape, f32) for _ in "cxy"] + [
        pltpu.VMEM((sizes["z"],) + shape, f32),
        pltpu.SemaphoreType.DMA((4, sizes["z"])),
        pltpu.SemaphoreType.DMA((4, sizes["z"])),
    ]


def small_steps(sizes, small, total, refs):
    boxes, lanes, small_send, small_recv = refs[:3], refs[3], refs[4], refs[5]

    def copies(me, phase):
        dim = "cxyz"[phase]
        source = small if phase == 0 else boxes[phase - 1].at[1]
        source = lanes.at[me["z"]] if dim == "z" else source
        return [
            pltpu.make_async_remote_copy(
                src_ref=source,
                dst_ref=lanes.at[me["z"]] if dim == "z" else boxes[phase].at[0],
                send_sem=small_send.at[phase, hop],
                recv_sem=small_recv.at[phase, hop],
                device_id=device(sizes, moved(sizes, me, dim, hop)),
                device_id_type=MESH,
            )
            for hop in range(1, sizes[dim])
        ]

    def tick(step):
        me = place(sizes)
        if step > 0:
            for copy in copies(me, step - 1):
                copy.wait_recv()
            if step < 4:
                mine = small[...] if step == 1 else boxes[step - 2][1]
                boxes[step - 1][1] = mine + boxes[step - 1][0]
            else:
                value = lanes[0]
                for index in range(1, sizes["z"]):
                    value = value + lanes[index]
                total[...] = value
        if step < 4:
            if step == 3:
                lanes[me["z"]] = boxes[2][1]
            for copy in copies(me, step):
                copy.start()

    def finish():
        me = place(sizes)
        for phase in range(4):
            for copy in copies(me, phase):
                copy.wait_send()

    return tick, finish


def scatter_kernel(sizes, streams, count, *refs):
    terms, small = refs[:count], refs[count]
    sums, total = refs[count + 1 : 2 * count + 1], refs[2 * count + 1]
    rest = refs[2 * count + 2 :]
    tick, finish = scatter_steps(sizes, streams, terms, sums, rest[:-6])
    small_tick, small_finish = small_steps(sizes, small, total, rest[-6:])
    for step in range(len(agenda(streams))):
        tick(step)
        if step < 5:
            small_tick(step)
    finish()
    small_finish()


def scatter(sizes, streams, terms, small, call):
    count = len(terms)
    blocks, buffers = scatter_setup(sizes, streams, terms)
    vmem = pl.BlockSpec(memory_space=pltpu.VMEM)
    return pl.pallas_call(
        functools.partial(scatter_kernel, sizes, streams, count),
        out_shape=[
            jax.ShapeDtypeStruct((block.shape[4], block.shape[5]), f32) for block in blocks
        ]
        + [jax.ShapeDtypeStruct(small.shape, f32)],
        in_specs=[HBM] * count + [vmem],
        out_specs=[vmem] * (count + 1),
        scratch_shapes=buffers + small_buffers(sizes, small.shape),
        compiler_params=pltpu.CompilerParams(
            collective_id=call, has_side_effects=True, vmem_limit_bytes=VMEM_LIMIT
        ),
        name="grads_scatter",
    )(*blocks, small)


GATHER_ORDERS = ("zxyc", "yzxc")
SCATTER_ORDERS = ("cyxz", "cxzy")


def planned(terms, orders, chunks):
    streams = []
    for index, (count, lag, per_lag) in enumerate(chunks):
        streams += cut(index, terms[index].shape[1], count, 0.64, orders, lag, per_lag)
    return streams


def per_device(
    sizes,
    tokens,
    doc_ids,
    attn_gain,
    mixer_in,
    mixer_small,
    conv_weight,
    decay_log,
    decay_bias,
    out_gain,
    mixer_out,
    ffn_gain,
    ffn_in,
    ffn_out,
    out_grad,
):
    row_count, seq_len, model_width = tokens.shape
    heads, width = decay_log.shape[0], out_gain.shape[0]
    shard_rows = mixer_in.shape[0]
    small_cols = mixer_small.shape[1]
    channels = conv_weight.shape[0]
    devices = model_width // shard_rows
    ff_width = ffn_out.shape[0]
    own = (
        shard_rows % 16 == 0
        and row_count == 1
        and sizes["x"] == 2
        and sizes["y"] == 2
        and sizes["c"] == 2
    )
    in_shard = (
        mixer_in.astype(low)
        .reshape(shard_rows, 6, heads, width)
        .transpose(0, 2, 1, 3)
        .reshape(shard_rows, -1)
    )
    small_shard = jnp.pad(mixer_small.astype(low), ((0, 0), (0, 128 - small_cols)))
    line_width = channels + (-channels % 128)
    lines_shard = jnp.concatenate(
        [
            jnp.pad(conv_weight.astype(low).T, ((0, 0), (0, line_width - channels))),
            jnp.pad(
                jnp.stack([attn_gain, ffn_gain]).astype(low), ((0, 10), (0, line_width - shard_rows))
            ),
        ]
    )
    out_shard, ffn_out_shard = mixer_out.astype(low).T, ffn_out.astype(low).T
    late_shards = [out_shard, ffn_in.astype(low), ffn_out_shard]
    early_shards = [in_shard, small_shard, lines_shard]
    if own:
        early = planned(early_shards, GATHER_ORDERS, ((8, 0, 4), (1, 0, 1), (1, 0, 1)))
        in_full, small_full, lines = gather(sizes, early, early_shards, 1)
    else:
        in_full, small_full, lines = [gathered(shard) for shard in early_shards]
    lines = lines.reshape(devices, 16, line_width)
    taps = (
        lines[:, :4, :channels]
        .transpose(1, 0, 2)
        .reshape(4, 5, heads, width)
        .transpose(0, 2, 1, 3)
        .reshape(4, -1)
        .astype(f32)
    )
    attn_row = lines[:, 4, :shard_rows].reshape(1, model_width).astype(f32)
    ffn_row = lines[:, 5, :shard_rows].reshape(1, model_width).astype(f32)
    rates = jnp.pad(
        jnp.stack([decay_log, decay_bias]), ((0, 6), (2 * heads, 128 - 3 * heads))
    )

    def shared(index):
        doc = doc_ids[index].astype(f32)
        before = [
            jnp.concatenate([jnp.full((distance,), -1.0), doc[:-distance]]) for distance in (1, 2, 3)
        ]
        marks = jnp.stack([doc] + [jnp.where(entry == doc, 1.0, 0.0) for entry in before], axis=1)
        return [
            tokens[index],
            attn_row,
            in_full,
            small_full,
            taps,
            jnp.pad(marks, ((0, 0), (0, 4))),
            jnp.broadcast_to(doc[None], (8, seq_len)),
            rates,
            out_gain[None],
        ]

    each = [shared(index) for index in range(row_count)]
    if own:
        late = planned(late_shards, GATHER_ORDERS, ((1, 0, 1), (4, 0, 2), (2, 2, 2)))
        mixed, saved, late_full = mixer_forward(
            sizes, late, (0, 2, 4, 7, 8, 8, 8), each[0], late_shards, heads, 2
        )
        saves = [saved]
        out_t, ffn_in_full, ffn_out_t = late_full
    else:
        done = [mixer_forward(sizes, [], (), entry, [], heads, 2) for entry in each]
        mixed = jnp.concatenate([entry[0] for entry in done])
        saves = [entry[1] for entry in done]
        out_t, ffn_in_full, ffn_out_t = [gathered(shard) for shard in late_shards]

    inputs = tokens.reshape(row_count * seq_len, model_width).astype(f32)
    middle = inputs + dims(mixed, out_t, 1, 1)
    ffn_normed, ffn_scale = rms_parts(middle)
    ffn_rows = (ffn_normed * ffn_row).astype(low)
    gate_up = jnp.dot(ffn_rows, ffn_in_full, preferred_element_type=f32)
    gate, up = gate_up[:, :ff_width], gate_up[:, ff_width:]
    slope = jax.nn.sigmoid(gate)
    hidden = (gate * slope * up).astype(low)
    result = middle + dims(hidden, ffn_out_t, 1, 1)
    grad_low = out_grad.reshape(row_count * seq_len, model_width)
    ffn_out_term = dims(grad_low, hidden, 0, 0).astype(low)
    hidden_grad = jnp.dot(grad_low, ffn_out_t, preferred_element_type=f32)
    gate_up_grad = jnp.concatenate(
        [hidden_grad * up * slope * (1.0 + gate * (1.0 - slope)), hidden_grad * gate * slope],
        axis=1,
    ).astype(low)
    ffn_in_term = dims(ffn_rows, gate_up_grad, 0, 0).astype(low)
    rows_grad = dims(gate_up_grad, ffn_in_full, 1, 1)
    middle_norm_grad, ffn_gain_term = rms_back(ffn_normed, ffn_scale, ffn_row, rows_grad)
    middle_grad = grad_low.astype(f32) + middle_norm_grad
    branch_grad = middle_grad.astype(low)
    out_term = dims(branch_grad, mixed, 0, 0).astype(low)
    mixed_grad = jnp.dot(branch_grad, out_t, preferred_element_type=f32)
    late_terms = [ffn_out_term, ffn_in_term, out_term]
    if own:
        late = planned(late_terms, SCATTER_ORDERS, ((2, 0, 2), (4, 1, 2), (1, 2, 1)))
        grads, late_sums = mixer_backward(
            sizes,
            late,
            (0, 1, 4, 7, 8, 8, 8),
            each[0],
            mixed_grad,
            saves[0],
            middle_grad,
            late_terms,
            heads,
            3,
        )
        grads = [grads]
    else:
        grads = [
            mixer_backward(
                sizes,
                [],
                (),
                entry,
                mixed_grad[index * seq_len : (index + 1) * seq_len],
                saves[index],
                middle_grad[index * seq_len : (index + 1) * seq_len],
                [],
                heads,
                3,
            )[0]
            for index, entry in enumerate(each)
        ]
        late_sums = [scattered(term).astype(f32) for term in late_terms]
    in_term, tap_term, small_term, small, attn_gain_term = [
        sum(entry[index] for entry in grads[1:]) + grads[0][index] if row_count > 1 else grads[0][index]
        for index in range(5)
    ]
    input_grad = jnp.stack([entry[5] for entry in grads])
    tap_term = (
        tap_term.reshape(4, heads, 5, width)
        .transpose(0, 2, 1, 3)
        .reshape(4, devices, channels)
        .transpose(1, 0, 2)
    )
    gain_terms = jnp.stack(
        [attn_gain_term.reshape(devices, shard_rows), ffn_gain_term.reshape(devices, shard_rows)],
        axis=1,
    )
    lines_term = jnp.concatenate(
        [
            jnp.pad(tap_term, ((0, 0), (0, 0), (0, line_width - channels))),
            jnp.pad(gain_terms, ((0, 0), (0, 10), (0, line_width - shard_rows))),
        ],
        axis=1,
    )
    lines_term = lines_term.astype(low).reshape(devices * 16, line_width)
    early_terms = [in_term, small_term, lines_term]
    if own:
        early = planned(early_terms, SCATTER_ORDERS, ((8, 0, 2), (1, 0, 1), (1, 0, 1)))
        in_sum, small_sum, lines_sum, small = scatter(sizes, early, early_terms, small, 4)
    else:
        in_sum, small_sum, lines_sum = [scattered(term).astype(f32) for term in early_terms]
        small = lax.psum(small, AXES)
    in_sum = (
        in_sum.reshape(shard_rows, heads, 6, width).transpose(0, 2, 1, 3).reshape(shard_rows, -1)
    )
    ffn_out_sum, ffn_in_sum, out_sum = late_sums
    outputs = result.astype(low).reshape(row_count, seq_len, model_width)
    return (
        outputs,
        input_grad,
        lines_sum[4, :shard_rows],
        in_sum,
        small_sum[:, :small_cols],
        lines_sum[:4, :channels].T,
        small[0, :heads],
        small[1, :heads],
        small[2],
        out_sum.T,
        lines_sum[5, :shard_rows],
        ffn_in_sum,
        ffn_out_sum.T,
    )


def solution(mesh):
    both = P(AXES)
    line = P(None, AXES)
    in_specs = (both, both, both, both, both, both, P(), P(), P(), line, both, both, line, both)
    out_specs = (both, both, both, both, both, both, P(), P(), P(), line, both, both, line)
    sizes = grid_of(mesh.shape["wide"], mesh.shape["narrow"])
    return jax.shard_map(
        functools.partial(per_device, sizes),
        mesh=mesh, in_specs=in_specs, out_specs=out_specs, check_vma=False
    )
```

```python
import functools
import jax
import jax.numpy as jnp
from jax import lax
from jax.experimental import pallas as pl
from jax.experimental.pallas import tpu as pltpu
from jax.sharding import PartitionSpec as P

norm_eps = 1e-06
low = jnp.bfloat16
f32 = jnp.float32
AXES = ("wide", "narrow")


def dims(left, right, left_dim, right_dim):
    return lax.dot_general(
        left, right, (((left_dim,), (right_dim,)), ((), ())), preferred_element_type=f32
    )


def one(left, right, left_dim=1, right_dim=0):
    return dims(left.astype(low), right.astype(low), left_dim, right_dim)


def parts(value):
    high = value.astype(low)
    return high, (value - high.astype(f32)).astype(low)


def three(left, right, left_dim=1, right_dim=0):
    left_high, left_rest = left if isinstance(left, tuple) else parts(left)
    right_high, right_rest = right if isinstance(right, tuple) else parts(right)
    return (
        dims(left_high, right_high, left_dim, right_dim)
        + dims(left_high, right_rest, left_dim, right_dim)
        + dims(left_rest, right_high, left_dim, right_dim)
    )


def sigmoid(value):
    return 1.0 / (1.0 + jnp.exp(-value))


def later(value, distance):
    return pltpu.roll(value, distance % value.shape[0], 0)


def short_conv(rows, taps, inside):
    summed = rows * taps[3:4]
    for distance in (1, 2, 3):
        summed = summed + later(rows, distance) * inside[distance - 1] * taps[3 - distance : 4 - distance]
    return summed


def short_conv_back(grad, rows, taps, inside):
    back = grad * taps[3:4]
    tap_grads = [jnp.sum(grad * rows, axis=0, keepdims=True)]
    for distance in (1, 2, 3):
        masked = grad * inside[distance - 1]
        back = back + later(masked, -distance) * taps[3 - distance : 4 - distance]
        tap_grads.append(jnp.sum(masked * later(rows, distance), axis=0, keepdims=True))
    return back, jnp.concatenate(tap_grads[::-1], axis=0)


def unit(rows):
    scale = lax.rsqrt(jnp.sum(rows * rows, axis=1, keepdims=True) + norm_eps)
    return rows * scale, scale


def unit_back(normed, scale, grad):
    return scale * (grad - normed * jnp.sum(grad * normed, axis=1, keepdims=True))


def iotas(count):
    return (
        lax.broadcasted_iota(jnp.int32, (count, count), 0),
        lax.broadcasted_iota(jnp.int32, (count, count), 1),
    )


def decay_matrix(rate_col, rate_row, doc_col, doc_row):
    row, col = iotas(rate_col.shape[0])
    same = doc_col == doc_row
    causal = same & (row >= col)
    sum_col = jnp.sum(jnp.where(causal, rate_row, 0.0), axis=1, keepdims=True)
    sum_row = jnp.sum(jnp.where(same & (row <= col), rate_col, 0.0), axis=0, keepdims=True)
    spread = jnp.where(row > col, jnp.minimum(sum_col - sum_row, 0.0), 0.0)
    return jnp.where(causal, jnp.exp(spread), 0.0), causal


def quad(a, b, c, d):
    return jnp.concatenate(
        [jnp.concatenate([a, b], axis=1), jnp.concatenate([c, d], axis=1)], axis=0
    )


PAIRS = ((0, 0), (1, 0), (1, 1))


def decay_tiles(decay):
    half = decay.shape[0] // 2
    row, col = iotas(half)
    keys, queries = {}, {}
    for i, j in PAIRS:
        tile = decay[i * half : (i + 1) * half, j * half : (j + 1) * half]
        strict = jnp.where(row > col, tile, 0.0) if i == j else tile
        keys[i, j] = quad(strict, strict, tile, strict if i == j else tile)
        queries[i, j] = jnp.concatenate([tile, tile], axis=1)
    return keys, queries


def tiles(first, second):
    half = first.shape[0] // 2
    return [
        jnp.concatenate([first[:half], second[:half]], axis=0),
        jnp.concatenate([first[half:], second[half:]], axis=0),
    ]


def untiled(pair):
    half = pair[0].shape[0] // 2
    return (
        jnp.concatenate([pair[0][:half], pair[1][:half]], axis=0),
        jnp.concatenate([pair[0][half:], pair[1][half:]], axis=0),
    )


def inverses(systems):
    count = systems[0].shape[0]
    half = count // 2
    row, col = iotas(count)
    row_token, col_token = row & (half - 1), col & (half - 1)
    apart = jnp.where(row_token > col_token, row_token ^ col_token, 0)
    eye = jnp.where(row == col, 1.0, 0.0)
    solved = [eye - jnp.where(row_token == col_token, system, 0.0) for system in systems]
    lows = [system.astype(low) for system in systems]
    size = 1
    while size < half:
        inside = jnp.where((apart >= size) & (apart < 2 * size), 1.0, 0.0).astype(low)
        rounded = [value.astype(low) for value in solved]
        products = [dims(entry * inside, value, 1, 0) for entry, value in zip(lows, rounded)]
        solved = [
            value - dims(kept, product.astype(low), 1, 0)
            for value, kept, product in zip(solved, rounded, products)
        ]
        size *= 2
    refined = []
    for system, value, kept in zip(systems, solved, (parts(value) for value in solved)):
        left = eye - value - three(system, kept)
        refined.append(value + dims(kept[0], left.astype(low), 1, 0))
    return refined


def mixer_values(pieces, taps, beta, rate_col, doc_col, inside, rate_row, doc_row):
    convolved = [short_conv(piece, tap, inside) for piece, tap in zip(pieces, taps)]
    slopes = [sigmoid(value) for value in convolved]
    active = [value * slope for value, slope in zip(convolved, slopes)]
    decay, causal = decay_matrix(rate_col, rate_row, doc_col, doc_row)
    return convolved, slopes, active, decay


def lane_of(shape):
    return lax.broadcasted_iota(jnp.int32, shape, 1)


def pick(values, lane):
    return jnp.sum(jnp.where(lane_of(values.shape) == lane, values, 0.0), axis=1, keepdims=True)


def as_row(col):
    row, column = iotas(col.shape[0])
    return jnp.sum(jnp.where(row == column, col, 0.0), axis=0, keepdims=True)


def head_scalars(head, heads, logits, rates, marks):
    first = sigmoid(pick(logits, head))
    second = sigmoid(pick(logits, heads + head))
    speed = -jnp.exp(pick(rates[0:1], 2 * heads + head))
    soft = pick(logits, 2 * heads + head) + pick(rates[1:2], 2 * heads + head)
    rate = speed * (jnp.maximum(soft, 0.0) + jnp.log1p(jnp.exp(-jnp.abs(soft))))
    doc = marks[:, 0:1]
    inside = [marks[:, 1:2], marks[:, 2:3], marks[:, 3:4]]
    return first, second, speed, soft, rate, doc, inside


def rms_scale(inputs):
    return lax.rsqrt(jnp.mean(inputs * inputs, axis=1, keepdims=True) + norm_eps)


def forward_head(pieces, taps, scalars, doc_row, gain, between):
    first_beta, second_beta, _, _, rate, doc, inside = scalars
    beta = tiles(first_beta, second_beta)
    _, _, active, decay = mixer_values(
        pieces[:5], taps, beta, rate, doc, inside, as_row(rate), doc_row
    )
    half = decay.shape[0] // 2
    width = active[0].shape[1]
    query = unit(active[0])[0] * width ** (-0.5)
    key = tiles(unit(active[1])[0], unit(active[2])[0])
    value = tiles(active[3], active[4])
    key_decay, query_decay = decay_tiles(decay)
    system = {
        (i, j): beta[i] * key_decay[i, j] * three(key[i], key[j], 1, 1) for i, j in PAIRS
    }
    inverse = [parts(entry) for entry in inverses([system[0, 0], system[1, 1]])]
    between()
    first = three(inverse[0], beta[0] * value[0])
    second = three(inverse[1], beta[1] * value[1] - three(system[1, 0], first))
    queries = [query[:half], query[half:]]
    reads = {(i, j): query_decay[i, j] * three(queries[i], key[j], 1, 1) for i, j in PAIRS}
    out = jnp.concatenate(
        [three(reads[0, 0], first), three(reads[1, 0], first) + three(reads[1, 1], second)], axis=0
    )
    gate = pieces[5]
    mixed = out * rms_scale(out) * gain * (gate * sigmoid(gate))
    return mixed.astype(low), inverse, [first, second], out


def tap_slices(tap_ref, head, width):
    inner = tap_ref.shape[1] // 5
    return [
        pl.ds(pl.multiple_of(group * inner + head * width, 128), width) for group in range(5)
    ]


def unpack_lines(line_ref, tap_ref, row_ref, channels, shard_rows):
    for index in range(line_ref.shape[0]):
        lines = line_ref[index].astype(f32)
        tap_ref[:, index * channels : (index + 1) * channels] = lines[0:4, :channels]
        row_ref[0:2, index * shard_rows : (index + 1) * shard_rows] = lines[4:6, :shard_rows]


def forward_kernel(sizes, streams, count, calls, heads, channels, *refs):
    refs = list(refs)
    token_ref, mark_ref, doc_ref, rate_ref, gain_ref = [refs.pop(0) for _ in range(5)]
    shards = [refs.pop(0) for _ in range(count)]
    mixed_ref, piece_ref, inverse_ref, update_ref, out_ref, logit_ref, normed_ref = [
        refs.pop(0) for _ in range(7)
    ]
    tap_ref, row_ref = refs.pop(0), refs.pop(0)
    fulls = [refs.pop(0) for _ in range(count)]
    in_ref, small_ref, line_ref, load_sem = [refs.pop(0) for _ in range(4)]
    head = pl.program_id(0)
    width = gain_ref.shape[1]
    tick, finish = gather_steps(sizes, streams, shards, fulls, refs)

    def ticks(slot):
        for step, place_at in enumerate(calls):
            if place_at % 2 == slot and place_at < 2 * heads:
                pl.when(head == place_at // 2)(functools.partial(tick, step))

    ticks(0)

    @pl.when(head == 0)
    def _():
        copies = [
            pltpu.make_async_copy(fulls[1], small_ref, load_sem.at[1]),
            pltpu.make_async_copy(fulls[2], line_ref, load_sem.at[2]),
        ]
        for copy in copies:
            copy.start()
        row_ref[...] = jnp.zeros_like(row_ref)
        for copy in copies:
            copy.wait()
        shard_rows = shards[0].shape[0]
        devices = row_ref.shape[1] // shard_rows
        unpack_lines(
            line_ref.reshape(devices, *line_ref.shape[4:]), tap_ref, row_ref, channels, shard_rows
        )
        inputs = token_ref[...].astype(f32)
        normed = (inputs * rms_scale(inputs) * row_ref[0:1]).astype(low)
        normed_ref[...] = normed
        logit_ref[...] = dims(normed, small_ref[...].reshape(-1, small_ref.shape[-1]), 1, 0)

    cols = pl.ds(pl.multiple_of(head * 6 * width, 128), 6 * width)
    copy = pltpu.make_async_copy(fulls[0].at[:, :, :, :, :, cols], in_ref, load_sem.at[0])
    copy.start()
    copy.wait()
    projected = dims(normed_ref[...], in_ref[...].reshape(-1, 6 * width), 1, 0)
    piece_ref[0] = projected
    pieces = [projected[:, group * width : (group + 1) * width] for group in range(6)]
    taps = [tap_ref[:, span] for span in tap_slices(tap_ref, head, width)]
    scalars = head_scalars(head, heads, logit_ref[...], rate_ref[...], mark_ref[...])
    mixed, inverse, update, out = forward_head(
        pieces, taps, scalars, doc_ref[0:1], gain_ref[...], lambda: ticks(1)
    )
    mixed_ref[...] = mixed
    for tile in (0, 1):
        inverse_ref[0, 2 * tile] = inverse[tile][0]
        inverse_ref[0, 2 * tile + 1] = inverse[tile][1]
        update_ref[0, tile] = update[tile]
    out_ref[...] = out

    @pl.when(head == heads - 1)
    def _():
        for step, place_at in enumerate(calls):
            if place_at >= 2 * heads:
                tick(step)
        finish()


def plain_forward_kernel(heads, *refs):
    token_ref, mark_ref, doc_ref, rate_ref, gain_ref, in_ref, small_ref, tap_ref, row_ref = refs[:9]
    mixed_ref, piece_ref, inverse_ref, update_ref, out_ref, logit_ref, normed_ref = refs[9:]
    head = pl.program_id(0)
    width = gain_ref.shape[1]

    @pl.when(head == 0)
    def _():
        inputs = token_ref[...].astype(f32)
        normed = (inputs * rms_scale(inputs) * row_ref[0:1]).astype(low)
        normed_ref[...] = normed
        logit_ref[...] = dims(normed, small_ref[...], 1, 0)

    projected = dims(normed_ref[...], in_ref[...], 1, 0)
    piece_ref[0] = projected
    pieces = [projected[:, group * width : (group + 1) * width] for group in range(6)]
    taps = [tap_ref[:, span] for span in tap_slices(tap_ref, head, width)]
    scalars = head_scalars(head, heads, logit_ref[...], rate_ref[...], mark_ref[...])
    mixed, inverse, update, out = forward_head(
        pieces, taps, scalars, doc_ref[0:1], gain_ref[...], lambda: None
    )
    mixed_ref[...] = mixed
    for tile in (0, 1):
        inverse_ref[0, 2 * tile] = inverse[tile][0]
        inverse_ref[0, 2 * tile + 1] = inverse[tile][1]
        update_ref[0, tile] = update[tile]
    out_ref[...] = out


def backward_head(pieces, taps, scalars, doc_row, gain, grad, inverse, update, out):
    first_beta, second_beta, speed, soft, rate, doc, inside = scalars
    beta = tiles(first_beta, second_beta)
    convolved, slopes, active, decay = mixer_values(
        pieces[:5], taps, beta, rate, doc, inside, as_row(rate), doc_row
    )
    count = decay.shape[0]
    half = count // 2
    width = active[0].shape[1]
    root = width ** (-0.5)
    gate = pieces[5]
    scale = rms_scale(out)
    normed = out * scale
    gate_slope = sigmoid(gate)
    opened = gate * gate_slope
    normed_grad = grad * opened * gain
    gain_grad = jnp.sum(grad * opened * normed, axis=0, keepdims=True)
    gate_grad = grad * normed * gain * (gate_slope * (1.0 + gate * (1.0 - gate_slope)))
    out_grad = scale * (normed_grad - normed * jnp.mean(normed_grad * normed, axis=1, keepdims=True))

    query_unit, query_scale = unit(active[0])
    key_first, first_scale = unit(active[1])
    key_second, second_scale = unit(active[2])
    query = query_unit * root
    key = tiles(key_first, key_second)
    value = tiles(active[3], active[4])
    key_decay, query_decay = decay_tiles(decay)
    key_parts = [parts(entry) for entry in key]
    query_parts = [parts(query[:half]), parts(query[half:])]
    key_low = [entry[0] for entry in key_parts]
    query_low = [entry[0] for entry in query_parts]
    update = [parts(entry) for entry in update]
    gram = {(i, j): three(key_parts[i], key_parts[j], 1, 1) for i, j in PAIRS}
    cross = {(i, j): three(query_parts[i], key_parts[j], 1, 1) for i, j in PAIRS}
    reads = {(i, j): parts(query_decay[i, j] * cross[i, j]) for i, j in PAIRS}
    outs = [parts(out_grad[:half]), parts(out_grad[half:])]
    read_grad = {(i, j): three(outs[i], update[j], 1, 1) for i, j in PAIRS}
    first_grad = three(reads[0, 0], outs[0], 0, 0) + three(reads[1, 0], outs[1], 0, 0)
    second_grad = three(reads[1, 1], outs[1], 0, 0)
    target_second = three(inverse[1], second_grad, 0, 0)
    link = beta[1] * key_decay[1, 0] * gram[1, 0]
    target_first = three(inverse[0], first_grad - three(link, target_second, 0, 0), 0, 0)
    target = [target_first, target_second]
    target_parts = [parts(entry) for entry in target]
    beta_grad = [jnp.sum(target[i] * value[i], axis=1, keepdims=True) for i in (0, 1)]
    value_grad = [beta[i] * target[i] for i in (0, 1)]
    key_grad = [None, None]
    query_grad = [None, None]
    energy = {}

    def add(total, term):
        return term if total is None else total + term

    for i, j in PAIRS:
        weighted = -three(target_parts[i], update[j], 1, 1) * key_decay[i, j]
        product = weighted * gram[i, j]
        beta_grad[i] = beta_grad[i] + jnp.sum(product, axis=1, keepdims=True)
        gram_grad = (beta[i] * weighted).astype(low)
        key_energy = beta[i] * product
        key_grad[i] = add(key_grad[i], dims(gram_grad, key_low[j], 1, 0))
        key_grad[j] = add(key_grad[j], dims(gram_grad, key_low[i], 0, 0))
        cross_grad = read_grad[i, j] * query_decay[i, j]
        query_energy = cross_grad * cross[i, j]
        cross_low = cross_grad.astype(low)
        query_grad[i] = add(query_grad[i], dims(cross_low, key_low[j], 1, 0))
        key_grad[j] = add(key_grad[j], dims(cross_low, query_low[i], 0, 0))
        energy[i, j] = (
            key_energy[:half, :half]
            + key_energy[:half, half:]
            + key_energy[half:, :half]
            + key_energy[half:, half:]
            + query_energy[:, :half]
            + query_energy[:, half:]
        )
    whole = quad(energy[0, 0], jnp.zeros((half, half), f32), energy[1, 0], energy[1, 1])
    sum_grad = as_row(jnp.sum(whole, axis=1, keepdims=True)) - jnp.sum(whole, axis=0, keepdims=True)
    row, col = iotas(count)
    rate_grad = jnp.sum(
        jnp.where((doc == doc_row) & (col >= row), sum_grad, 0.0), axis=1, keepdims=True
    )
    first_beta_grad, second_beta_grad = untiled(beta_grad)
    soft_grad = rate_grad * speed * sigmoid(soft)
    log_grad = jnp.sum(rate_grad * rate, axis=0, keepdims=True)
    bias_grad = jnp.sum(soft_grad, axis=0, keepdims=True)
    logit_grads = [
        first_beta_grad * first_beta * (1.0 - first_beta),
        second_beta_grad * second_beta * (1.0 - second_beta),
        soft_grad,
    ]
    first_key_grad, second_key_grad = untiled(key_grad)
    first_value_grad, second_value_grad = untiled(value_grad)
    active_grads = [
        unit_back(query_unit, query_scale, jnp.concatenate(query_grad, axis=0) * root),
        unit_back(key_first, first_scale, first_key_grad),
        unit_back(key_second, second_scale, second_key_grad),
        first_value_grad,
        second_value_grad,
    ]
    piece_grads, tap_grads = [], []
    for group in range(5):
        slope = slopes[group]
        conv_grad = active_grads[group] * (slope * (1.0 + convolved[group] * (1.0 - slope)))
        back, tap_grad = short_conv_back(conv_grad, pieces[group], taps[group], inside)
        piece_grads.append(back.astype(low))
        tap_grads.append(tap_grad)
    piece_grads.append(gate_grad.astype(low))
    return piece_grads, tap_grads, logit_grads, log_grad, bias_grad, gain_grad


def backward_kernel(sizes, streams, count, calls, heads, *refs):
    refs = list(refs)
    token_ref, mark_ref, doc_ref, rate_ref, gain_ref = [refs.pop(0) for _ in range(5)]
    in_ref, small_ref, tap_ref, row_ref = [refs.pop(0) for _ in range(4)]
    grad_ref, piece_ref, inverse_ref, update_ref, out_ref, logit_ref, normed_ref, middle_ref = [
        refs.pop(0) for _ in range(8)
    ]
    terms = [refs.pop(0) for _ in range(count)]
    in_grad_ref, tap_grad_ref, small_grad_ref, sums_ref, gain_grad_ref, token_grad_ref = [
        refs.pop(0) for _ in range(6)
    ]
    sums = [refs.pop(0) for _ in range(count)]
    logit_grad_ref, normed_grad_ref = refs.pop(0), refs.pop(0)
    head = pl.program_id(0)
    if count:
        tick, finish = scatter_steps(sizes, streams, terms, sums, refs)
        for step, place_at in enumerate(calls):
            if place_at < heads:
                pl.when(head == place_at)(functools.partial(tick, step))

    @pl.when(head == 0)
    def _():
        logit_grad_ref[...] = jnp.zeros_like(logit_grad_ref)
        normed_grad_ref[...] = jnp.zeros_like(normed_grad_ref)
        sums_ref[...] = jnp.zeros_like(sums_ref)

    width = gain_ref.shape[1]
    pieces = [piece_ref[0, :, group * width : (group + 1) * width] for group in range(6)]
    spans = tap_slices(tap_ref, head, width)
    taps = [tap_ref[:, span] for span in spans]
    scalars = head_scalars(head, heads, logit_ref[...], rate_ref[...], mark_ref[...])
    piece_grads, tap_grads, logit_grads, log_grad, bias_grad, gain_grad = backward_head(
        pieces,
        taps,
        scalars,
        doc_ref[0:1],
        gain_ref[...],
        grad_ref[...],
        [(inverse_ref[0, 0], inverse_ref[0, 1]), (inverse_ref[0, 2], inverse_ref[0, 3])],
        [update_ref[0, 0], update_ref[0, 1]],
        out_ref[...],
    )
    for group in range(5):
        tap_grad_ref[:, spans[group]] = tap_grads[group]
    projected_grad = jnp.concatenate(piece_grads, axis=1)
    in_grad_ref[...] = dims(normed_ref[...], projected_grad, 0, 0).astype(low)
    normed_grad_ref[...] += dims(projected_grad, in_ref[...], 1, 1)
    lane = lane_of(logit_grad_ref.shape)
    spread = jnp.zeros(logit_grad_ref.shape, f32)
    for index, entry in enumerate(logit_grads):
        spread = spread + jnp.where(lane == index * heads + head, entry, 0.0)
    logit_grad_ref[...] += spread
    line = lane_of((1, width))
    sums_ref[0:1] += jnp.where(line == head, log_grad, 0.0)
    sums_ref[1:2] += jnp.where(line == head, bias_grad, 0.0)
    sums_ref[2:3] += gain_grad

    @pl.when(head == heads - 1)
    def _():
        logit_low = logit_grad_ref[...].astype(low)
        small_grad_ref[...] = dims(normed_ref[...], logit_low, 0, 0).astype(low)
        grad = normed_grad_ref[...] + dims(logit_low, small_ref[...], 1, 1)
        inputs = token_ref[...].astype(f32)
        scale = rms_scale(inputs)
        normed = inputs * scale
        gain_grad_ref[...] = jnp.sum(grad * normed, axis=0, keepdims=True)
        weighted = grad * row_ref[0:1]
        back = scale * (weighted - normed * jnp.mean(weighted * normed, axis=1, keepdims=True))
        token_grad_ref[...] = (middle_ref[...] + back).astype(low)
        if count:
            for step, place_at in enumerate(calls):
                if place_at >= heads:
                    tick(step)
            finish()


def whole_spec(shape):
    return pl.BlockSpec(shape, lambda h: (0,) * len(shape))


def head_spec(*shape):
    return pl.BlockSpec((1,) + shape, lambda h: (h,) + (0,) * len(shape))


def col_spec(rows, width):
    return pl.BlockSpec((rows, width), lambda h: (0, h))


HBM = pl.BlockSpec(memory_space=pltpu.HBM)
VMEM_LIMIT = 62 << 20


def shared_specs(seq_len, model_width, width):
    return [
        whole_spec((seq_len, model_width)),
        whole_spec((seq_len, 8)),
        whole_spec((8, seq_len)),
        whole_spec((8, 128)),
        whole_spec((1, width)),
    ]


def weight_specs(model_width, heads, width):
    return [
        col_spec(model_width, 6 * width),
        whole_spec((model_width, 128)),
        whole_spec((4, heads * 5 * width)),
        whole_spec((8, model_width)),
    ]


def saved_specs(seq_len, model_width, width):
    return [
        head_spec(seq_len, 6 * width),
        head_spec(4, seq_len, seq_len),
        head_spec(2, seq_len, width),
        col_spec(seq_len, width),
        whole_spec((seq_len, 128)),
        whole_spec((seq_len, model_width)),
    ]


def saved_shapes(seq_len, model_width, heads, width):
    return [
        jax.ShapeDtypeStruct((heads, seq_len, 6 * width), f32),
        jax.ShapeDtypeStruct((heads, 4, seq_len, seq_len), low),
        jax.ShapeDtypeStruct((heads, 2, seq_len, width), f32),
        jax.ShapeDtypeStruct((seq_len, heads * width), f32),
        jax.ShapeDtypeStruct((seq_len, 128), f32),
        jax.ShapeDtypeStruct((seq_len, model_width), low),
    ]


def plain_forward(shared, weights, heads):
    seq_len, model_width = shared[0].shape
    width = shared[-1].shape[1]
    outs = pl.pallas_call(
        functools.partial(plain_forward_kernel, heads),
        grid=(heads,),
        in_specs=shared_specs(seq_len, model_width, width)
        + weight_specs(model_width, heads, width),
        out_specs=[col_spec(seq_len, width)] + saved_specs(seq_len, model_width, width),
        out_shape=[jax.ShapeDtypeStruct((seq_len, heads * width), low)]
        + saved_shapes(seq_len, model_width, heads, width),
        compiler_params=pltpu.CompilerParams(vmem_limit_bytes=VMEM_LIMIT),
        name="plain_forward",
    )(*shared, *weights)
    return outs[0], outs[1:]


def mixer_forward(sizes, streams, calls, shared, shards, heads, channels, call):
    seq_len, model_width = shared[0].shape
    width = shared[-1].shape[1]
    count = len(shards)
    total = slots(sizes, streams)
    shape = tuple(sizes[dim] for dim in "zyxc")
    outs = pl.pallas_call(
        functools.partial(forward_kernel, sizes, streams, count, calls, heads, channels),
        grid=(heads,),
        in_specs=shared_specs(seq_len, model_width, width) + [HBM] * count,
        out_specs=[col_spec(seq_len, width)]
        + saved_specs(seq_len, model_width, width)
        + weight_specs(model_width, heads, width)[2:]
        + [HBM] * count,
        out_shape=[jax.ShapeDtypeStruct((seq_len, heads * width), low)]
        + saved_shapes(seq_len, model_width, heads, width)
        + [
            jax.ShapeDtypeStruct((4, heads * 5 * width), f32),
            jax.ShapeDtypeStruct((8, model_width), f32),
        ]
        + [jax.ShapeDtypeStruct(shape + shard.shape, shard.dtype) for shard in shards],
        scratch_shapes=[
            pltpu.VMEM(shape + (shards[0].shape[0], 6 * width), low),
            pltpu.VMEM(shape + shards[1].shape, low),
            pltpu.VMEM(shape + shards[2].shape, low),
            pltpu.SemaphoreType.DMA((3,)),
            pltpu.SemaphoreType.DMA((total,)),
            pltpu.SemaphoreType.DMA((total,)),
            pltpu.SemaphoreType.DMA((count,)),
        ],
        compiler_params=pltpu.CompilerParams(
            vmem_limit_bytes=VMEM_LIMIT, collective_id=call, has_side_effects=True
        ),
        name="mixer_forward",
    )(*shared, *shards)
    fulls = [out.reshape((-1, out.shape[-1])) for out in outs[9:]]
    return outs[0], outs[1:7], fulls[:2] + list(outs[7:9]), fulls[3:]


def mixer_backward(sizes, streams, calls, shared, weights, grad, saved, middle_grad, terms, heads, call):
    seq_len, model_width = shared[0].shape
    width = shared[-1].shape[1]
    count = len(terms)
    scratch = [pltpu.VMEM((seq_len, 128), f32), pltpu.VMEM((seq_len, model_width), f32)]
    extra, blocks = {}, []
    if count:
        extra = dict(collective_id=call, has_side_effects=True)
        blocks, buffers = scatter_setup(sizes, streams, terms)
        scratch = scratch + buffers
    outs = pl.pallas_call(
        functools.partial(backward_kernel, sizes, streams, count, calls, heads),
        grid=(heads,),
        in_specs=shared_specs(seq_len, model_width, width)
        + weight_specs(model_width, heads, width)
        + [col_spec(seq_len, width)]
        + saved_specs(seq_len, model_width, width)
        + [whole_spec((seq_len, model_width))]
        + [HBM] * count,
        out_specs=[
            col_spec(model_width, 6 * width),
            whole_spec((4, heads * 5 * width)),
            whole_spec((model_width, 128)),
            whole_spec((8, width)),
            whole_spec((1, model_width)),
            whole_spec((seq_len, model_width)),
        ]
        + [whole_spec((block.shape[4], block.shape[5])) for block in blocks],
        out_shape=[
            jax.ShapeDtypeStruct((model_width, heads * 6 * width), low),
            jax.ShapeDtypeStruct((4, heads * 5 * width), f32),
            jax.ShapeDtypeStruct((model_width, 128), low),
            jax.ShapeDtypeStruct((8, width), f32),
            jax.ShapeDtypeStruct((1, model_width), f32),
            jax.ShapeDtypeStruct((seq_len, model_width), low),
        ]
        + [jax.ShapeDtypeStruct((block.shape[4], block.shape[5]), f32) for block in blocks],
        scratch_shapes=scratch,
        compiler_params=pltpu.CompilerParams(vmem_limit_bytes=VMEM_LIMIT, **extra),
        name="mixer_backward",
    )(*shared, *weights, grad, *saved, middle_grad, *blocks)
    return outs[:6], outs[6:]


def rms_parts(inputs):
    scale = lax.rsqrt(jnp.mean(inputs * inputs, axis=-1, keepdims=True) + norm_eps)
    return inputs * scale, scale


def rms_back(normed, scale, gain_row, grad):
    weighted = grad * gain_row
    return (
        scale * (weighted - normed * jnp.mean(weighted * normed, axis=-1, keepdims=True)),
        jnp.sum(grad * normed, axis=0),
    )


def gathered(shard):
    return lax.all_gather(shard, AXES, axis=0, tiled=True)


def scattered(whole):
    return lax.psum_scatter(whole, AXES, scatter_dimension=0, tiled=True)


MESH = pl.DeviceIdType.MESH


def grid_of(wide, narrow):
    pair = 2 if narrow % 2 == 0 else 1
    half = 2 if wide % 2 == 0 else 1
    return {"z": wide // half, "y": half, "x": narrow // pair, "c": pair}


def place(sizes):
    wide, narrow = lax.axis_index("wide"), lax.axis_index("narrow")
    return {
        "z": wide // sizes["y"],
        "y": lax.rem(wide, sizes["y"]),
        "x": narrow // sizes["c"],
        "c": lax.rem(narrow, sizes["c"]),
    }


def device(sizes, at):
    return (at["z"] * sizes["y"] + at["y"], at["x"] * sizes["c"] + at["c"])


def moved(sizes, at, dim, step):
    other = dict(at)
    other[dim] = lax.rem(at[dim] + step, sizes[dim])
    return other


def meet(sizes, me):
    barrier = pltpu.get_barrier_semaphore()
    count = 0
    for dim in "zyxc":
        for step in range(1, sizes[dim]):
            pl.semaphore_signal(
                barrier,
                inc=1,
                device_id=device(sizes, moved(sizes, me, dim, step)),
                device_id_type=MESH,
            )
            count += 1
    pl.semaphore_wait(barrier, count)


def slots(sizes, streams):
    return sum(sizes[dim] - 1 for stream in streams for dim in stream[3])


def cut(array, cols, chunks, share, orders, first_lag, per_lag):
    units = cols // 128
    streams, start = [], 0
    edges = []
    for chunk in range(chunks):
        edges += [(chunk + share) / chunks, (chunk + 1) / chunks]
    for index, edge in enumerate(edges):
        stop = round(edge * units)
        if stop > start:
            lag = first_lag + (index // 2) // per_lag
            streams.append((array, start * 128, (stop - start) * 128, orders[index % 2], lag))
        start = stop
    return streams


def agenda(streams, order):
    last = max(stream[4] for stream in streams) + 5
    return [
        [
            (index, phase)
            for phase in order
            for index, stream in enumerate(streams)
            if step - stream[4] == phase
        ]
        for step in range(last)
    ]


def slot_table(sizes, streams):
    table, used = {}, 0
    for index, stream in enumerate(streams):
        for phase in range(4):
            table[index, phase] = used
            used += sizes[stream[3][phase]] - 1
    return table


def gather_steps(sizes, streams, shards, fulls, sems):
    send_sem, recv_sem, local_sem = sems
    table = slot_table(sizes, streams)
    plan = agenda(streams, GATHER_STEPS)

    def local(me):
        return [
            pltpu.make_async_copy(
                shard, full.at[me["z"], me["y"], me["x"], me["c"]], local_sem.at[index]
            )
            for index, (shard, full) in enumerate(zip(shards, fulls))
        ]

    def copies(me, index, phase):
        array, col, width, order, lag = streams[index]
        dim = order[phase]
        block = tuple(slice(None) if d in order[:phase] else me[d] for d in "zyxc")
        target = fulls[array].at[block + (slice(None), pl.ds(col, width))]
        source = shards[array].at[:, pl.ds(col, width)] if phase == 0 else target
        return [
            pltpu.make_async_remote_copy(
                src_ref=source,
                dst_ref=target,
                send_sem=send_sem.at[table[index, phase] + hop - 1],
                recv_sem=recv_sem.at[table[index, phase] + hop - 1],
                device_id=device(sizes, moved(sizes, me, dim, hop)),
                device_id_type=MESH,
            )
            for hop in range(1, sizes[dim])
        ]

    def tick(step):
        me = place(sizes)
        if step == 0:
            for copy in local(me):
                copy.start()
            meet(sizes, me)
        if step == 1:
            for copy in local(me):
                copy.wait()
        for index, phase in plan[step]:
            if phase > 0:
                for copy in copies(me, index, phase - 1):
                    copy.wait_recv()
            if phase < 4:
                for copy in copies(me, index, phase):
                    copy.start()

    def finish():
        me = place(sizes)
        for index in range(len(streams)):
            for phase in range(4):
                for copy in copies(me, index, phase):
                    copy.wait_send()

    return tick, finish


def gather_kernel(sizes, streams, count, *refs):
    tick, finish = gather_steps(
        sizes, streams, refs[:count], refs[count : 2 * count], refs[2 * count :]
    )
    for step in range(len(agenda(streams, GATHER_STEPS))):
        tick(step)
    finish()


def gather(sizes, streams, shards, call):
    count = len(shards)
    total = slots(sizes, streams)
    shape = tuple(sizes[dim] for dim in "zyxc")
    outs = pl.pallas_call(
        functools.partial(gather_kernel, sizes, streams, count),
        out_shape=[jax.ShapeDtypeStruct(shape + shard.shape, shard.dtype) for shard in shards],
        in_specs=[HBM] * count,
        out_specs=[HBM] * count,
        scratch_shapes=[
            pltpu.SemaphoreType.DMA((total,)),
            pltpu.SemaphoreType.DMA((total,)),
            pltpu.SemaphoreType.DMA((count,)),
        ],
        compiler_params=pltpu.CompilerParams(collective_id=call, has_side_effects=True),
        name="weights_gather",
    )(*shards)
    return [out.reshape((-1, out.shape[-1])) for out in outs]


def scatter_setup(sizes, streams, terms):
    shape = tuple(sizes[dim] for dim in "zyxc")
    devices = shape[0] * shape[1] * shape[2] * shape[3]
    blocks = [
        term.reshape(shape + (term.shape[0] // devices, term.shape[1])) for term in terms
    ]
    total = slots(sizes, streams)
    buffers = [
        pltpu.SemaphoreType.DMA((total,)),
        pltpu.SemaphoreType.DMA((total,)),
        pltpu.SemaphoreType.DMA((len(streams),)),
    ]
    for array, col, width, order, lag in streams:
        tail = (blocks[array].shape[4], width)
        buffers.append(pltpu.VMEM(shape[:3] + tail, low))
        for phase in range(4):
            kept = tuple(sizes[dim] for dim in "zyx" if dim not in order[: phase + 1])
            buffers.append(pltpu.VMEM((sizes[order[phase]] - 1,) + kept + tail, low))
    return blocks, buffers


def scatter_steps(sizes, streams, terms, sums, refs):
    send_sem, recv_sem, local_sem = refs[:3]
    held = [refs[3 + 5 * index] for index in range(len(streams))]
    got = {
        (index, phase): refs[4 + 5 * index + phase]
        for index in range(len(streams))
        for phase in range(4)
    }
    table = slot_table(sizes, streams)
    plan = agenda(streams, SCATTER_STEPS)

    def load(me, index):
        array, col, width, order, lag = streams[index]
        return pltpu.make_async_copy(
            terms[array].at[:, :, :, me["c"], :, pl.ds(col, width)], held[index], local_sem.at[index]
        )

    def copies(me, index, phase):
        array, col, width, order, lag = streams[index]
        dim = order[phase]
        found = []
        for hop in range(1, sizes[dim]):
            to = moved(sizes, me, dim, hop)
            if phase == 0:
                source = terms[array].at[:, :, :, to["c"], :, pl.ds(col, width)]
            else:
                block = tuple(
                    me[d] if d in order[:phase] else (to[d] if d == dim else slice(None))
                    for d in "zyx"
                )
                source = held[index].at[block]
            found.append(
                pltpu.make_async_remote_copy(
                    src_ref=source,
                    dst_ref=got[index, phase].at[hop - 1],
                    send_sem=send_sem.at[table[index, phase] + hop - 1],
                    recv_sem=recv_sem.at[table[index, phase] + hop - 1],
                    device_id=device(sizes, to),
                    device_id_type=MESH,
                )
            )
        return found

    def combine(me, index, phase):
        array, col, width, order, lag = streams[index]
        kept = [d for d in "zyx" if d not in order[: phase + 1]]
        total = 1
        for d in kept:
            total *= sizes[d]

        def body(flat, carry):
            at, rest = dict(me), flat
            for d in reversed(kept):
                at[d] = lax.rem(rest, sizes[d])
                rest = rest // sizes[d]
            where = tuple(at[d] for d in "zyx")
            inner = tuple(at[d] for d in kept)
            value = held[index][where]
            others = [got[index, phase][(hop,) + inner] for hop in range(sizes[order[phase]] - 1)]
            if phase == 3 or len(others) > 1:
                value = value.astype(f32)
                for other in others:
                    value = value + other.astype(f32)
            else:
                value = value + others[0]
            if phase == 3:
                sums[array][:, pl.ds(col, width)] = value
            else:
                held[index][where] = value.astype(low)
            return carry

        if total == 1:
            body(0, 0)
        else:
            lax.fori_loop(0, total, body, 0)

    def tick(step):
        me = place(sizes)
        if step == 0:
            for index in range(len(streams)):
                load(me, index).start()
            meet(sizes, me)
        for index, phase in plan[step]:
            if phase > 0:
                for copy in copies(me, index, phase - 1):
                    copy.wait_recv()
                if phase == 1:
                    load(me, index).wait()
                combine(me, index, phase - 1)
            if phase < 4:
                for copy in copies(me, index, phase):
                    copy.start()

    def finish():
        me = place(sizes)
        for index in range(len(streams)):
            for phase in range(4):
                for copy in copies(me, index, phase):
                    copy.wait_send()

    return tick, finish


def small_buffers(sizes, shape):
    return [pltpu.VMEM((2,) + shape, f32) for _ in "cxy"] + [
        pltpu.VMEM((sizes["z"],) + shape, f32),
        pltpu.SemaphoreType.DMA((4, sizes["z"])),
        pltpu.SemaphoreType.DMA((4, sizes["z"])),
    ]


def small_steps(sizes, small, total, refs):
    boxes, lanes, small_send, small_recv = refs[:3], refs[3], refs[4], refs[5]

    def copies(me, phase):
        dim = "cxyz"[phase]
        source = small if phase == 0 else boxes[phase - 1].at[1]
        source = lanes.at[me["z"]] if dim == "z" else source
        return [
            pltpu.make_async_remote_copy(
                src_ref=source,
                dst_ref=lanes.at[me["z"]] if dim == "z" else boxes[phase].at[0],
                send_sem=small_send.at[phase, hop],
                recv_sem=small_recv.at[phase, hop],
                device_id=device(sizes, moved(sizes, me, dim, hop)),
                device_id_type=MESH,
            )
            for hop in range(1, sizes[dim])
        ]

    def tick(step):
        me = place(sizes)
        if step > 0:
            for copy in copies(me, step - 1):
                copy.wait_recv()
            if step < 4:
                mine = small[...] if step == 1 else boxes[step - 2][1]
                boxes[step - 1][1] = mine + boxes[step - 1][0]
            else:
                value = lanes[0]
                for index in range(1, sizes["z"]):
                    value = value + lanes[index]
                total[...] = value
        if step < 4:
            if step == 3:
                lanes[me["z"]] = boxes[2][1]
            for copy in copies(me, step):
                copy.start()

    def finish():
        me = place(sizes)
        for phase in range(4):
            for copy in copies(me, phase):
                copy.wait_send()

    return tick, finish


def scatter_kernel(sizes, streams, count, *refs):
    terms, small = refs[:count], refs[count]
    sums, total = refs[count + 1 : 2 * count + 1], refs[2 * count + 1]
    rest = refs[2 * count + 2 :]
    tick, finish = scatter_steps(sizes, streams, terms, sums, rest[:-6])
    small_tick, small_finish = small_steps(sizes, small, total, rest[-6:])
    for step in range(len(agenda(streams, SCATTER_STEPS))):
        tick(step)
        if step < 5:
            small_tick(step)
    finish()
    small_finish()


def scatter(sizes, streams, terms, small, call):
    count = len(terms)
    blocks, buffers = scatter_setup(sizes, streams, terms)
    vmem = pl.BlockSpec(memory_space=pltpu.VMEM)
    return pl.pallas_call(
        functools.partial(scatter_kernel, sizes, streams, count),
        out_shape=[
            jax.ShapeDtypeStruct((block.shape[4], block.shape[5]), f32) for block in blocks
        ]
        + [jax.ShapeDtypeStruct(small.shape, f32)],
        in_specs=[HBM] * count + [vmem],
        out_specs=[vmem] * (count + 1),
        scratch_shapes=buffers + small_buffers(sizes, small.shape),
        compiler_params=pltpu.CompilerParams(
            collective_id=call, has_side_effects=True, vmem_limit_bytes=VMEM_LIMIT
        ),
        name="grads_scatter",
    )(*blocks, small)


GATHER_STEPS = (0, 1, 2, 3, 4)
SCATTER_STEPS = (0, 1, 3, 2, 4)
GATHER_ORDERS = ("zxyc", "yzxc")
SCATTER_ORDERS = ("cyxz", "cxzy")


FORWARD_PLAN = ((4, 0, 1), (1, 0, 1), (1, 0, 1), (1, 4, 1), (4, 4, 1), (2, 8, 1))
FORWARD_CALLS = (0, 0, 0, 0, 0, 2, 4, 6, 8, 10, 12, 14, 16, 16)


def planned(terms, orders, chunks):
    streams = []
    for index, (count, lag, per_lag) in enumerate(chunks):
        streams += cut(index, terms[index].shape[1], count, 0.64, orders, lag, per_lag)
    return streams


def per_device(
    sizes,
    tokens,
    doc_ids,
    attn_gain,
    mixer_in,
    mixer_small,
    conv_weight,
    decay_log,
    decay_bias,
    out_gain,
    mixer_out,
    ffn_gain,
    ffn_in,
    ffn_out,
    out_grad,
):
    row_count, seq_len, model_width = tokens.shape
    heads, width = decay_log.shape[0], out_gain.shape[0]
    shard_rows = mixer_in.shape[0]
    small_cols = mixer_small.shape[1]
    channels = conv_weight.shape[0]
    devices = model_width // shard_rows
    ff_width = ffn_out.shape[0]
    own = (
        shard_rows % 16 == 0
        and row_count == 1
        and sizes["x"] == 2
        and sizes["y"] == 2
        and sizes["c"] == 2
    )
    in_shard = (
        mixer_in.astype(low)
        .reshape(shard_rows, 6, heads, width)
        .transpose(0, 2, 1, 3)
        .reshape(shard_rows, -1)
    )
    small_shard = jnp.pad(mixer_small.astype(low), ((0, 0), (0, 128 - small_cols)))
    line_width = channels + (-channels % 128)
    lines_shard = jnp.concatenate(
        [
            jnp.pad(conv_weight.astype(low).T, ((0, 0), (0, line_width - channels))),
            jnp.pad(
                jnp.stack([attn_gain, ffn_gain]).astype(low), ((0, 10), (0, line_width - shard_rows))
            ),
        ]
    )
    out_shard, ffn_out_shard = mixer_out.astype(low).T, ffn_out.astype(low).T
    late_shards = [out_shard, ffn_in.astype(low), ffn_out_shard]
    early_shards = [in_shard, small_shard, lines_shard]
    rates = jnp.pad(
        jnp.stack([decay_log, decay_bias]), ((0, 6), (2 * heads, 128 - 3 * heads))
    )

    def shared(index):
        doc = doc_ids[index].astype(f32)
        before = [
            jnp.concatenate([jnp.full((distance,), -1.0), doc[:-distance]]) for distance in (1, 2, 3)
        ]
        marks = jnp.stack([doc] + [jnp.where(entry == doc, 1.0, 0.0) for entry in before], axis=1)
        return [
            tokens[index],
            jnp.pad(marks, ((0, 0), (0, 4))),
            jnp.broadcast_to(doc[None], (8, seq_len)),
            rates,
            out_gain[None],
        ]

    each = [shared(index) for index in range(row_count)]
    if own:
        shards = early_shards + late_shards
        mixed, saved, weights, late_full = mixer_forward(
            sizes,
            planned(shards, GATHER_ORDERS, FORWARD_PLAN),
            FORWARD_CALLS,
            each[0],
            shards,
            heads,
            channels,
            1,
        )
        saves = [saved]
        ffn_row = weights[3][1:2]
    else:
        in_full, small_full, lines = [gathered(shard) for shard in early_shards]
        lines = lines.reshape(devices, 16, line_width).astype(f32)
        taps = lines[:, :4, :channels].transpose(1, 0, 2).reshape(4, -1)
        rows = lines[:, 4:6, :shard_rows].transpose(1, 0, 2).reshape(2, model_width)
        ffn_row = rows[1:2]
        weights = [in_full, small_full, taps, jnp.pad(rows, ((0, 6), (0, 0)))]
        done = [plain_forward(entry, weights, heads) for entry in each]
        mixed = jnp.concatenate([entry[0] for entry in done])
        saves = [entry[1] for entry in done]
        late_full = [gathered(shard) for shard in late_shards]
    out_t, ffn_in_full, ffn_out_t = late_full

    inputs = tokens.reshape(row_count * seq_len, model_width).astype(f32)
    middle = inputs + dims(mixed, out_t, 1, 1)
    ffn_normed, ffn_scale = rms_parts(middle)
    ffn_rows = (ffn_normed * ffn_row).astype(low)
    gate_up = jnp.dot(ffn_rows, ffn_in_full, preferred_element_type=f32)
    gate, up = gate_up[:, :ff_width], gate_up[:, ff_width:]
    slope = jax.nn.sigmoid(gate)
    hidden = (gate * slope * up).astype(low)
    result = middle + dims(hidden, ffn_out_t, 1, 1)
    grad_low = out_grad.reshape(row_count * seq_len, model_width)
    ffn_out_term = dims(grad_low, hidden, 0, 0).astype(low)
    hidden_grad = jnp.dot(grad_low, ffn_out_t, preferred_element_type=f32)
    gate_up_grad = jnp.concatenate(
        [hidden_grad * up * slope * (1.0 + gate * (1.0 - slope)), hidden_grad * gate * slope],
        axis=1,
    ).astype(low)
    ffn_in_term = dims(ffn_rows, gate_up_grad, 0, 0).astype(low)
    rows_grad = dims(gate_up_grad, ffn_in_full, 1, 1)
    middle_norm_grad, ffn_gain_term = rms_back(ffn_normed, ffn_scale, ffn_row, rows_grad)
    middle_grad = grad_low.astype(f32) + middle_norm_grad
    branch_grad = middle_grad.astype(low)
    out_term = dims(branch_grad, mixed, 0, 0).astype(low)
    mixed_grad = jnp.dot(branch_grad, out_t, preferred_element_type=f32)
    late_terms = [ffn_out_term, ffn_in_term, out_term]
    if own:
        late = planned(late_terms, SCATTER_ORDERS, ((2, 0, 1), (4, 2, 1), (1, 6, 1)))
        grads, late_sums = mixer_backward(
            sizes,
            late,
            (0, 1, 2, 3, 4, 5, 6, 7, 8, 8, 8),
            each[0],
            weights,
            mixed_grad,
            saves[0],
            middle_grad,
            late_terms,
            heads,
            3,
        )
        grads = [grads]
    else:
        grads = [
            mixer_backward(
                sizes,
                [],
                (),
                entry,
                weights,
                mixed_grad[index * seq_len : (index + 1) * seq_len],
                saves[index],
                middle_grad[index * seq_len : (index + 1) * seq_len],
                [],
                heads,
                3,
            )[0]
            for index, entry in enumerate(each)
        ]
        late_sums = [scattered(term).astype(f32) for term in late_terms]
    in_term, tap_term, small_term, small, attn_gain_term = [
        sum(entry[index] for entry in grads[1:]) + grads[0][index] if row_count > 1 else grads[0][index]
        for index in range(5)
    ]
    input_grad = jnp.stack([entry[5] for entry in grads])
    tap_term = tap_term.reshape(4, devices, channels).transpose(1, 0, 2)
    gain_terms = jnp.stack(
        [attn_gain_term.reshape(devices, shard_rows), ffn_gain_term.reshape(devices, shard_rows)],
        axis=1,
    )
    lines_term = jnp.concatenate(
        [
            jnp.pad(tap_term, ((0, 0), (0, 0), (0, line_width - channels))),
            jnp.pad(gain_terms, ((0, 0), (0, 10), (0, line_width - shard_rows))),
        ],
        axis=1,
    )
    lines_term = lines_term.astype(low).reshape(devices * 16, line_width)
    early_terms = [in_term, small_term, lines_term]
    if own:
        early = planned(early_terms, SCATTER_ORDERS, ((8, 0, 2), (1, 0, 1), (1, 0, 1)))
        in_sum, small_sum, lines_sum, small = scatter(sizes, early, early_terms, small, 4)
    else:
        in_sum, small_sum, lines_sum = [scattered(term).astype(f32) for term in early_terms]
        small = lax.psum(small, AXES)
    in_sum = (
        in_sum.reshape(shard_rows, heads, 6, width).transpose(0, 2, 1, 3).reshape(shard_rows, -1)
    )
    ffn_out_sum, ffn_in_sum, out_sum = late_sums
    outputs = result.astype(low).reshape(row_count, seq_len, model_width)
    return (
        outputs,
        input_grad,
        lines_sum[4, :shard_rows],
        in_sum,
        small_sum[:, :small_cols],
        lines_sum[:4, :channels].T,
        small[0, :heads],
        small[1, :heads],
        small[2],
        out_sum.T,
        lines_sum[5, :shard_rows],
        ffn_in_sum,
        ffn_out_sum.T,
    )


def solution(mesh):
    both = P(AXES)
    line = P(None, AXES)
    in_specs = (both, both, both, both, both, both, P(), P(), P(), line, both, both, line, both)
    out_specs = (both, both, both, both, both, both, P(), P(), P(), line, both, both, line)
    sizes = grid_of(mesh.shape["wide"], mesh.shape["narrow"])
    return jax.shard_map(
        functools.partial(per_device, sizes),
        mesh=mesh, in_specs=in_specs, out_specs=out_specs, check_vma=False
    )
```

```python
import functools
import jax
import jax.numpy as jnp
from jax import lax
from jax.experimental import pallas as pl
from jax.experimental.pallas import tpu as pltpu
from jax.sharding import PartitionSpec as P

norm_eps = 1e-06
low = jnp.bfloat16
f32 = jnp.float32
AXES = ("wide", "narrow")


def dims(left, right, left_dim, right_dim):
    return lax.dot_general(
        left, right, (((left_dim,), (right_dim,)), ((), ())), preferred_element_type=f32
    )


def one(left, right, left_dim=1, right_dim=0):
    return dims(left.astype(low), right.astype(low), left_dim, right_dim)


def parts(value):
    high = value.astype(low)
    return high, (value - high.astype(f32)).astype(low)


def three(left, right, left_dim=1, right_dim=0):
    left_high, left_rest = left if isinstance(left, tuple) else parts(left)
    right_high, right_rest = right if isinstance(right, tuple) else parts(right)
    return (
        dims(left_high, right_high, left_dim, right_dim)
        + dims(left_high, right_rest, left_dim, right_dim)
        + dims(left_rest, right_high, left_dim, right_dim)
    )


def sigmoid(value):
    return 1.0 / (1.0 + jnp.exp(-value))


def later(value, distance):
    return pltpu.roll(value, distance % value.shape[0], 0)


def short_conv(rows, taps, inside):
    summed = rows * taps[3:4]
    for distance in (1, 2, 3):
        summed = summed + later(rows, distance) * inside[distance - 1] * taps[3 - distance : 4 - distance]
    return summed


def short_conv_back(grad, rows, taps, inside):
    back = grad * taps[3:4]
    tap_grads = [jnp.sum(grad * rows, axis=0, keepdims=True)]
    for distance in (1, 2, 3):
        masked = grad * inside[distance - 1]
        back = back + later(masked, -distance) * taps[3 - distance : 4 - distance]
        tap_grads.append(jnp.sum(masked * later(rows, distance), axis=0, keepdims=True))
    return back, jnp.concatenate(tap_grads[::-1], axis=0)


def unit(rows):
    scale = lax.rsqrt(jnp.sum(rows * rows, axis=1, keepdims=True) + norm_eps)
    return rows * scale, scale


def unit_back(normed, scale, grad):
    return scale * (grad - normed * jnp.sum(grad * normed, axis=1, keepdims=True))


def iotas(count):
    return (
        lax.broadcasted_iota(jnp.int32, (count, count), 0),
        lax.broadcasted_iota(jnp.int32, (count, count), 1),
    )


def decay_matrix(rate_col, rate_row, doc_col, doc_row):
    row, col = iotas(rate_col.shape[0])
    same = doc_col == doc_row
    causal = same & (row >= col)
    sum_col = jnp.sum(jnp.where(causal, rate_row, 0.0), axis=1, keepdims=True)
    sum_row = jnp.sum(jnp.where(same & (row <= col), rate_col, 0.0), axis=0, keepdims=True)
    spread = jnp.where(row > col, jnp.minimum(sum_col - sum_row, 0.0), 0.0)
    return jnp.where(causal, jnp.exp(spread), 0.0), causal


def quad(a, b, c, d):
    return jnp.concatenate(
        [jnp.concatenate([a, b], axis=1), jnp.concatenate([c, d], axis=1)], axis=0
    )


PAIRS = ((0, 0), (1, 0), (1, 1))


def decay_tiles(decay):
    half = decay.shape[0] // 2
    row, col = iotas(half)
    keys, queries = {}, {}
    for i, j in PAIRS:
        tile = decay[i * half : (i + 1) * half, j * half : (j + 1) * half]
        strict = jnp.where(row > col, tile, 0.0) if i == j else tile
        keys[i, j] = quad(strict, strict, tile, strict if i == j else tile)
        queries[i, j] = jnp.concatenate([tile, tile], axis=1)
    return keys, queries


def tiles(first, second):
    half = first.shape[0] // 2
    return [
        jnp.concatenate([first[:half], second[:half]], axis=0),
        jnp.concatenate([first[half:], second[half:]], axis=0),
    ]


def untiled(pair):
    half = pair[0].shape[0] // 2
    return (
        jnp.concatenate([pair[0][:half], pair[1][:half]], axis=0),
        jnp.concatenate([pair[0][half:], pair[1][half:]], axis=0),
    )


def inverses(systems):
    count = systems[0].shape[0]
    half = count // 2
    row, col = iotas(count)
    row_token, col_token = row & (half - 1), col & (half - 1)
    apart = jnp.where(row_token > col_token, row_token ^ col_token, 0)
    eye = jnp.where(row == col, 1.0, 0.0)
    solved = [eye - jnp.where(row_token == col_token, system, 0.0) for system in systems]
    lows = [system.astype(low) for system in systems]
    size = 1
    while size < half:
        inside = jnp.where((apart >= size) & (apart < 2 * size), 1.0, 0.0).astype(low)
        rounded = [value.astype(low) for value in solved]
        products = [dims(entry * inside, value, 1, 0) for entry, value in zip(lows, rounded)]
        solved = [
            value - dims(kept, product.astype(low), 1, 0)
            for value, kept, product in zip(solved, rounded, products)
        ]
        size *= 2
    refined = []
    for system, value, kept in zip(systems, solved, (parts(value) for value in solved)):
        left = eye - value - three(system, kept)
        refined.append(value + dims(kept[0], left.astype(low), 1, 0))
    return refined


def mixer_values(pieces, taps, beta, rate_col, doc_col, inside, rate_row, doc_row):
    convolved = [short_conv(piece, tap, inside) for piece, tap in zip(pieces, taps)]
    slopes = [sigmoid(value) for value in convolved]
    active = [value * slope for value, slope in zip(convolved, slopes)]
    decay, causal = decay_matrix(rate_col, rate_row, doc_col, doc_row)
    return convolved, slopes, active, decay


def lane_of(shape):
    return lax.broadcasted_iota(jnp.int32, shape, 1)


def pick(values, lane):
    return jnp.sum(jnp.where(lane_of(values.shape) == lane, values, 0.0), axis=1, keepdims=True)


def as_row(col):
    row, column = iotas(col.shape[0])
    return jnp.sum(jnp.where(row == column, col, 0.0), axis=0, keepdims=True)


def head_scalars(head, heads, logits, log_row, bias_row, marks):
    first = sigmoid(pick(logits, head))
    second = sigmoid(pick(logits, heads + head))
    speed = -jnp.exp(pick(log_row, head))
    soft = pick(logits, 2 * heads + head) + pick(bias_row, head)
    rate = speed * (jnp.maximum(soft, 0.0) + jnp.log1p(jnp.exp(-jnp.abs(soft))))
    doc = marks[:, 0:1]
    inside = [marks[:, 1:2], marks[:, 2:3], marks[:, 3:4]]
    return first, second, speed, soft, rate, doc, inside


def rms_scale(inputs):
    return lax.rsqrt(jnp.mean(inputs * inputs, axis=1, keepdims=True) + norm_eps)


def forward_head(pieces, taps, scalars, doc_row, gain, between):
    first_beta, second_beta, _, _, rate, doc, inside = scalars
    beta = tiles(first_beta, second_beta)
    _, _, active, decay = mixer_values(
        pieces[:5], taps, beta, rate, doc, inside, as_row(rate), doc_row
    )
    half = decay.shape[0] // 2
    width = active[0].shape[1]
    query = unit(active[0])[0] * width ** (-0.5)
    key = tiles(unit(active[1])[0], unit(active[2])[0])
    value = tiles(active[3], active[4])
    key_decay, query_decay = decay_tiles(decay)
    system = {
        (i, j): beta[i] * key_decay[i, j] * three(key[i], key[j], 1, 1) for i, j in PAIRS
    }
    inverse = [parts(entry) for entry in inverses([system[0, 0], system[1, 1]])]
    between()
    first = three(inverse[0], beta[0] * value[0])
    second = three(inverse[1], beta[1] * value[1] - three(system[1, 0], first))
    queries = [query[:half], query[half:]]
    reads = {(i, j): query_decay[i, j] * three(queries[i], key[j], 1, 1) for i, j in PAIRS}
    out = jnp.concatenate(
        [three(reads[0, 0], first), three(reads[1, 0], first) + three(reads[1, 1], second)], axis=0
    )
    gate = pieces[5]
    mixed = out * rms_scale(out) * gain * (gate * sigmoid(gate))
    return mixed.astype(low), inverse, [first, second], out


def tap_slices(tap_ref, head, width):
    inner = tap_ref.shape[1] // 5
    return [
        pl.ds(pl.multiple_of(group * inner + head * width, 128), width) for group in range(5)
    ]


def mark_documents(id_ref, mark_ref, doc_ref):
    doc_row = id_ref[...].astype(f32)
    row, col = iotas(doc_row.shape[1])
    lane = lane_of(mark_ref.shape)
    doc = jnp.sum(jnp.where(row == col, doc_row, 0.0), axis=1, keepdims=True)
    marks = jnp.where(lane == 0, doc, 0.0)
    place_in_row = lax.broadcasted_iota(jnp.int32, doc.shape, 0)
    for distance in (1, 2, 3):
        before = jnp.sum(jnp.where(col == row - distance, doc_row, 0.0), axis=1, keepdims=True)
        inside = (before == doc) & (place_in_row >= distance)
        marks = jnp.where((lane == distance) & inside, 1.0, marks)
    mark_ref[...] = marks
    doc_ref[...] = jnp.broadcast_to(doc_row, doc_ref.shape)


def unpack_lines(line_ref, tap_ref, row_ref, channels, shard_rows):
    for index in range(line_ref.shape[0]):
        lines = line_ref[index].astype(f32)
        tap_ref[:, index * channels : (index + 1) * channels] = lines[0:4, :channels]
        row_ref[0:2, index * shard_rows : (index + 1) * shard_rows] = lines[4:6, :shard_rows]


def forward_kernel(sizes, streams, count, calls, heads, channels, *refs):
    refs = list(refs)
    token_ref, id_ref, log_ref, bias_ref, gain_ref = [refs.pop(0) for _ in range(5)]
    shards = [refs.pop(0) for _ in range(count)]
    mixed_ref, piece_ref, inverse_ref, update_ref, out_ref, logit_ref, normed_ref = [
        refs.pop(0) for _ in range(7)
    ]
    tap_ref, row_ref, mark_ref, doc_ref = [refs.pop(0) for _ in range(4)]
    fulls = [refs.pop(0) for _ in range(count)]
    in_ref, small_ref, line_ref, load_sem = [refs.pop(0) for _ in range(4)]
    head = pl.program_id(0)
    width = gain_ref.shape[1]
    tick, finish = gather_steps(sizes, streams, shards, fulls, refs)

    def ticks(slot):
        for step, place_at in enumerate(calls):
            if place_at % 2 == slot and place_at < 2 * heads:
                pl.when(head == place_at // 2)(functools.partial(tick, step))

    ticks(0)

    @pl.when(head == 0)
    def _():
        copies = [
            pltpu.make_async_copy(fulls[1], small_ref, load_sem.at[1]),
            pltpu.make_async_copy(fulls[2], line_ref, load_sem.at[2]),
        ]
        for copy in copies:
            copy.start()
        row_ref[...] = jnp.zeros_like(row_ref)
        mark_documents(id_ref, mark_ref, doc_ref)
        for copy in copies:
            copy.wait()
        shard_rows = shards[0].shape[0]
        devices = row_ref.shape[1] // shard_rows
        unpack_lines(
            line_ref.reshape(devices, *line_ref.shape[4:]), tap_ref, row_ref, channels, shard_rows
        )
        inputs = token_ref[...].astype(f32)
        normed = (inputs * rms_scale(inputs) * row_ref[0:1]).astype(low)
        normed_ref[...] = normed
        logit_ref[...] = dims(normed, small_ref[...].reshape(-1, small_ref.shape[-1]), 1, 0)

    cols = pl.ds(pl.multiple_of(head * 6 * width, 128), 6 * width)
    copy = pltpu.make_async_copy(fulls[0].at[:, :, :, :, :, cols], in_ref, load_sem.at[0])
    copy.start()
    copy.wait()
    projected = dims(normed_ref[...], in_ref[...].reshape(-1, 6 * width), 1, 0)
    piece_ref[0] = projected
    pieces = [projected[:, group * width : (group + 1) * width] for group in range(6)]
    taps = [tap_ref[:, span] for span in tap_slices(tap_ref, head, width)]
    scalars = head_scalars(
        head, heads, logit_ref[...], log_ref[...], bias_ref[...], mark_ref[...]
    )
    mixed, inverse, update, out = forward_head(
        pieces, taps, scalars, doc_ref[0:1], gain_ref[...], lambda: ticks(1)
    )
    mixed_ref[...] = mixed
    for tile in (0, 1):
        inverse_ref[0, 2 * tile] = inverse[tile][0]
        inverse_ref[0, 2 * tile + 1] = inverse[tile][1]
        update_ref[0, tile] = update[tile]
    out_ref[...] = out

    @pl.when(head == heads - 1)
    def _():
        for step, place_at in enumerate(calls):
            if place_at >= 2 * heads:
                tick(step)
        finish()


def plain_forward_kernel(heads, *refs):
    token_ref, log_ref, bias_ref, gain_ref = refs[:4]
    in_ref, small_ref, tap_ref, row_ref, mark_ref, doc_ref = refs[4:10]
    mixed_ref, piece_ref, inverse_ref, update_ref, out_ref, logit_ref, normed_ref = refs[10:]
    head = pl.program_id(0)
    width = gain_ref.shape[1]

    @pl.when(head == 0)
    def _():
        inputs = token_ref[...].astype(f32)
        normed = (inputs * rms_scale(inputs) * row_ref[0:1]).astype(low)
        normed_ref[...] = normed
        logit_ref[...] = dims(normed, small_ref[...], 1, 0)

    projected = dims(normed_ref[...], in_ref[...], 1, 0)
    piece_ref[0] = projected
    pieces = [projected[:, group * width : (group + 1) * width] for group in range(6)]
    taps = [tap_ref[:, span] for span in tap_slices(tap_ref, head, width)]
    scalars = head_scalars(
        head, heads, logit_ref[...], log_ref[...], bias_ref[...], mark_ref[...]
    )
    mixed, inverse, update, out = forward_head(
        pieces, taps, scalars, doc_ref[0:1], gain_ref[...], lambda: None
    )
    mixed_ref[...] = mixed
    for tile in (0, 1):
        inverse_ref[0, 2 * tile] = inverse[tile][0]
        inverse_ref[0, 2 * tile + 1] = inverse[tile][1]
        update_ref[0, tile] = update[tile]
    out_ref[...] = out


def backward_head(pieces, taps, scalars, doc_row, gain, grad, inverse, update, out):
    first_beta, second_beta, speed, soft, rate, doc, inside = scalars
    beta = tiles(first_beta, second_beta)
    convolved, slopes, active, decay = mixer_values(
        pieces[:5], taps, beta, rate, doc, inside, as_row(rate), doc_row
    )
    count = decay.shape[0]
    half = count // 2
    width = active[0].shape[1]
    root = width ** (-0.5)
    gate = pieces[5]
    scale = rms_scale(out)
    normed = out * scale
    gate_slope = sigmoid(gate)
    opened = gate * gate_slope
    normed_grad = grad * opened * gain
    gain_grad = jnp.sum(grad * opened * normed, axis=0, keepdims=True)
    gate_grad = grad * normed * gain * (gate_slope * (1.0 + gate * (1.0 - gate_slope)))
    out_grad = scale * (normed_grad - normed * jnp.mean(normed_grad * normed, axis=1, keepdims=True))

    query_unit, query_scale = unit(active[0])
    key_first, first_scale = unit(active[1])
    key_second, second_scale = unit(active[2])
    query = query_unit * root
    key = tiles(key_first, key_second)
    value = tiles(active[3], active[4])
    key_decay, query_decay = decay_tiles(decay)
    key_parts = [parts(entry) for entry in key]
    query_parts = [parts(query[:half]), parts(query[half:])]
    key_low = [entry[0] for entry in key_parts]
    query_low = [entry[0] for entry in query_parts]
    update = [parts(entry) for entry in update]
    gram = {(i, j): three(key_parts[i], key_parts[j], 1, 1) for i, j in PAIRS}
    cross = {(i, j): three(query_parts[i], key_parts[j], 1, 1) for i, j in PAIRS}
    reads = {(i, j): parts(query_decay[i, j] * cross[i, j]) for i, j in PAIRS}
    outs = [parts(out_grad[:half]), parts(out_grad[half:])]
    read_grad = {(i, j): three(outs[i], update[j], 1, 1) for i, j in PAIRS}
    first_grad = three(reads[0, 0], outs[0], 0, 0) + three(reads[1, 0], outs[1], 0, 0)
    second_grad = three(reads[1, 1], outs[1], 0, 0)
    target_second = three(inverse[1], second_grad, 0, 0)
    link = beta[1] * key_decay[1, 0] * gram[1, 0]
    target_first = three(inverse[0], first_grad - three(link, target_second, 0, 0), 0, 0)
    target = [target_first, target_second]
    target_parts = [parts(entry) for entry in target]
    beta_grad = [jnp.sum(target[i] * value[i], axis=1, keepdims=True) for i in (0, 1)]
    value_grad = [beta[i] * target[i] for i in (0, 1)]
    key_grad = [None, None]
    query_grad = [None, None]
    energy = {}

    def add(total, term):
        return term if total is None else total + term

    for i, j in PAIRS:
        weighted = -three(target_parts[i], update[j], 1, 1) * key_decay[i, j]
        product = weighted * gram[i, j]
        beta_grad[i] = beta_grad[i] + jnp.sum(product, axis=1, keepdims=True)
        gram_grad = (beta[i] * weighted).astype(low)
        key_energy = beta[i] * product
        key_grad[i] = add(key_grad[i], dims(gram_grad, key_low[j], 1, 0))
        key_grad[j] = add(key_grad[j], dims(gram_grad, key_low[i], 0, 0))
        cross_grad = read_grad[i, j] * query_decay[i, j]
        query_energy = cross_grad * cross[i, j]
        cross_low = cross_grad.astype(low)
        query_grad[i] = add(query_grad[i], dims(cross_low, key_low[j], 1, 0))
        key_grad[j] = add(key_grad[j], dims(cross_low, query_low[i], 0, 0))
        energy[i, j] = (
            key_energy[:half, :half]
            + key_energy[:half, half:]
            + key_energy[half:, :half]
            + key_energy[half:, half:]
            + query_energy[:, :half]
            + query_energy[:, half:]
        )
    whole = quad(energy[0, 0], jnp.zeros((half, half), f32), energy[1, 0], energy[1, 1])
    sum_grad = as_row(jnp.sum(whole, axis=1, keepdims=True)) - jnp.sum(whole, axis=0, keepdims=True)
    row, col = iotas(count)
    rate_grad = jnp.sum(
        jnp.where((doc == doc_row) & (col >= row), sum_grad, 0.0), axis=1, keepdims=True
    )
    first_beta_grad, second_beta_grad = untiled(beta_grad)
    soft_grad = rate_grad * speed * sigmoid(soft)
    log_grad = jnp.sum(rate_grad * rate, axis=0, keepdims=True)
    bias_grad = jnp.sum(soft_grad, axis=0, keepdims=True)
    logit_grads = [
        first_beta_grad * first_beta * (1.0 - first_beta),
        second_beta_grad * second_beta * (1.0 - second_beta),
        soft_grad,
    ]
    first_key_grad, second_key_grad = untiled(key_grad)
    first_value_grad, second_value_grad = untiled(value_grad)
    active_grads = [
        unit_back(query_unit, query_scale, jnp.concatenate(query_grad, axis=0) * root),
        unit_back(key_first, first_scale, first_key_grad),
        unit_back(key_second, second_scale, second_key_grad),
        first_value_grad,
        second_value_grad,
    ]
    piece_grads, tap_grads = [], []
    for group in range(5):
        slope = slopes[group]
        conv_grad = active_grads[group] * (slope * (1.0 + convolved[group] * (1.0 - slope)))
        back, tap_grad = short_conv_back(conv_grad, pieces[group], taps[group], inside)
        piece_grads.append(back.astype(low))
        tap_grads.append(tap_grad)
    piece_grads.append(gate_grad.astype(low))
    return piece_grads, tap_grads, logit_grads, log_grad, bias_grad, gain_grad


def pack_lines(line_ref, tap_grad, gain_grads, channels, shard_rows):
    line_ref[...] = jnp.zeros_like(line_ref)
    for index in range(line_ref.shape[0]):
        line_ref[index, 0:4, :channels] = tap_grad[:, index * channels : (index + 1) * channels]
        for row, grad in enumerate(gain_grads):
            line_ref[index, 4 + row : 5 + row, :shard_rows] = grad[
                :, index * shard_rows : (index + 1) * shard_rows
            ]


def backward_kernel(sizes, streams, sizes_of, calls, heads, channels, *refs):
    refs = list(refs)
    count = len(sizes_of)
    token_ref, log_ref, bias_ref, gain_ref = [refs.pop(0) for _ in range(4)]
    in_ref, small_ref, tap_ref, row_ref, mark_ref, doc_ref = [refs.pop(0) for _ in range(6)]
    grad_ref, piece_ref, inverse_ref, update_ref, out_ref, logit_ref, normed_ref, middle_ref = [
        refs.pop(0) for _ in range(8)
    ]
    ffn_gain_ref = refs.pop(0)
    factors = [tuple(refs.pop(0) for _ in range(size)) for size in sizes_of]
    in_grad_ref, line_grad_ref, small_grad_ref, sums_ref, token_grad_ref = [
        refs.pop(0) for _ in range(5)
    ]
    sums = [refs.pop(0) for _ in range(count)]
    logit_grad_ref, normed_grad_ref, tap_grad_ref, line_ref = [refs.pop(0) for _ in range(4)]
    head = pl.program_id(0)
    if count:
        tick, finish = scatter_steps(sizes, streams, factors, sums, refs)
        for step, place_at in enumerate(calls):
            if place_at < heads:
                pl.when(head == place_at)(functools.partial(tick, step))

    @pl.when(head == 0)
    def _():
        logit_grad_ref[...] = jnp.zeros_like(logit_grad_ref)
        normed_grad_ref[...] = jnp.zeros_like(normed_grad_ref)
        sums_ref[...] = jnp.zeros_like(sums_ref)

    width = gain_ref.shape[1]
    pieces = [piece_ref[0, :, group * width : (group + 1) * width] for group in range(6)]
    spans = tap_slices(tap_ref, head, width)
    taps = [tap_ref[:, span] for span in spans]
    scalars = head_scalars(
        head, heads, logit_ref[...], log_ref[...], bias_ref[...], mark_ref[...]
    )
    piece_grads, tap_grads, logit_grads, log_grad, bias_grad, gain_grad = backward_head(
        pieces,
        taps,
        scalars,
        doc_ref[0:1],
        gain_ref[...],
        grad_ref[...],
        [(inverse_ref[0, 0], inverse_ref[0, 1]), (inverse_ref[0, 2], inverse_ref[0, 3])],
        [update_ref[0, 0], update_ref[0, 1]],
        out_ref[...],
    )
    for group in range(5):
        tap_grad_ref[:, spans[group]] = tap_grads[group]
    projected_grad = jnp.concatenate(piece_grads, axis=1)
    in_grad_ref[...] = dims(normed_ref[...], projected_grad, 0, 0).astype(low)
    normed_grad_ref[...] += dims(projected_grad, in_ref[...], 1, 1)
    lane = lane_of(logit_grad_ref.shape)
    spread = jnp.zeros(logit_grad_ref.shape, f32)
    for index, entry in enumerate(logit_grads):
        spread = spread + jnp.where(lane == index * heads + head, entry, 0.0)
    logit_grad_ref[...] += spread
    line = lane_of((1, width))
    sums_ref[0:1] += jnp.where(line == head, log_grad, 0.0)
    sums_ref[1:2] += jnp.where(line == head, bias_grad, 0.0)
    sums_ref[2:3] += gain_grad

    @pl.when(head == heads - 1)
    def _():
        logit_low = logit_grad_ref[...].astype(low)
        small_grad_ref[...] = dims(normed_ref[...], logit_low, 0, 0).astype(low)
        grad = normed_grad_ref[...] + dims(logit_low, small_ref[...], 1, 1)
        inputs = token_ref[...].astype(f32)
        scale = rms_scale(inputs)
        normed = inputs * scale
        gain_grads = [jnp.sum(grad * normed, axis=0, keepdims=True), ffn_gain_ref[...]]
        shard_rows = in_ref.shape[0] // line_ref.shape[0]
        pack_lines(line_ref, tap_grad_ref[...], gain_grads, channels, shard_rows)
        line_grad_ref[...] = line_ref[...].astype(low)
        weighted = grad * row_ref[0:1]
        back = scale * (weighted - normed * jnp.mean(weighted * normed, axis=1, keepdims=True))
        token_grad_ref[...] = (middle_ref[...] + back).astype(low)
        if count:
            for step, place_at in enumerate(calls):
                if place_at >= heads:
                    tick(step)
            finish()


def whole_spec(shape):
    return pl.BlockSpec(shape, lambda h: (0,) * len(shape))


def head_spec(*shape):
    return pl.BlockSpec((1,) + shape, lambda h: (h,) + (0,) * len(shape))


def col_spec(rows, width):
    return pl.BlockSpec((rows, width), lambda h: (0, h))


HBM = pl.BlockSpec(memory_space=pltpu.HBM)
VMEM_LIMIT = 56 << 20


def shared_specs(seq_len, model_width, heads, width):
    return [
        whole_spec((seq_len, model_width)),
        whole_spec((1, heads)),
        whole_spec((1, heads)),
        whole_spec((1, width)),
    ]


def weight_specs(seq_len, model_width, heads, width):
    return [
        col_spec(model_width, 6 * width),
        whole_spec((model_width, 128)),
        whole_spec((4, heads * 5 * width)),
        whole_spec((8, model_width)),
        whole_spec((seq_len, 8)),
        whole_spec((8, seq_len)),
    ]


def saved_specs(seq_len, model_width, width):
    return [
        head_spec(seq_len, 6 * width),
        head_spec(4, seq_len, seq_len),
        head_spec(2, seq_len, width),
        col_spec(seq_len, width),
        whole_spec((seq_len, 128)),
        whole_spec((seq_len, model_width)),
    ]


def saved_shapes(seq_len, model_width, heads, width):
    return [
        jax.ShapeDtypeStruct((heads, seq_len, 6 * width), f32),
        jax.ShapeDtypeStruct((heads, 4, seq_len, seq_len), low),
        jax.ShapeDtypeStruct((heads, 2, seq_len, width), f32),
        jax.ShapeDtypeStruct((seq_len, heads * width), f32),
        jax.ShapeDtypeStruct((seq_len, 128), f32),
        jax.ShapeDtypeStruct((seq_len, model_width), low),
    ]


def plain_forward(shared, weights, heads):
    seq_len, model_width = shared[0].shape
    width = shared[-1].shape[1]
    outs = pl.pallas_call(
        functools.partial(plain_forward_kernel, heads),
        grid=(heads,),
        in_specs=shared_specs(seq_len, model_width, heads, width)
        + weight_specs(seq_len, model_width, heads, width),
        out_specs=[col_spec(seq_len, width)] + saved_specs(seq_len, model_width, width),
        out_shape=[jax.ShapeDtypeStruct((seq_len, heads * width), low)]
        + saved_shapes(seq_len, model_width, heads, width),
        compiler_params=pltpu.CompilerParams(vmem_limit_bytes=VMEM_LIMIT),
        name="plain_forward",
    )(*shared, *weights)
    return outs[0], outs[1:]


def mixer_forward(sizes, streams, calls, shared, doc_row, shards, heads, channels, call):
    seq_len, model_width = shared[0].shape
    width = shared[-1].shape[1]
    count = len(shards)
    total = slots(sizes, streams)
    shape = tuple(sizes[dim] for dim in "zyxc")
    outs = pl.pallas_call(
        functools.partial(forward_kernel, sizes, streams, count, calls, heads, channels),
        grid=(heads,),
        in_specs=shared_specs(seq_len, model_width, heads, width)[:1]
        + [whole_spec((1, seq_len))]
        + shared_specs(seq_len, model_width, heads, width)[1:]
        + [HBM] * count,
        out_specs=[col_spec(seq_len, width)]
        + saved_specs(seq_len, model_width, width)
        + weight_specs(seq_len, model_width, heads, width)[2:]
        + [HBM] * count,
        out_shape=[jax.ShapeDtypeStruct((seq_len, heads * width), low)]
        + saved_shapes(seq_len, model_width, heads, width)
        + [
            jax.ShapeDtypeStruct((4, heads * 5 * width), f32),
            jax.ShapeDtypeStruct((8, model_width), f32),
            jax.ShapeDtypeStruct((seq_len, 8), f32),
            jax.ShapeDtypeStruct((8, seq_len), f32),
        ]
        + [jax.ShapeDtypeStruct(shape + shard.shape, shard.dtype) for shard in shards],
        scratch_shapes=[
            pltpu.VMEM(shape + (shards[0].shape[0], 6 * width), low),
            pltpu.VMEM(shape + shards[1].shape, low),
            pltpu.VMEM(shape + shards[2].shape, low),
            pltpu.SemaphoreType.DMA((3,)),
            pltpu.SemaphoreType.DMA((total,)),
            pltpu.SemaphoreType.DMA((total,)),
            pltpu.SemaphoreType.DMA((count,)),
        ],
        compiler_params=pltpu.CompilerParams(
            vmem_limit_bytes=44 << 20, collective_id=call, has_side_effects=True
        ),
        name="mixer_forward",
    )(shared[0], doc_row, *shared[1:], *shards)
    fulls = [out.reshape((-1, out.shape[-1])) for out in outs[11:]]
    return outs[0], outs[1:7], fulls[:2] + list(outs[7:11]), fulls[3:]


def mixer_backward(
    sizes, streams, calls, shared, weights, grad, saved, middle_grad, ffn_gain, factors, layout, call
):
    seq_len, model_width = shared[0].shape
    heads, channels, devices, line_width = layout
    width = shared[-1].shape[1]
    count = len(factors)
    line_shape = (devices, 16, line_width)
    scratch = [
        pltpu.VMEM((seq_len, 128), f32),
        pltpu.VMEM((seq_len, model_width), f32),
        pltpu.VMEM((4, heads * 5 * width), f32),
        pltpu.VMEM(line_shape, f32),
    ]
    extra = {}
    outs_cols = [sum(right.shape[1] for right in entry[1:]) for entry in factors]
    if count:
        extra = dict(collective_id=call, has_side_effects=True)
        rows = model_width // devices
        scratch = scratch + scatter_buffers(sizes, streams, [rows] * count, False)
        scratch.append(pltpu.VMEM(staging_shape(sizes, streams, rows), low))
    flat = [factor for entry in factors for factor in entry]
    once = pl.Buffered(1)
    outs = pl.pallas_call(
        functools.partial(
            backward_kernel, sizes, streams, [len(entry) for entry in factors], calls, heads, channels
        ),
        grid=(heads,),
        in_specs=shared_specs(seq_len, model_width, heads, width)
        + weight_specs(seq_len, model_width, heads, width)
        + [col_spec(seq_len, width)]
        + saved_specs(seq_len, model_width, width)
        + [pl.BlockSpec((seq_len, model_width), lambda h: (0, 0), pipeline_mode=once)]
        + [whole_spec((1, model_width))]
        + [pl.BlockSpec(entry.shape, lambda h: (0, 0), pipeline_mode=once) for entry in flat],
        out_specs=[
            col_spec(model_width, 6 * width),
            whole_spec(line_shape),
            whole_spec((model_width, 128)),
            whole_spec((8, width)),
            whole_spec((seq_len, model_width)),
        ]
        + [whole_spec((model_width // devices, cols)) for cols in outs_cols],
        out_shape=[
            jax.ShapeDtypeStruct((model_width, heads * 6 * width), low),
            jax.ShapeDtypeStruct(line_shape, low),
            jax.ShapeDtypeStruct((model_width, 128), low),
            jax.ShapeDtypeStruct((8, width), f32),
            jax.ShapeDtypeStruct((seq_len, model_width), low),
        ]
        + [jax.ShapeDtypeStruct((model_width // devices, cols), f32) for cols in outs_cols],
        scratch_shapes=scratch,
        compiler_params=pltpu.CompilerParams(vmem_limit_bytes=VMEM_LIMIT, **extra),
        name="mixer_backward",
    )(*shared, *weights, grad, *saved, middle_grad, ffn_gain, *flat)
    return outs[:5], outs[5:]


def rms_parts(inputs):
    scale = lax.rsqrt(jnp.mean(inputs * inputs, axis=-1, keepdims=True) + norm_eps)
    return inputs * scale, scale


def rms_back(normed, scale, gain_row, grad):
    weighted = grad * gain_row
    return (
        scale * (weighted - normed * jnp.mean(weighted * normed, axis=-1, keepdims=True)),
        jnp.sum(grad * normed, axis=0),
    )


def gathered(shard):
    return lax.all_gather(shard, AXES, axis=0, tiled=True)


def scattered(whole):
    return lax.psum_scatter(whole, AXES, scatter_dimension=0, tiled=True)


MESH = pl.DeviceIdType.MESH


def grid_of(wide, narrow):
    pair = 2 if narrow % 2 == 0 else 1
    half = 2 if wide % 2 == 0 else 1
    return {"z": wide // half, "y": half, "x": narrow // pair, "c": pair}


def place(sizes):
    wide, narrow = lax.axis_index("wide"), lax.axis_index("narrow")
    return {
        "z": wide // sizes["y"],
        "y": lax.rem(wide, sizes["y"]),
        "x": narrow // sizes["c"],
        "c": lax.rem(narrow, sizes["c"]),
    }


def device(sizes, at):
    return (at["z"] * sizes["y"] + at["y"], at["x"] * sizes["c"] + at["c"])


def moved(sizes, at, dim, step):
    other = dict(at)
    other[dim] = lax.rem(at[dim] + step, sizes[dim])
    return other


def meet(sizes, me):
    barrier = pltpu.get_barrier_semaphore()
    count = 0
    for dim in "zyxc":
        for step in range(1, sizes[dim]):
            pl.semaphore_signal(
                barrier,
                inc=1,
                device_id=device(sizes, moved(sizes, me, dim, step)),
                device_id_type=MESH,
            )
            count += 1
    pl.semaphore_wait(barrier, count)


def slots(sizes, streams):
    return sum(sizes[dim] - 1 for stream in streams for dim in stream[3])


def cut(array, cols, chunks, share, orders, first_lag, per_lag):
    units = cols // 128
    streams, start = [], 0
    edges = []
    for chunk in range(chunks):
        edges += [(chunk + share) / chunks, (chunk + 1) / chunks]
    for index, edge in enumerate(edges):
        stop = round(edge * units)
        if stop > start:
            lag = first_lag + (index // 2) // per_lag
            streams.append((array, start * 128, (stop - start) * 128, orders[index % 2], lag))
        start = stop
    return streams


def agenda(streams, order):
    last = max(stream[4] for stream in streams) + 5
    return [
        [
            (index, phase)
            for phase in order
            for index, stream in enumerate(streams)
            if step - stream[4] == phase
        ]
        for step in range(last)
    ]


def slot_table(sizes, streams):
    table, used = {}, 0
    for index, stream in enumerate(streams):
        for phase in range(4):
            table[index, phase] = used
            used += sizes[stream[3][phase]] - 1
    return table


def gather_steps(sizes, streams, shards, fulls, sems):
    send_sem, recv_sem, local_sem = sems
    table = slot_table(sizes, streams)
    plan = agenda(streams, GATHER_STEPS)

    def local(me):
        return [
            pltpu.make_async_copy(
                shard, full.at[me["z"], me["y"], me["x"], me["c"]], local_sem.at[index]
            )
            for index, (shard, full) in enumerate(zip(shards, fulls))
        ]

    def copies(me, index, phase):
        array, col, width, order, lag = streams[index]
        dim = order[phase]
        block = tuple(slice(None) if d in order[:phase] else me[d] for d in "zyxc")
        target = fulls[array].at[block + (slice(None), pl.ds(col, width))]
        source = shards[array].at[:, pl.ds(col, width)] if phase == 0 else target
        return [
            pltpu.make_async_remote_copy(
                src_ref=source,
                dst_ref=target,
                send_sem=send_sem.at[table[index, phase] + hop - 1],
                recv_sem=recv_sem.at[table[index, phase] + hop - 1],
                device_id=device(sizes, moved(sizes, me, dim, hop)),
                device_id_type=MESH,
            )
            for hop in range(1, sizes[dim])
        ]

    def tick(step):
        me = place(sizes)
        if step == 0:
            for copy in local(me):
                copy.start()
            meet(sizes, me)
        if step == 1:
            for copy in local(me):
                copy.wait()
        for index, phase in plan[step]:
            if phase > 0:
                for copy in copies(me, index, phase - 1):
                    copy.wait_recv()
            if phase < 4:
                for copy in copies(me, index, phase):
                    copy.start()

    def finish():
        me = place(sizes)
        for index in range(len(streams)):
            for phase in range(4):
                for copy in copies(me, index, phase):
                    copy.wait_send()

    return tick, finish


def gather_kernel(sizes, streams, count, *refs):
    tick, finish = gather_steps(
        sizes, streams, refs[:count], refs[count : 2 * count], refs[2 * count :]
    )
    for step in range(len(agenda(streams, GATHER_STEPS))):
        tick(step)
    finish()


def gather(sizes, streams, shards, call):
    count = len(shards)
    total = slots(sizes, streams)
    shape = tuple(sizes[dim] for dim in "zyxc")
    outs = pl.pallas_call(
        functools.partial(gather_kernel, sizes, streams, count),
        out_shape=[jax.ShapeDtypeStruct(shape + shard.shape, shard.dtype) for shard in shards],
        in_specs=[HBM] * count,
        out_specs=[HBM] * count,
        scratch_shapes=[
            pltpu.SemaphoreType.DMA((total,)),
            pltpu.SemaphoreType.DMA((total,)),
            pltpu.SemaphoreType.DMA((count,)),
        ],
        compiler_params=pltpu.CompilerParams(collective_id=call, has_side_effects=True),
        name="weights_gather",
    )(*shards)
    return [out.reshape((-1, out.shape[-1])) for out in outs]


def scatter_buffers(sizes, streams, rows, stored):
    shape = tuple(sizes[dim] for dim in "zyx")
    total = slots(sizes, streams)
    buffers = [
        pltpu.SemaphoreType.DMA((total,)),
        pltpu.SemaphoreType.DMA((total,)),
        pltpu.SemaphoreType.DMA((len(streams),)),
    ]
    for array, col, width, order, lag in streams:
        tail = (rows[array], width)
        if stored:
            buffers.append(pltpu.VMEM(shape + tail, low))
        for phase in range(4):
            kept = tuple(sizes[dim] for dim in "zyx" if dim not in order[: phase + 1])
            buffers.append(pltpu.VMEM((sizes[order[phase]] - 1,) + kept + tail, low))
    return buffers


def group_of(streams, lag):
    return [index for index, stream in enumerate(streams) if stream[4] == lag]


def staging_shape(sizes, streams, rows):
    widest = max(
        sum(streams[index][2] for index in group_of(streams, lag))
        for lag in range(1 + max(stream[4] for stream in streams))
    )
    return tuple(sizes[dim] for dim in "zyxc") + (rows, widest)


def scatter_steps(sizes, streams, terms, sums, refs, heads=None):
    send_sem, recv_sem, local_sem = refs[:3]
    computed = isinstance(terms[0], tuple)
    refs = list(refs[3:])
    held, got = [], {}
    for index in range(len(streams)):
        if not computed:
            held.append(refs.pop(0))
        for phase in range(4):
            got[index, phase] = refs.pop(0)
        if computed:
            held.append(got[index, 0].at[0])
    staging = refs.pop(0) if computed else None
    table = slot_table(sizes, streams)
    plan = agenda(streams, SCATTER_STEPS)

    def part(index, core):
        array, col, width, order, lag = streams[index]
        if computed:
            first = min(streams[other][1] for other in group_of(streams, lag))
            return staging.at[:, :, :, core, :, pl.ds(col - first, width)]
        return terms[array].at[:, :, :, core, :, pl.ds(col, width)]

    def produce(lag):
        group = group_of(streams, lag)
        array = streams[group[0]][0]
        first = min(streams[index][1] for index in group)
        left_ref, rights = terms[array][0], terms[array][1:]
        share = rights[0].shape[1]
        flat = staging.reshape(-1, *staging.shape[4:])
        rows = staging.shape[4]
        block = 256
        for index in group:
            col, width = streams[index][1], streams[index][2]
            inner = col % share
            right = rights[col // share][:, inner : inner + width]
            assert inner + width <= share
            for start in range(0, left_ref.shape[1], block):
                product = dims(left_ref[:, start : start + block], right, 0, 0).astype(low)
                flat[start // rows : (start + block) // rows, :, col - first : col - first + width] = (
                    product.reshape(block // rows, rows, width)
                )

    def load(me, index):
        return pltpu.make_async_copy(part(index, me["c"]), held[index], local_sem.at[index])

    def copies(me, index, phase):
        array, col, width, order, lag = streams[index]
        dim = order[phase]
        found = []
        for hop in range(1, sizes[dim]):
            to = moved(sizes, me, dim, hop)
            if phase == 0:
                source = part(index, to["c"])
            else:
                block = tuple(
                    me[d] if d in order[:phase] else (to[d] if d == dim else slice(None))
                    for d in "zyx"
                )
                source = held[index].at[block]
            found.append(
                pltpu.make_async_remote_copy(
                    src_ref=source,
                    dst_ref=got[index, phase].at[hop - 1],
                    send_sem=send_sem.at[table[index, phase] + hop - 1],
                    recv_sem=recv_sem.at[table[index, phase] + hop - 1],
                    device_id=device(sizes, to),
                    device_id_type=MESH,
                )
            )
        return found

    def combine(me, index, phase):
        array, col, width, order, lag = streams[index]
        kept = [d for d in "zyx" if d not in order[: phase + 1]]
        total = 1
        for d in kept:
            total *= sizes[d]

        def body(flat, carry):
            at, rest = dict(me), flat
            for d in reversed(kept):
                at[d] = lax.rem(rest, sizes[d])
                rest = rest // sizes[d]
            where = tuple(at[d] for d in "zyx")
            inner = tuple(at[d] for d in kept)
            value = held[index][where]
            if computed and phase == 0:
                held[index][where] = value + part(index, me["c"])[where]
                return carry
            others = [got[index, phase][(hop,) + inner] for hop in range(sizes[order[phase]] - 1)]
            if phase == 3 or len(others) > 1:
                value = value.astype(f32)
                for other in others:
                    value = value + other.astype(f32)
            else:
                value = value + others[0]
            if phase < 3:
                held[index][where] = value.astype(low)
            elif heads is None or array > 0:
                sums[array][:, pl.ds(col, width)] = value
            else:
                for tile in range(width // 128):
                    head, group = divmod(col // 128 + tile, 6)
                    target = (group * heads + head) * 128
                    sums[array][:, target : target + 128] = value[:, tile * 128 : tile * 128 + 128]
            return carry

        if total == 1:
            body(0, 0)
        else:
            lax.fori_loop(0, total, body, 0)

    def tick(step):
        me = place(sizes)
        if step == 0:
            meet(sizes, me)
        fresh = group_of(streams, step)
        if computed:
            for index in group_of(streams, step - 1):
                for copy in copies(me, index, 0):
                    copy.wait_recv()
                combine(me, index, 0)
                for copy in copies(me, index, 0):
                    copy.wait_send()
            if fresh:
                produce(step)
        elif step == 0:
            for index in range(len(streams)):
                load(me, index).start()
        for index, phase in plan[step]:
            if phase > (1 if computed else 0):
                for copy in copies(me, index, phase - 1):
                    copy.wait_recv()
                if phase == 1:
                    load(me, index).wait()
                combine(me, index, phase - 1)
            if phase < 4:
                for copy in copies(me, index, phase):
                    copy.start()

    def finish():
        me = place(sizes)
        for index in range(len(streams)):
            for phase in range(1 if computed else 0, 4):
                for copy in copies(me, index, phase):
                    copy.wait_send()

    return tick, finish


def small_buffers(sizes, shape):
    return [pltpu.VMEM((2,) + shape, f32) for _ in "cxy"] + [
        pltpu.VMEM((sizes["z"],) + shape, f32),
        pltpu.SemaphoreType.DMA((4, sizes["z"])),
        pltpu.SemaphoreType.DMA((4, sizes["z"])),
    ]


def small_steps(sizes, small, total, refs):
    boxes, lanes, small_send, small_recv = refs[:3], refs[3], refs[4], refs[5]

    def copies(me, phase):
        dim = "cxyz"[phase]
        source = small if phase == 0 else boxes[phase - 1].at[1]
        source = lanes.at[me["z"]] if dim == "z" else source
        return [
            pltpu.make_async_remote_copy(
                src_ref=source,
                dst_ref=lanes.at[me["z"]] if dim == "z" else boxes[phase].at[0],
                send_sem=small_send.at[phase, hop],
                recv_sem=small_recv.at[phase, hop],
                device_id=device(sizes, moved(sizes, me, dim, hop)),
                device_id_type=MESH,
            )
            for hop in range(1, sizes[dim])
        ]

    def tick(step):
        me = place(sizes)
        if step > 0:
            for copy in copies(me, step - 1):
                copy.wait_recv()
            if step < 4:
                mine = small[...] if step == 1 else boxes[step - 2][1]
                boxes[step - 1][1] = mine + boxes[step - 1][0]
            else:
                value = lanes[0]
                for index in range(1, sizes["z"]):
                    value = value + lanes[index]
                total[...] = value
        if step < 4:
            if step == 3:
                lanes[me["z"]] = boxes[2][1]
            for copy in copies(me, step):
                copy.start()

    def finish():
        me = place(sizes)
        for phase in range(4):
            for copy in copies(me, phase):
                copy.wait_send()

    return tick, finish


def scatter_kernel(sizes, streams, count, heads, *refs):
    terms, small = refs[:count], refs[count]
    sums, total = refs[count + 1 : 2 * count + 1], refs[2 * count + 1]
    rest = refs[2 * count + 2 :]
    tick, finish = scatter_steps(sizes, streams, terms, sums, rest[:-6], heads)
    small_tick, small_finish = small_steps(sizes, small, total, rest[-6:])
    for step in range(len(agenda(streams, SCATTER_STEPS))):
        tick(step)
        if step < 5:
            small_tick(step)
    finish()
    small_finish()


def scatter(sizes, streams, terms, small, heads, call):
    count = len(terms)
    shape = tuple(sizes[dim] for dim in "zyxc")
    devices = shape[0] * shape[1] * shape[2] * shape[3]
    blocks = [
        term.reshape(shape + (term.shape[0] // devices, term.shape[1])) for term in terms
    ]
    buffers = scatter_buffers(sizes, streams, [block.shape[4] for block in blocks], True)
    vmem = pl.BlockSpec(memory_space=pltpu.VMEM)
    return pl.pallas_call(
        functools.partial(scatter_kernel, sizes, streams, count, heads),
        out_shape=[
            jax.ShapeDtypeStruct((block.shape[4], block.shape[5]), f32) for block in blocks
        ]
        + [jax.ShapeDtypeStruct(small.shape, f32)],
        in_specs=[HBM] * count + [vmem],
        out_specs=[vmem] * (count + 1),
        scratch_shapes=buffers + small_buffers(sizes, small.shape),
        compiler_params=pltpu.CompilerParams(
            collective_id=call, has_side_effects=True, vmem_limit_bytes=44 << 20
        ),
        name="grads_scatter",
    )(*blocks, small)


GATHER_STEPS = (0, 1, 2, 3, 4)
SCATTER_STEPS = (0, 1, 3, 2, 4)
GATHER_ORDERS = ("zxyc", "yzxc")
SCATTER_ORDERS = ("cyxz", "cxzy")


BACKWARD_PLAN = ((2, 0, 1), (4, 2, 1), (1, 6, 1))
BACKWARD_CALLS = (0, 1, 2, 3, 4, 5, 6, 7, 8, 8, 8)
FORWARD_PLAN = ((4, 0, 1), (1, 0, 1), (1, 0, 1), (1, 4, 1), (4, 4, 1), (2, 8, 1))
FORWARD_CALLS = (0, 0, 0, 0, 0, 2, 4, 6, 8, 10, 12, 14, 16, 16)


def planned(terms, orders, chunks):
    streams = []
    for index, (count, lag, per_lag) in enumerate(chunks):
        streams += cut(index, terms[index].shape[1], count, 0.64, orders, lag, per_lag)
    return streams


def per_device(
    sizes,
    tokens,
    doc_ids,
    attn_gain,
    mixer_in,
    mixer_small,
    conv_weight,
    decay_log,
    decay_bias,
    out_gain,
    mixer_out,
    ffn_gain,
    ffn_in,
    ffn_out,
    out_grad,
):
    row_count, seq_len, model_width = tokens.shape
    heads, width = decay_log.shape[0], out_gain.shape[0]
    shard_rows = mixer_in.shape[0]
    small_cols = mixer_small.shape[1]
    channels = conv_weight.shape[0]
    devices = model_width // shard_rows
    ff_width = ffn_out.shape[0]
    own = (
        shard_rows % 16 == 0
        and row_count == 1
        and sizes["x"] == 2
        and sizes["y"] == 2
        and sizes["c"] == 2
    )
    in_shard = (
        mixer_in.astype(low)
        .reshape(shard_rows, 6, heads, width)
        .transpose(0, 2, 1, 3)
        .reshape(shard_rows, -1)
    )
    small_shard = jnp.pad(mixer_small.astype(low), ((0, 0), (0, 128 - small_cols)))
    line_width = channels + (-channels % 128)
    lines_shard = jnp.concatenate(
        [
            jnp.pad(conv_weight.astype(low).T, ((0, 0), (0, line_width - channels))),
            jnp.pad(
                jnp.stack([attn_gain, ffn_gain]).astype(low), ((0, 10), (0, line_width - shard_rows))
            ),
        ]
    )
    out_shard, ffn_out_shard = mixer_out.astype(low).T, ffn_out.astype(low).T
    late_shards = [out_shard, ffn_in.astype(low), ffn_out_shard]
    early_shards = [in_shard, small_shard, lines_shard]
    each = [
        [tokens[index], decay_log[None], decay_bias[None], out_gain[None]]
        for index in range(row_count)
    ]
    if own:
        shards = early_shards + late_shards
        mixed, saved, weights, late_full = mixer_forward(
            sizes,
            planned(shards, GATHER_ORDERS, FORWARD_PLAN),
            FORWARD_CALLS,
            each[0],
            doc_ids,
            shards,
            heads,
            channels,
            1,
        )
        saves, weights = [saved], [weights]
        ffn_row = weights[0][3][1:2]
    else:
        in_full, small_full, lines = [gathered(shard) for shard in early_shards]
        lines = lines.reshape(devices, 16, line_width).astype(f32)
        taps = lines[:, :4, :channels].transpose(1, 0, 2).reshape(4, -1)
        rows = lines[:, 4:6, :shard_rows].transpose(1, 0, 2).reshape(2, model_width)
        ffn_row = rows[1:2]
        weights = []
        for index in range(row_count):
            doc = doc_ids[index].astype(f32)
            before = [
                jnp.concatenate([jnp.full((distance,), -1.0), doc[:-distance]])
                for distance in (1, 2, 3)
            ]
            marks = [doc] + [jnp.where(entry == doc, 1.0, 0.0) for entry in before]
            weights.append(
                [
                    in_full,
                    small_full,
                    taps,
                    jnp.pad(rows, ((0, 6), (0, 0))),
                    jnp.pad(jnp.stack(marks, axis=1), ((0, 0), (0, 4))),
                    jnp.broadcast_to(doc[None], (8, seq_len)),
                ]
            )
        done = [plain_forward(*entry, heads) for entry in zip(each, weights)]
        mixed = jnp.concatenate([entry[0] for entry in done])
        saves = [entry[1] for entry in done]
        late_full = [gathered(shard) for shard in late_shards]
    out_t, ffn_in_full, ffn_out_t = late_full

    inputs = tokens.reshape(row_count * seq_len, model_width).astype(f32)
    middle = inputs + dims(mixed, out_t, 1, 1)
    ffn_normed, ffn_scale = rms_parts(middle)
    ffn_rows = (ffn_normed * ffn_row).astype(low)
    gate_up = jnp.dot(ffn_rows, ffn_in_full, preferred_element_type=f32)
    gate, up = gate_up[:, :ff_width], gate_up[:, ff_width:]
    slope = jax.nn.sigmoid(gate)
    hidden = (gate * slope * up).astype(low)
    result = middle + dims(hidden, ffn_out_t, 1, 1)
    grad_low = out_grad.reshape(row_count * seq_len, model_width)
    hidden_grad = jnp.dot(grad_low, ffn_out_t, preferred_element_type=f32)
    gate_grad = (hidden_grad * up * slope * (1.0 + gate * (1.0 - slope))).astype(low)
    up_grad = (hidden_grad * gate * slope).astype(low)
    gate_up_grad = jnp.concatenate([gate_grad, up_grad], axis=1)
    rows_grad = dims(gate_up_grad, ffn_in_full, 1, 1)
    middle_norm_grad, ffn_gain_term = rms_back(ffn_normed, ffn_scale, ffn_row, rows_grad)
    middle_grad = grad_low.astype(f32) + middle_norm_grad
    branch_grad = middle_grad.astype(low)
    mixed_grad = jnp.dot(branch_grad, out_t, preferred_element_type=f32)
    factors = [(grad_low, hidden), (ffn_rows, gate_grad, up_grad), (branch_grad, mixed)]
    layout = (heads, channels, devices, line_width)
    ffn_gain_line = ffn_gain_term[None]
    if own:
        late = planned([ffn_out_t, ffn_in_full, out_t], SCATTER_ORDERS, BACKWARD_PLAN)
        grads, late_sums = mixer_backward(
            sizes,
            late,
            BACKWARD_CALLS,
            each[0],
            weights[0],
            mixed_grad,
            saves[0],
            middle_grad,
            ffn_gain_line,
            factors,
            layout,
            3,
        )
        grads = [grads]
    else:
        grads = []
        for index, entry in enumerate(each):
            rows = slice(index * seq_len, (index + 1) * seq_len)
            share = ffn_gain_line if index == 0 else jnp.zeros_like(ffn_gain_line)
            grads.append(
                mixer_backward(
                    sizes,
                    [],
                    (),
                    entry,
                    weights[index],
                    mixed_grad[rows],
                    saves[index],
                    middle_grad[rows],
                    share,
                    [],
                    layout,
                    3,
                )[0]
            )
        late_sums = [
            scattered(dims(left, jnp.concatenate(right, axis=1), 0, 0).astype(low)).astype(f32)
            for left, *right in factors
        ]
    in_term, lines_term, small_term, small = [
        functools.reduce(jnp.add, [entry[index] for entry in grads]) for index in range(4)
    ]
    input_grad = jnp.stack([entry[4] for entry in grads])
    lines_term = lines_term.reshape(devices * 16, line_width)
    early_terms = [in_term, small_term, lines_term]
    if own:
        early = planned(early_terms, SCATTER_ORDERS, ((8, 0, 2), (1, 0, 1), (1, 0, 1)))
        in_sum, small_sum, lines_sum, small = scatter(
            sizes, early, early_terms, small, heads, 4
        )
    else:
        in_sum, small_sum, lines_sum = [scattered(term).astype(f32) for term in early_terms]
        small = lax.psum(small, AXES)
        in_sum = (
            in_sum.reshape(shard_rows, heads, 6, width)
            .transpose(0, 2, 1, 3)
            .reshape(shard_rows, -1)
        )
    ffn_out_sum, ffn_in_sum, out_sum = late_sums
    outputs = result.astype(low).reshape(row_count, seq_len, model_width)
    return (
        outputs,
        input_grad,
        lines_sum[4, :shard_rows],
        in_sum,
        small_sum[:, :small_cols],
        lines_sum[:4, :channels].T,
        small[0, :heads],
        small[1, :heads],
        small[2],
        out_sum.T,
        lines_sum[5, :shard_rows],
        ffn_in_sum,
        ffn_out_sum.T,
    )


def solution(mesh):
    both = P(AXES)
    line = P(None, AXES)
    in_specs = (both, both, both, both, both, both, P(), P(), P(), line, both, both, line, both)
    out_specs = (both, both, both, both, both, both, P(), P(), P(), line, both, both, line)
    sizes = grid_of(mesh.shape["wide"], mesh.shape["narrow"])
    return jax.shard_map(
        functools.partial(per_device, sizes),
        mesh=mesh, in_specs=in_specs, out_specs=out_specs, check_vma=False
    )
```

```python
import functools
import jax
import jax.numpy as jnp
from jax import lax
from jax.experimental import pallas as pl
from jax.experimental.pallas import tpu as pltpu
from jax.sharding import PartitionSpec as P

norm_eps = 1e-06
low = jnp.bfloat16
f32 = jnp.float32
AXES = ("wide", "narrow")


def dims(left, right, left_dim, right_dim):
    return lax.dot_general(
        left, right, (((left_dim,), (right_dim,)), ((), ())), preferred_element_type=f32
    )


def one(left, right, left_dim=1, right_dim=0):
    return dims(left.astype(low), right.astype(low), left_dim, right_dim)


def parts(value):
    high = value.astype(low)
    return high, (value - high.astype(f32)).astype(low)


def three(left, right, left_dim=1, right_dim=0):
    left_high, left_rest = left if isinstance(left, tuple) else parts(left)
    right_high, right_rest = right if isinstance(right, tuple) else parts(right)
    return (
        dims(left_high, right_high, left_dim, right_dim)
        + dims(left_high, right_rest, left_dim, right_dim)
        + dims(left_rest, right_high, left_dim, right_dim)
    )


def sigmoid(value):
    return 1.0 / (1.0 + jnp.exp(-value))


def later(value, distance):
    return pltpu.roll(value, distance % value.shape[0], 0)


def short_conv(rows, taps, inside):
    summed = rows * taps[3:4]
    for distance in (1, 2, 3):
        summed = summed + later(rows, distance) * inside[distance - 1] * taps[3 - distance : 4 - distance]
    return summed


def short_conv_back(grad, rows, taps, inside):
    back = grad * taps[3:4]
    tap_grads = [jnp.sum(grad * rows, axis=0, keepdims=True)]
    for distance in (1, 2, 3):
        masked = grad * inside[distance - 1]
        back = back + later(masked, -distance) * taps[3 - distance : 4 - distance]
        tap_grads.append(jnp.sum(masked * later(rows, distance), axis=0, keepdims=True))
    return back, jnp.concatenate(tap_grads[::-1], axis=0)


def unit(rows):
    scale = lax.rsqrt(jnp.sum(rows * rows, axis=1, keepdims=True) + norm_eps)
    return rows * scale, scale


def unit_back(normed, scale, grad):
    return scale * (grad - normed * jnp.sum(grad * normed, axis=1, keepdims=True))


def iotas(count):
    return (
        lax.broadcasted_iota(jnp.int32, (count, count), 0),
        lax.broadcasted_iota(jnp.int32, (count, count), 1),
    )


def decay_matrix(rate_col, rate_row, doc_col, doc_row):
    row, col = iotas(rate_col.shape[0])
    same = doc_col == doc_row
    causal = same & (row >= col)
    sum_col = jnp.sum(jnp.where(causal, rate_row, 0.0), axis=1, keepdims=True)
    sum_row = jnp.sum(jnp.where(same & (row <= col), rate_col, 0.0), axis=0, keepdims=True)
    spread = jnp.where(row > col, jnp.minimum(sum_col - sum_row, 0.0), 0.0)
    return jnp.where(causal, jnp.exp(spread), 0.0), causal


def quad(a, b, c, d):
    return jnp.concatenate(
        [jnp.concatenate([a, b], axis=1), jnp.concatenate([c, d], axis=1)], axis=0
    )


PAIRS = ((0, 0), (1, 0), (1, 1))


def decay_tiles(decay):
    half = decay.shape[0] // 2
    row, col = iotas(half)
    keys, queries = {}, {}
    for i, j in PAIRS:
        tile = decay[i * half : (i + 1) * half, j * half : (j + 1) * half]
        strict = jnp.where(row > col, tile, 0.0) if i == j else tile
        keys[i, j] = quad(strict, strict, tile, strict if i == j else tile)
        queries[i, j] = jnp.concatenate([tile, tile], axis=1)
    return keys, queries


def tiles(first, second):
    half = first.shape[0] // 2
    return [
        jnp.concatenate([first[:half], second[:half]], axis=0),
        jnp.concatenate([first[half:], second[half:]], axis=0),
    ]


def untiled(pair):
    half = pair[0].shape[0] // 2
    return (
        jnp.concatenate([pair[0][:half], pair[1][:half]], axis=0),
        jnp.concatenate([pair[0][half:], pair[1][half:]], axis=0),
    )


def inverses(systems):
    count = systems[0].shape[0]
    half = count // 2
    row, col = iotas(count)
    row_token, col_token = row & (half - 1), col & (half - 1)
    apart = jnp.where(row_token > col_token, row_token ^ col_token, 0)
    eye = jnp.where(row == col, 1.0, 0.0)
    solved = [eye - jnp.where(row_token == col_token, system, 0.0) for system in systems]
    lows = [system.astype(low) for system in systems]
    size = 1
    while size < half:
        inside = jnp.where((apart >= size) & (apart < 2 * size), 1.0, 0.0).astype(low)
        rounded = [value.astype(low) for value in solved]
        products = [dims(entry * inside, value, 1, 0) for entry, value in zip(lows, rounded)]
        solved = [
            value - dims(kept, product.astype(low), 1, 0)
            for value, kept, product in zip(solved, rounded, products)
        ]
        size *= 2
    refined = []
    for system, value, kept in zip(systems, solved, (parts(value) for value in solved)):
        left = eye - value - three(system, kept)
        refined.append(value + dims(kept[0], left.astype(low), 1, 0))
    return refined


def mixer_values(pieces, taps, beta, rate_col, doc_col, inside, rate_row, doc_row):
    convolved = [short_conv(piece, tap, inside) for piece, tap in zip(pieces, taps)]
    slopes = [sigmoid(value) for value in convolved]
    active = [value * slope for value, slope in zip(convolved, slopes)]
    decay, causal = decay_matrix(rate_col, rate_row, doc_col, doc_row)
    return convolved, slopes, active, decay


def lane_of(shape):
    return lax.broadcasted_iota(jnp.int32, shape, 1)


def pick(values, lane):
    return jnp.sum(jnp.where(lane_of(values.shape) == lane, values, 0.0), axis=1, keepdims=True)


def as_row(col):
    row, column = iotas(col.shape[0])
    return jnp.sum(jnp.where(row == column, col, 0.0), axis=0, keepdims=True)


def head_scalars(head, heads, logits, log_row, bias_row, marks):
    first = sigmoid(pick(logits, head))
    second = sigmoid(pick(logits, heads + head))
    speed = -jnp.exp(pick(log_row, head))
    soft = pick(logits, 2 * heads + head) + pick(bias_row, head)
    rate = speed * (jnp.maximum(soft, 0.0) + jnp.log1p(jnp.exp(-jnp.abs(soft))))
    doc = marks[:, 0:1]
    inside = [marks[:, 1:2], marks[:, 2:3], marks[:, 3:4]]
    return first, second, speed, soft, rate, doc, inside


def rms_scale(inputs):
    return lax.rsqrt(jnp.mean(inputs * inputs, axis=1, keepdims=True) + norm_eps)


def forward_head(pieces, taps, scalars, doc_row, gain, between):
    first_beta, second_beta, _, _, rate, doc, inside = scalars
    beta = tiles(first_beta, second_beta)
    _, _, active, decay = mixer_values(
        pieces[:5], taps, beta, rate, doc, inside, as_row(rate), doc_row
    )
    half = decay.shape[0] // 2
    width = active[0].shape[1]
    query = unit(active[0])[0] * width ** (-0.5)
    key = tiles(unit(active[1])[0], unit(active[2])[0])
    value = tiles(active[3], active[4])
    key_decay, query_decay = decay_tiles(decay)
    system = {
        (i, j): beta[i] * key_decay[i, j] * three(key[i], key[j], 1, 1) for i, j in PAIRS
    }
    inverse = [parts(entry) for entry in inverses([system[0, 0], system[1, 1]])]
    between()
    first = three(inverse[0], beta[0] * value[0])
    second = three(inverse[1], beta[1] * value[1] - three(system[1, 0], first))
    queries = [query[:half], query[half:]]
    reads = {(i, j): query_decay[i, j] * three(queries[i], key[j], 1, 1) for i, j in PAIRS}
    out = jnp.concatenate(
        [three(reads[0, 0], first), three(reads[1, 0], first) + three(reads[1, 1], second)], axis=0
    )
    gate = pieces[5]
    mixed = out * rms_scale(out) * gain * (gate * sigmoid(gate))
    return mixed.astype(low), inverse, [first, second], out


def tap_slices(tap_ref, head, width):
    inner = tap_ref.shape[1] // 5
    return [
        pl.ds(pl.multiple_of(group * inner + head * width, 128), width) for group in range(5)
    ]


def mark_documents(id_ref, mark_ref, doc_ref):
    doc_row = id_ref[...].astype(f32)
    row, col = iotas(doc_row.shape[1])
    lane = lane_of(mark_ref.shape)
    doc = jnp.sum(jnp.where(row == col, doc_row, 0.0), axis=1, keepdims=True)
    marks = jnp.where(lane == 0, doc, 0.0)
    place_in_row = lax.broadcasted_iota(jnp.int32, doc.shape, 0)
    for distance in (1, 2, 3):
        before = jnp.sum(jnp.where(col == row - distance, doc_row, 0.0), axis=1, keepdims=True)
        inside = (before == doc) & (place_in_row >= distance)
        marks = jnp.where((lane == distance) & inside, 1.0, marks)
    mark_ref[...] = marks
    doc_ref[...] = jnp.broadcast_to(doc_row, doc_ref.shape)


def unpack_lines(line_ref, tap_ref, row_ref, channels, shard_rows):
    for index in range(line_ref.shape[0]):
        lines = line_ref[index].astype(f32)
        tap_ref[:, index * channels : (index + 1) * channels] = lines[0:4, :channels]
        row_ref[0:2, index * shard_rows : (index + 1) * shard_rows] = lines[4:6, :shard_rows]


def forward_kernel(sizes, streams, count, calls, heads, channels, *refs):
    refs = list(refs)
    token_ref, id_ref, log_ref, bias_ref, gain_ref = [refs.pop(0) for _ in range(5)]
    shards = [refs.pop(0) for _ in range(count)]
    mixed_ref, piece_ref, inverse_ref, update_ref, out_ref, logit_ref, normed_ref = [
        refs.pop(0) for _ in range(7)
    ]
    tap_ref, row_ref, mark_ref, doc_ref = [refs.pop(0) for _ in range(4)]
    fulls = [refs.pop(0) for _ in range(count)]
    in_ref, small_ref, line_ref, load_sem = [refs.pop(0) for _ in range(4)]
    head = pl.program_id(0)
    width = gain_ref.shape[1]
    tick, finish = gather_steps(sizes, streams, shards, fulls, refs)

    def ticks(slot):
        for step, place_at in enumerate(calls):
            if place_at % 2 == slot and place_at < 2 * heads:
                pl.when(head == place_at // 2)(functools.partial(tick, step))

    ticks(0)

    @pl.when(head == 0)
    def _():
        copies = [
            pltpu.make_async_copy(fulls[1], small_ref, load_sem.at[1]),
            pltpu.make_async_copy(fulls[2], line_ref, load_sem.at[2]),
        ]
        for copy in copies:
            copy.start()
        row_ref[...] = jnp.zeros_like(row_ref)
        mark_documents(id_ref, mark_ref, doc_ref)
        for copy in copies:
            copy.wait()
        shard_rows = shards[0].shape[0]
        devices = row_ref.shape[1] // shard_rows
        unpack_lines(
            line_ref.reshape(devices, *line_ref.shape[4:]), tap_ref, row_ref, channels, shard_rows
        )
        inputs = token_ref[...].astype(f32)
        normed = (inputs * rms_scale(inputs) * row_ref[0:1]).astype(low)
        normed_ref[...] = normed
        logit_ref[...] = dims(normed, small_ref[...].reshape(-1, small_ref.shape[-1]), 1, 0)

    cols = pl.ds(pl.multiple_of(head * 6 * width, 128), 6 * width)
    copy = pltpu.make_async_copy(fulls[0].at[:, :, :, :, :, cols], in_ref, load_sem.at[0])
    copy.start()
    copy.wait()
    projected = dims(normed_ref[...], in_ref[...].reshape(-1, 6 * width), 1, 0)
    piece_ref[0] = projected
    pieces = [projected[:, group * width : (group + 1) * width] for group in range(6)]
    taps = [tap_ref[:, span] for span in tap_slices(tap_ref, head, width)]
    scalars = head_scalars(
        head, heads, logit_ref[...], log_ref[...], bias_ref[...], mark_ref[...]
    )
    mixed, inverse, update, out = forward_head(
        pieces, taps, scalars, doc_ref[0:1], gain_ref[...], lambda: ticks(1)
    )
    mixed_ref[...] = mixed
    for tile in (0, 1):
        inverse_ref[0, 2 * tile] = inverse[tile][0]
        inverse_ref[0, 2 * tile + 1] = inverse[tile][1]
        update_ref[0, tile] = update[tile]
    out_ref[...] = out

    @pl.when(head == heads - 1)
    def _():
        for step, place_at in enumerate(calls):
            if place_at >= 2 * heads:
                tick(step)
        finish()


def plain_forward_kernel(heads, *refs):
    token_ref, log_ref, bias_ref, gain_ref = refs[:4]
    in_ref, small_ref, tap_ref, row_ref, mark_ref, doc_ref = refs[4:10]
    mixed_ref, piece_ref, inverse_ref, update_ref, out_ref, logit_ref, normed_ref = refs[10:]
    head = pl.program_id(0)
    width = gain_ref.shape[1]

    @pl.when(head == 0)
    def _():
        inputs = token_ref[...].astype(f32)
        normed = (inputs * rms_scale(inputs) * row_ref[0:1]).astype(low)
        normed_ref[...] = normed
        logit_ref[...] = dims(normed, small_ref[...], 1, 0)

    projected = dims(normed_ref[...], in_ref[...], 1, 0)
    piece_ref[0] = projected
    pieces = [projected[:, group * width : (group + 1) * width] for group in range(6)]
    taps = [tap_ref[:, span] for span in tap_slices(tap_ref, head, width)]
    scalars = head_scalars(
        head, heads, logit_ref[...], log_ref[...], bias_ref[...], mark_ref[...]
    )
    mixed, inverse, update, out = forward_head(
        pieces, taps, scalars, doc_ref[0:1], gain_ref[...], lambda: None
    )
    mixed_ref[...] = mixed
    for tile in (0, 1):
        inverse_ref[0, 2 * tile] = inverse[tile][0]
        inverse_ref[0, 2 * tile + 1] = inverse[tile][1]
        update_ref[0, tile] = update[tile]
    out_ref[...] = out


def backward_head(pieces, taps, scalars, doc_row, gain, grad, inverse, update, out):
    first_beta, second_beta, speed, soft, rate, doc, inside = scalars
    beta = tiles(first_beta, second_beta)
    convolved, slopes, active, decay = mixer_values(
        pieces[:5], taps, beta, rate, doc, inside, as_row(rate), doc_row
    )
    count = decay.shape[0]
    half = count // 2
    width = active[0].shape[1]
    root = width ** (-0.5)
    gate = pieces[5]
    scale = rms_scale(out)
    normed = out * scale
    gate_slope = sigmoid(gate)
    opened = gate * gate_slope
    normed_grad = grad * opened * gain
    gain_grad = jnp.sum(grad * opened * normed, axis=0, keepdims=True)
    gate_grad = grad * normed * gain * (gate_slope * (1.0 + gate * (1.0 - gate_slope)))
    out_grad = scale * (normed_grad - normed * jnp.mean(normed_grad * normed, axis=1, keepdims=True))

    query_unit, query_scale = unit(active[0])
    key_first, first_scale = unit(active[1])
    key_second, second_scale = unit(active[2])
    query = query_unit * root
    key = tiles(key_first, key_second)
    value = tiles(active[3], active[4])
    key_decay, query_decay = decay_tiles(decay)
    key_parts = [parts(entry) for entry in key]
    query_parts = [parts(query[:half]), parts(query[half:])]
    key_low = [entry[0] for entry in key_parts]
    query_low = [entry[0] for entry in query_parts]
    update = [parts(entry) for entry in update]
    gram = {(i, j): three(key_parts[i], key_parts[j], 1, 1) for i, j in PAIRS}
    cross = {(i, j): three(query_parts[i], key_parts[j], 1, 1) for i, j in PAIRS}
    reads = {(i, j): parts(query_decay[i, j] * cross[i, j]) for i, j in PAIRS}
    outs = [parts(out_grad[:half]), parts(out_grad[half:])]
    read_grad = {(i, j): three(outs[i], update[j], 1, 1) for i, j in PAIRS}
    first_grad = three(reads[0, 0], outs[0], 0, 0) + three(reads[1, 0], outs[1], 0, 0)
    second_grad = three(reads[1, 1], outs[1], 0, 0)
    target_second = three(inverse[1], second_grad, 0, 0)
    link = beta[1] * key_decay[1, 0] * gram[1, 0]
    target_first = three(inverse[0], first_grad - three(link, target_second, 0, 0), 0, 0)
    target = [target_first, target_second]
    target_parts = [parts(entry) for entry in target]
    beta_grad = [jnp.sum(target[i] * value[i], axis=1, keepdims=True) for i in (0, 1)]
    value_grad = [beta[i] * target[i] for i in (0, 1)]
    key_grad = [None, None]
    query_grad = [None, None]
    energy = {}

    def add(total, term):
        return term if total is None else total + term

    for i, j in PAIRS:
        weighted = -three(target_parts[i], update[j], 1, 1) * key_decay[i, j]
        product = weighted * gram[i, j]
        beta_grad[i] = beta_grad[i] + jnp.sum(product, axis=1, keepdims=True)
        gram_grad = (beta[i] * weighted).astype(low)
        key_energy = beta[i] * product
        key_grad[i] = add(key_grad[i], dims(gram_grad, key_low[j], 1, 0))
        key_grad[j] = add(key_grad[j], dims(gram_grad, key_low[i], 0, 0))
        cross_grad = read_grad[i, j] * query_decay[i, j]
        query_energy = cross_grad * cross[i, j]
        cross_low = cross_grad.astype(low)
        query_grad[i] = add(query_grad[i], dims(cross_low, key_low[j], 1, 0))
        key_grad[j] = add(key_grad[j], dims(cross_low, query_low[i], 0, 0))
        energy[i, j] = (
            key_energy[:half, :half]
            + key_energy[:half, half:]
            + key_energy[half:, :half]
            + key_energy[half:, half:]
            + query_energy[:, :half]
            + query_energy[:, half:]
        )
    whole = quad(energy[0, 0], jnp.zeros((half, half), f32), energy[1, 0], energy[1, 1])
    sum_grad = as_row(jnp.sum(whole, axis=1, keepdims=True)) - jnp.sum(whole, axis=0, keepdims=True)
    row, col = iotas(count)
    rate_grad = jnp.sum(
        jnp.where((doc == doc_row) & (col >= row), sum_grad, 0.0), axis=1, keepdims=True
    )
    first_beta_grad, second_beta_grad = untiled(beta_grad)
    soft_grad = rate_grad * speed * sigmoid(soft)
    log_grad = jnp.sum(rate_grad * rate, axis=0, keepdims=True)
    bias_grad = jnp.sum(soft_grad, axis=0, keepdims=True)
    logit_grads = [
        first_beta_grad * first_beta * (1.0 - first_beta),
        second_beta_grad * second_beta * (1.0 - second_beta),
        soft_grad,
    ]
    first_key_grad, second_key_grad = untiled(key_grad)
    first_value_grad, second_value_grad = untiled(value_grad)
    active_grads = [
        unit_back(query_unit, query_scale, jnp.concatenate(query_grad, axis=0) * root),
        unit_back(key_first, first_scale, first_key_grad),
        unit_back(key_second, second_scale, second_key_grad),
        first_value_grad,
        second_value_grad,
    ]
    piece_grads, tap_grads = [], []
    for group in range(5):
        slope = slopes[group]
        conv_grad = active_grads[group] * (slope * (1.0 + convolved[group] * (1.0 - slope)))
        back, tap_grad = short_conv_back(conv_grad, pieces[group], taps[group], inside)
        piece_grads.append(back.astype(low))
        tap_grads.append(tap_grad)
    piece_grads.append(gate_grad.astype(low))
    return piece_grads, tap_grads, logit_grads, log_grad, bias_grad, gain_grad


def pack_lines(line_ref, tap_grad, gain_grads, channels, shard_rows):
    line_ref[...] = jnp.zeros_like(line_ref)
    for index in range(line_ref.shape[0]):
        line_ref[index, 0:4, :channels] = tap_grad[:, index * channels : (index + 1) * channels]
        for row, grad in enumerate(gain_grads):
            line_ref[index, 4 + row : 5 + row, :shard_rows] = grad[
                :, index * shard_rows : (index + 1) * shard_rows
            ]


def backward_kernel(sizes, streams, sizes_of, calls, heads, channels, *refs):
    refs = list(refs)
    count = len(sizes_of)
    token_ref, log_ref, bias_ref, gain_ref = [refs.pop(0) for _ in range(4)]
    in_ref, small_ref, tap_ref, row_ref, mark_ref, doc_ref = [refs.pop(0) for _ in range(6)]
    grad_ref, piece_ref, inverse_ref, update_ref, out_ref, logit_ref, normed_ref, middle_ref = [
        refs.pop(0) for _ in range(8)
    ]
    ffn_gain_ref = refs.pop(0)
    factors = [tuple(refs.pop(0) for _ in range(size)) for size in sizes_of]
    in_grad_ref, line_grad_ref, small_grad_ref, sums_ref, token_grad_ref = [
        refs.pop(0) for _ in range(5)
    ]
    sums = [refs.pop(0) for _ in range(count)]
    logit_grad_ref, normed_grad_ref, tap_grad_ref, line_ref = [refs.pop(0) for _ in range(4)]
    head = pl.program_id(0)
    if count:
        tick, finish = scatter_steps(sizes, streams, factors, sums, refs)
        for step, place_at in enumerate(calls):
            if place_at < heads:
                pl.when(head == place_at)(functools.partial(tick, step))

    @pl.when(head == 0)
    def _():
        logit_grad_ref[...] = jnp.zeros_like(logit_grad_ref)
        normed_grad_ref[...] = jnp.zeros_like(normed_grad_ref)
        sums_ref[...] = jnp.zeros_like(sums_ref)

    width = gain_ref.shape[1]
    pieces = [piece_ref[0, :, group * width : (group + 1) * width] for group in range(6)]
    spans = tap_slices(tap_ref, head, width)
    taps = [tap_ref[:, span] for span in spans]
    scalars = head_scalars(
        head, heads, logit_ref[...], log_ref[...], bias_ref[...], mark_ref[...]
    )
    piece_grads, tap_grads, logit_grads, log_grad, bias_grad, gain_grad = backward_head(
        pieces,
        taps,
        scalars,
        doc_ref[0:1],
        gain_ref[...],
        grad_ref[...],
        [(inverse_ref[0, 0], inverse_ref[0, 1]), (inverse_ref[0, 2], inverse_ref[0, 3])],
        [update_ref[0, 0], update_ref[0, 1]],
        out_ref[...],
    )
    for group in range(5):
        tap_grad_ref[:, spans[group]] = tap_grads[group]
    projected_grad = jnp.concatenate(piece_grads, axis=1)
    in_grad_ref[...] = dims(normed_ref[...], projected_grad, 0, 0).astype(low)
    normed_grad_ref[...] += dims(projected_grad, in_ref[...], 1, 1)
    lane = lane_of(logit_grad_ref.shape)
    spread = jnp.zeros(logit_grad_ref.shape, f32)
    for index, entry in enumerate(logit_grads):
        spread = spread + jnp.where(lane == index * heads + head, entry, 0.0)
    logit_grad_ref[...] += spread
    line = lane_of((1, width))
    sums_ref[0:1] += jnp.where(line == head, log_grad, 0.0)
    sums_ref[1:2] += jnp.where(line == head, bias_grad, 0.0)
    sums_ref[2:3] += gain_grad

    @pl.when(head == heads - 1)
    def _():
        logit_low = logit_grad_ref[...].astype(low)
        small_grad_ref[...] = dims(normed_ref[...], logit_low, 0, 0).astype(low)
        grad = normed_grad_ref[...] + dims(logit_low, small_ref[...], 1, 1)
        inputs = token_ref[...].astype(f32)
        scale = rms_scale(inputs)
        normed = inputs * scale
        gain_grads = [jnp.sum(grad * normed, axis=0, keepdims=True), ffn_gain_ref[...]]
        shard_rows = in_ref.shape[0] // line_ref.shape[0]
        pack_lines(line_ref, tap_grad_ref[...], gain_grads, channels, shard_rows)
        line_grad_ref[...] = line_ref[...].astype(low)
        weighted = grad * row_ref[0:1]
        back = scale * (weighted - normed * jnp.mean(weighted * normed, axis=1, keepdims=True))
        token_grad_ref[...] = (middle_ref[...] + back).astype(low)
        if count:
            for step, place_at in enumerate(calls):
                if place_at >= heads:
                    tick(step)
            finish()


def whole_spec(shape):
    return pl.BlockSpec(shape, lambda h: (0,) * len(shape))


def head_spec(*shape):
    return pl.BlockSpec((1,) + shape, lambda h: (h,) + (0,) * len(shape))


def col_spec(rows, width):
    return pl.BlockSpec((rows, width), lambda h: (0, h))


HBM = pl.BlockSpec(memory_space=pltpu.HBM)
VMEM_LIMIT = 56 << 20


def shared_specs(seq_len, model_width, heads, width):
    return [
        whole_spec((seq_len, model_width)),
        whole_spec((1, heads)),
        whole_spec((1, heads)),
        whole_spec((1, width)),
    ]


def weight_specs(seq_len, model_width, heads, width):
    return [
        col_spec(model_width, 6 * width),
        whole_spec((model_width, 128)),
        whole_spec((4, heads * 5 * width)),
        whole_spec((8, model_width)),
        whole_spec((seq_len, 8)),
        whole_spec((8, seq_len)),
    ]


def saved_specs(seq_len, model_width, width):
    return [
        head_spec(seq_len, 6 * width),
        head_spec(4, seq_len, seq_len),
        head_spec(2, seq_len, width),
        col_spec(seq_len, width),
        whole_spec((seq_len, 128)),
        whole_spec((seq_len, model_width)),
    ]


def saved_shapes(seq_len, model_width, heads, width):
    return [
        jax.ShapeDtypeStruct((heads, seq_len, 6 * width), f32),
        jax.ShapeDtypeStruct((heads, 4, seq_len, seq_len), low),
        jax.ShapeDtypeStruct((heads, 2, seq_len, width), f32),
        jax.ShapeDtypeStruct((seq_len, heads * width), f32),
        jax.ShapeDtypeStruct((seq_len, 128), f32),
        jax.ShapeDtypeStruct((seq_len, model_width), low),
    ]


def plain_forward(shared, weights, heads):
    seq_len, model_width = shared[0].shape
    width = shared[-1].shape[1]
    outs = pl.pallas_call(
        functools.partial(plain_forward_kernel, heads),
        grid=(heads,),
        in_specs=shared_specs(seq_len, model_width, heads, width)
        + weight_specs(seq_len, model_width, heads, width),
        out_specs=[col_spec(seq_len, width)] + saved_specs(seq_len, model_width, width),
        out_shape=[jax.ShapeDtypeStruct((seq_len, heads * width), low)]
        + saved_shapes(seq_len, model_width, heads, width),
        compiler_params=pltpu.CompilerParams(vmem_limit_bytes=VMEM_LIMIT),
        name="plain_forward",
    )(*shared, *weights)
    return outs[0], outs[1:]


def mixer_forward(sizes, streams, calls, shared, doc_row, shards, heads, channels, call):
    seq_len, model_width = shared[0].shape
    width = shared[-1].shape[1]
    count = len(shards)
    total = slots(sizes, streams)
    shape = tuple(sizes[dim] for dim in "zyxc")
    outs = pl.pallas_call(
        functools.partial(forward_kernel, sizes, streams, count, calls, heads, channels),
        grid=(heads,),
        in_specs=shared_specs(seq_len, model_width, heads, width)[:1]
        + [whole_spec((1, seq_len))]
        + shared_specs(seq_len, model_width, heads, width)[1:]
        + [HBM] * count,
        out_specs=[col_spec(seq_len, width)]
        + saved_specs(seq_len, model_width, width)
        + weight_specs(seq_len, model_width, heads, width)[2:]
        + [HBM] * count,
        out_shape=[jax.ShapeDtypeStruct((seq_len, heads * width), low)]
        + saved_shapes(seq_len, model_width, heads, width)
        + [
            jax.ShapeDtypeStruct((4, heads * 5 * width), f32),
            jax.ShapeDtypeStruct((8, model_width), f32),
            jax.ShapeDtypeStruct((seq_len, 8), f32),
            jax.ShapeDtypeStruct((8, seq_len), f32),
        ]
        + [jax.ShapeDtypeStruct(shape + shard.shape, shard.dtype) for shard in shards],
        scratch_shapes=[
            pltpu.VMEM(shape + (shards[0].shape[0], 6 * width), low),
            pltpu.VMEM(shape + shards[1].shape, low),
            pltpu.VMEM(shape + shards[2].shape, low),
            pltpu.SemaphoreType.DMA((3,)),
            pltpu.SemaphoreType.DMA((total,)),
            pltpu.SemaphoreType.DMA((total,)),
            pltpu.SemaphoreType.DMA((count,)),
        ],
        compiler_params=pltpu.CompilerParams(
            vmem_limit_bytes=44 << 20, collective_id=call, has_side_effects=True
        ),
        name="mixer_forward",
    )(shared[0], doc_row, *shared[1:], *shards)
    fulls = [out.reshape((-1, out.shape[-1])) for out in outs[11:]]
    return outs[0], outs[1:7], fulls[:2] + list(outs[7:11]), fulls[3:]


def mixer_backward(
    sizes, streams, calls, shared, weights, grad, saved, middle_grad, ffn_gain, factors, layout, call
):
    seq_len, model_width = shared[0].shape
    heads, channels, devices, line_width = layout
    width = shared[-1].shape[1]
    count = len(factors)
    line_shape = (devices, 16, line_width)
    scratch = [
        pltpu.VMEM((seq_len, 128), f32),
        pltpu.VMEM((seq_len, model_width), f32),
        pltpu.VMEM((4, heads * 5 * width), f32),
        pltpu.VMEM(line_shape, f32),
    ]
    extra = {}
    outs_cols = [sum(right.shape[1] for right in entry[1:]) for entry in factors]
    if count:
        extra = dict(collective_id=call, has_side_effects=True)
        rows = model_width // devices
        scratch = scratch + scatter_buffers(sizes, streams, [rows] * count, False)
        scratch.append(pltpu.VMEM(staging_shape(sizes, streams, rows), low))
    flat = [factor for entry in factors for factor in entry]
    once = pl.Buffered(1)
    outs = pl.pallas_call(
        functools.partial(
            backward_kernel, sizes, streams, [len(entry) for entry in factors], calls, heads, channels
        ),
        grid=(heads,),
        in_specs=shared_specs(seq_len, model_width, heads, width)
        + weight_specs(seq_len, model_width, heads, width)
        + [col_spec(seq_len, width)]
        + saved_specs(seq_len, model_width, width)
        + [pl.BlockSpec((seq_len, model_width), lambda h: (0, 0), pipeline_mode=once)]
        + [whole_spec((1, model_width))]
        + [pl.BlockSpec(entry.shape, lambda h: (0, 0), pipeline_mode=once) for entry in flat],
        out_specs=[
            col_spec(model_width, 6 * width),
            whole_spec(line_shape),
            whole_spec((model_width, 128)),
            whole_spec((8, width)),
            whole_spec((seq_len, model_width)),
        ]
        + [whole_spec((model_width // devices, cols)) for cols in outs_cols],
        out_shape=[
            jax.ShapeDtypeStruct((model_width, heads * 6 * width), low),
            jax.ShapeDtypeStruct(line_shape, low),
            jax.ShapeDtypeStruct((model_width, 128), low),
            jax.ShapeDtypeStruct((8, width), f32),
            jax.ShapeDtypeStruct((seq_len, model_width), low),
        ]
        + [jax.ShapeDtypeStruct((model_width // devices, cols), f32) for cols in outs_cols],
        scratch_shapes=scratch,
        compiler_params=pltpu.CompilerParams(vmem_limit_bytes=VMEM_LIMIT, **extra),
        name="mixer_backward",
    )(*shared, *weights, grad, *saved, middle_grad, ffn_gain, *flat)
    return outs[:5], outs[5:]


def rms_parts(inputs):
    scale = lax.rsqrt(jnp.mean(inputs * inputs, axis=-1, keepdims=True) + norm_eps)
    return inputs * scale, scale


def rms_back(normed, scale, gain_row, grad):
    weighted = grad * gain_row
    return (
        scale * (weighted - normed * jnp.mean(weighted * normed, axis=-1, keepdims=True)),
        jnp.sum(grad * normed, axis=0),
    )


def gathered(shard):
    return lax.all_gather(shard, AXES, axis=0, tiled=True)


def scattered(whole):
    return lax.psum_scatter(whole, AXES, scatter_dimension=0, tiled=True)


MESH = pl.DeviceIdType.MESH


def grid_of(wide, narrow):
    pair = 2 if narrow % 2 == 0 else 1
    half = 2 if wide % 2 == 0 else 1
    return {"z": wide // half, "y": half, "x": narrow // pair, "c": pair}


def place(sizes):
    wide, narrow = lax.axis_index("wide"), lax.axis_index("narrow")
    return {
        "z": wide // sizes["y"],
        "y": lax.rem(wide, sizes["y"]),
        "x": narrow // sizes["c"],
        "c": lax.rem(narrow, sizes["c"]),
    }


def device(sizes, at):
    return (at["z"] * sizes["y"] + at["y"], at["x"] * sizes["c"] + at["c"])


def moved(sizes, at, dim, step):
    other = dict(at)
    other[dim] = lax.rem(at[dim] + step, sizes[dim])
    return other


def meet(sizes, me):
    barrier = pltpu.get_barrier_semaphore()
    count = 0
    for dim in "zyxc":
        for step in range(1, sizes[dim]):
            pl.semaphore_signal(
                barrier,
                inc=1,
                device_id=device(sizes, moved(sizes, me, dim, step)),
                device_id_type=MESH,
            )
            count += 1
    pl.semaphore_wait(barrier, count)


def slots(sizes, streams):
    return sum(sizes[dim] - 1 for stream in streams for dim in stream[3])


def cut(array, cols, chunks, share, orders, first_lag, per_lag):
    units = cols // 128
    streams, start = [], 0
    edges = []
    for chunk in range(chunks):
        edges += [(chunk + share) / chunks, (chunk + 1) / chunks]
    for index, edge in enumerate(edges):
        stop = round(edge * units)
        if stop > start:
            lag = first_lag + (index // 2) // per_lag
            streams.append((array, start * 128, (stop - start) * 128, orders[index % 2], lag))
        start = stop
    return streams


def agenda(streams, order):
    last = max(stream[4] for stream in streams) + 5
    return [
        [
            (index, phase)
            for phase in order
            for index, stream in enumerate(streams)
            if step - stream[4] == phase
        ]
        for step in range(last)
    ]


def slot_table(sizes, streams):
    table, used = {}, 0
    for index, stream in enumerate(streams):
        for phase in range(4):
            table[index, phase] = used
            used += sizes[stream[3][phase]] - 1
    return table


def gather_steps(sizes, streams, shards, fulls, sems):
    send_sem, recv_sem, local_sem = sems
    table = slot_table(sizes, streams)
    plan = agenda(streams, GATHER_STEPS)

    def local(me):
        return [
            pltpu.make_async_copy(
                shard, full.at[me["z"], me["y"], me["x"], me["c"]], local_sem.at[index]
            )
            for index, (shard, full) in enumerate(zip(shards, fulls))
        ]

    def copies(me, index, phase):
        array, col, width, order, lag = streams[index]
        dim = order[phase]
        block = tuple(slice(None) if d in order[:phase] else me[d] for d in "zyxc")
        target = fulls[array].at[block + (slice(None), pl.ds(col, width))]
        source = shards[array].at[:, pl.ds(col, width)] if phase == 0 else target
        return [
            pltpu.make_async_remote_copy(
                src_ref=source,
                dst_ref=target,
                send_sem=send_sem.at[table[index, phase] + hop - 1],
                recv_sem=recv_sem.at[table[index, phase] + hop - 1],
                device_id=device(sizes, moved(sizes, me, dim, hop)),
                device_id_type=MESH,
            )
            for hop in range(1, sizes[dim])
        ]

    def tick(step):
        me = place(sizes)
        if step == 0:
            for copy in local(me):
                copy.start()
            meet(sizes, me)
        if step == 1:
            for copy in local(me):
                copy.wait()
        for index, phase in plan[step]:
            if phase > 0:
                for copy in copies(me, index, phase - 1):
                    copy.wait_recv()
            if phase < 4:
                for copy in copies(me, index, phase):
                    copy.start()

    def finish():
        me = place(sizes)
        for index in range(len(streams)):
            for phase in range(4):
                for copy in copies(me, index, phase):
                    copy.wait_send()

    return tick, finish


def gather_kernel(sizes, streams, count, *refs):
    tick, finish = gather_steps(
        sizes, streams, refs[:count], refs[count : 2 * count], refs[2 * count :]
    )
    for step in range(len(agenda(streams, GATHER_STEPS))):
        tick(step)
    finish()


def gather(sizes, streams, shards, call):
    count = len(shards)
    total = slots(sizes, streams)
    shape = tuple(sizes[dim] for dim in "zyxc")
    outs = pl.pallas_call(
        functools.partial(gather_kernel, sizes, streams, count),
        out_shape=[jax.ShapeDtypeStruct(shape + shard.shape, shard.dtype) for shard in shards],
        in_specs=[HBM] * count,
        out_specs=[HBM] * count,
        scratch_shapes=[
            pltpu.SemaphoreType.DMA((total,)),
            pltpu.SemaphoreType.DMA((total,)),
            pltpu.SemaphoreType.DMA((count,)),
        ],
        compiler_params=pltpu.CompilerParams(collective_id=call, has_side_effects=True),
        name="weights_gather",
    )(*shards)
    return [out.reshape((-1, out.shape[-1])) for out in outs]


def scatter_buffers(sizes, streams, rows, stored):
    shape = tuple(sizes[dim] for dim in "zyx")
    total = slots(sizes, streams)
    buffers = [
        pltpu.SemaphoreType.DMA((total,)),
        pltpu.SemaphoreType.DMA((total,)),
        pltpu.SemaphoreType.DMA((len(streams),)),
    ]
    for array, col, width, order, lag in streams:
        tail = (rows[array], width)
        if stored:
            buffers.append(pltpu.VMEM(shape + tail, low))
        for phase in range(4):
            kept = tuple(sizes[dim] for dim in "zyx" if dim not in order[: phase + 1])
            buffers.append(pltpu.VMEM((sizes[order[phase]] - 1,) + kept + tail, low))
    return buffers


def group_of(streams, lag):
    return [index for index, stream in enumerate(streams) if stream[4] == lag]


def staging_shape(sizes, streams, rows):
    widest = max(
        sum(streams[index][2] for index in group_of(streams, lag))
        for lag in range(1 + max(stream[4] for stream in streams))
    )
    return tuple(sizes[dim] for dim in "zyxc") + (rows, widest)


def scatter_steps(sizes, streams, terms, sums, refs, heads=None):
    send_sem, recv_sem, local_sem = refs[:3]
    computed = isinstance(terms[0], tuple)
    refs = list(refs[3:])
    held, got = [], {}
    for index in range(len(streams)):
        if not computed:
            held.append(refs.pop(0))
        for phase in range(4):
            got[index, phase] = refs.pop(0)
        if computed:
            held.append(got[index, 0].at[0])
    staging = refs.pop(0) if computed else None
    table = slot_table(sizes, streams)
    plan = agenda(streams, SCATTER_STEPS)

    def part(index, core):
        array, col, width, order, lag = streams[index]
        if computed:
            first = min(streams[other][1] for other in group_of(streams, lag))
            return staging.at[:, :, :, core, :, pl.ds(col - first, width)]
        return terms[array].at[:, :, :, core, :, pl.ds(col, width)]

    def produce(lag):
        group = group_of(streams, lag)
        array = streams[group[0]][0]
        first = min(streams[index][1] for index in group)
        left_ref, rights = terms[array][0], terms[array][1:]
        share = rights[0].shape[1]
        flat = staging.reshape(-1, *staging.shape[4:])
        rows = staging.shape[4]
        block = 256
        for index in group:
            col, width = streams[index][1], streams[index][2]
            inner = col % share
            right = rights[col // share][:, inner : inner + width]
            assert inner + width <= share
            for start in range(0, left_ref.shape[1], block):
                product = dims(left_ref[:, start : start + block], right, 0, 0).astype(low)
                flat[start // rows : (start + block) // rows, :, col - first : col - first + width] = (
                    product.reshape(block // rows, rows, width)
                )

    def load(me, index):
        return pltpu.make_async_copy(part(index, me["c"]), held[index], local_sem.at[index])

    def copies(me, index, phase):
        array, col, width, order, lag = streams[index]
        dim = order[phase]
        found = []
        for hop in range(1, sizes[dim]):
            to = moved(sizes, me, dim, hop)
            if phase == 0:
                source = part(index, to["c"])
            else:
                block = tuple(
                    me[d] if d in order[:phase] else (to[d] if d == dim else slice(None))
                    for d in "zyx"
                )
                source = held[index].at[block]
            found.append(
                pltpu.make_async_remote_copy(
                    src_ref=source,
                    dst_ref=got[index, phase].at[hop - 1],
                    send_sem=send_sem.at[table[index, phase] + hop - 1],
                    recv_sem=recv_sem.at[table[index, phase] + hop - 1],
                    device_id=device(sizes, to),
                    device_id_type=MESH,
                )
            )
        return found

    def combine(me, index, phase):
        array, col, width, order, lag = streams[index]
        kept = [d for d in "zyx" if d not in order[: phase + 1]]
        total = 1
        for d in kept:
            total *= sizes[d]

        def body(flat, carry):
            at, rest = dict(me), flat
            for d in reversed(kept):
                at[d] = lax.rem(rest, sizes[d])
                rest = rest // sizes[d]
            where = tuple(at[d] for d in "zyx")
            inner = tuple(at[d] for d in kept)
            value = held[index][where]
            if computed and phase == 0:
                held[index][where] = value + part(index, me["c"])[where]
                return carry
            others = [got[index, phase][(hop,) + inner] for hop in range(sizes[order[phase]] - 1)]
            if phase == 3 or len(others) > 1:
                value = value.astype(f32)
                for other in others:
                    value = value + other.astype(f32)
            else:
                value = value + others[0]
            if phase < 3:
                held[index][where] = value.astype(low)
            elif heads is None or array > 0:
                sums[array][:, pl.ds(col, width)] = value
            else:
                for tile in range(width // 128):
                    head, group = divmod(col // 128 + tile, 6)
                    target = (group * heads + head) * 128
                    sums[array][:, target : target + 128] = value[:, tile * 128 : tile * 128 + 128]
            return carry

        if total == 1:
            body(0, 0)
        else:
            lax.fori_loop(0, total, body, 0)

    def tick(step):
        me = place(sizes)
        if step == 0:
            meet(sizes, me)
        fresh = group_of(streams, step)
        if computed:
            for index in group_of(streams, step - 1):
                for copy in copies(me, index, 0):
                    copy.wait_recv()
                combine(me, index, 0)
                for copy in copies(me, index, 0):
                    copy.wait_send()
            if fresh:
                produce(step)
        elif step == 0:
            for index in range(len(streams)):
                load(me, index).start()
        for index, phase in plan[step]:
            if phase > (1 if computed else 0):
                for copy in copies(me, index, phase - 1):
                    copy.wait_recv()
                if phase == 1:
                    load(me, index).wait()
                combine(me, index, phase - 1)
            if phase < 4:
                for copy in copies(me, index, phase):
                    copy.start()

    def finish():
        me = place(sizes)
        for index in range(len(streams)):
            for phase in range(1 if computed else 0, 4):
                for copy in copies(me, index, phase):
                    copy.wait_send()

    return tick, finish


def small_buffers(sizes, shape):
    return [pltpu.VMEM((2,) + shape, f32) for _ in "cxy"] + [
        pltpu.VMEM((sizes["z"],) + shape, f32),
        pltpu.SemaphoreType.DMA((4, sizes["z"])),
        pltpu.SemaphoreType.DMA((4, sizes["z"])),
    ]


def small_steps(sizes, small, total, refs):
    boxes, lanes, small_send, small_recv = refs[:3], refs[3], refs[4], refs[5]

    def copies(me, phase):
        dim = "cxyz"[phase]
        source = small if phase == 0 else boxes[phase - 1].at[1]
        source = lanes.at[me["z"]] if dim == "z" else source
        return [
            pltpu.make_async_remote_copy(
                src_ref=source,
                dst_ref=lanes.at[me["z"]] if dim == "z" else boxes[phase].at[0],
                send_sem=small_send.at[phase, hop],
                recv_sem=small_recv.at[phase, hop],
                device_id=device(sizes, moved(sizes, me, dim, hop)),
                device_id_type=MESH,
            )
            for hop in range(1, sizes[dim])
        ]

    def tick(step):
        me = place(sizes)
        if step > 0:
            for copy in copies(me, step - 1):
                copy.wait_recv()
            if step < 4:
                mine = small[...] if step == 1 else boxes[step - 2][1]
                boxes[step - 1][1] = mine + boxes[step - 1][0]
            else:
                value = lanes[0]
                for index in range(1, sizes["z"]):
                    value = value + lanes[index]
                total[...] = value
        if step < 4:
            if step == 3:
                lanes[me["z"]] = boxes[2][1]
            for copy in copies(me, step):
                copy.start()

    def finish():
        me = place(sizes)
        for phase in range(4):
            for copy in copies(me, phase):
                copy.wait_send()

    return tick, finish


def scatter_kernel(sizes, streams, count, heads, *refs):
    terms, small = refs[:count], refs[count]
    sums, total = refs[count + 1 : 2 * count + 1], refs[2 * count + 1]
    rest = refs[2 * count + 2 :]
    tick, finish = scatter_steps(sizes, streams, terms, sums, rest[:-6], heads)
    small_tick, small_finish = small_steps(sizes, small, total, rest[-6:])
    for step in range(len(agenda(streams, SCATTER_STEPS))):
        tick(step)
        if step < 5:
            small_tick(step)
    finish()
    small_finish()


def scatter(sizes, streams, terms, small, heads, call):
    count = len(terms)
    shape = tuple(sizes[dim] for dim in "zyxc")
    devices = shape[0] * shape[1] * shape[2] * shape[3]
    blocks = [
        term.reshape(shape + (term.shape[0] // devices, term.shape[1])) for term in terms
    ]
    buffers = scatter_buffers(sizes, streams, [block.shape[4] for block in blocks], True)
    vmem = pl.BlockSpec(memory_space=pltpu.VMEM)
    return pl.pallas_call(
        functools.partial(scatter_kernel, sizes, streams, count, heads),
        out_shape=[
            jax.ShapeDtypeStruct((block.shape[4], block.shape[5]), f32) for block in blocks
        ]
        + [jax.ShapeDtypeStruct(small.shape, f32)],
        in_specs=[HBM] * count + [vmem],
        out_specs=[vmem] * (count + 1),
        scratch_shapes=buffers + small_buffers(sizes, small.shape),
        compiler_params=pltpu.CompilerParams(
            collective_id=call, has_side_effects=True, vmem_limit_bytes=44 << 20
        ),
        name="grads_scatter",
    )(*blocks, small)


GATHER_STEPS = (0, 1, 2, 3, 4)
SCATTER_STEPS = (0, 1, 3, 2, 4)
GATHER_ORDERS = ("zxyc", "yzxc")
SCATTER_ORDERS = ("cyxz", "cxzy")


BACKWARD_PLAN = ((2, 0, 1), (4, 2, 1), (1, 6, 1))
BACKWARD_CALLS = (0, 1, 2, 3, 4, 5, 6, 7, 8, 8, 8)
FORWARD_PLAN = ((4, 0, 1), (1, 0, 1), (1, 0, 1), (1, 4, 1), (4, 4, 1), (2, 8, 1))
FORWARD_CALLS = (0, 0, 0, 0, 0, 2, 4, 6, 8, 10, 12, 14, 16, 16)


def planned(terms, orders, chunks, share=0.64):
    streams = []
    for index, (count, lag, per_lag) in enumerate(chunks):
        streams += cut(index, terms[index].shape[1], count, share, orders, lag, per_lag)
    return streams


def per_device(
    sizes,
    tokens,
    doc_ids,
    attn_gain,
    mixer_in,
    mixer_small,
    conv_weight,
    decay_log,
    decay_bias,
    out_gain,
    mixer_out,
    ffn_gain,
    ffn_in,
    ffn_out,
    out_grad,
):
    row_count, seq_len, model_width = tokens.shape
    heads, width = decay_log.shape[0], out_gain.shape[0]
    shard_rows = mixer_in.shape[0]
    small_cols = mixer_small.shape[1]
    channels = conv_weight.shape[0]
    devices = model_width // shard_rows
    ff_width = ffn_out.shape[0]
    own = (
        shard_rows % 16 == 0
        and row_count == 1
        and sizes["x"] == 2
        and sizes["y"] == 2
        and sizes["c"] == 2
    )
    in_shard = (
        mixer_in.astype(low)
        .reshape(shard_rows, 6, heads, width)
        .transpose(0, 2, 1, 3)
        .reshape(shard_rows, -1)
    )
    small_shard = jnp.pad(mixer_small.astype(low), ((0, 0), (0, 128 - small_cols)))
    line_width = channels + (-channels % 128)
    lines_shard = jnp.concatenate(
        [
            jnp.pad(conv_weight.astype(low).T, ((0, 0), (0, line_width - channels))),
            jnp.pad(
                jnp.stack([attn_gain, ffn_gain]).astype(low), ((0, 10), (0, line_width - shard_rows))
            ),
        ]
    )
    out_shard, ffn_out_shard = mixer_out.astype(low).T, ffn_out.astype(low).T
    late_shards = [out_shard, ffn_in.astype(low), ffn_out_shard]
    early_shards = [in_shard, small_shard, lines_shard]
    each = [
        [tokens[index], decay_log[None], decay_bias[None], out_gain[None]]
        for index in range(row_count)
    ]
    if own:
        shards = early_shards + late_shards
        mixed, saved, weights, late_full = mixer_forward(
            sizes,
            planned(shards, GATHER_ORDERS, FORWARD_PLAN),
            FORWARD_CALLS,
            each[0],
            doc_ids,
            shards,
            heads,
            channels,
            1,
        )
        saves, weights = [saved], [weights]
        ffn_row = weights[0][3][1:2]
    else:
        in_full, small_full, lines = [gathered(shard) for shard in early_shards]
        lines = lines.reshape(devices, 16, line_width).astype(f32)
        taps = lines[:, :4, :channels].transpose(1, 0, 2).reshape(4, -1)
        rows = lines[:, 4:6, :shard_rows].transpose(1, 0, 2).reshape(2, model_width)
        ffn_row = rows[1:2]
        weights = []
        for index in range(row_count):
            doc = doc_ids[index].astype(f32)
            before = [
                jnp.concatenate([jnp.full((distance,), -1.0), doc[:-distance]])
                for distance in (1, 2, 3)
            ]
            marks = [doc] + [jnp.where(entry == doc, 1.0, 0.0) for entry in before]
            weights.append(
                [
                    in_full,
                    small_full,
                    taps,
                    jnp.pad(rows, ((0, 6), (0, 0))),
                    jnp.pad(jnp.stack(marks, axis=1), ((0, 0), (0, 4))),
                    jnp.broadcast_to(doc[None], (8, seq_len)),
                ]
            )
        done = [plain_forward(*entry, heads) for entry in zip(each, weights)]
        mixed = jnp.concatenate([entry[0] for entry in done])
        saves = [entry[1] for entry in done]
        late_full = [gathered(shard) for shard in late_shards]
    out_t, ffn_in_full, ffn_out_t = late_full

    inputs = tokens.reshape(row_count * seq_len, model_width).astype(f32)
    middle = inputs + dims(mixed, out_t, 1, 1)
    ffn_normed, ffn_scale = rms_parts(middle)
    ffn_rows = (ffn_normed * ffn_row).astype(low)
    gate_up = jnp.dot(ffn_rows, ffn_in_full, preferred_element_type=f32)
    gate, up = gate_up[:, :ff_width], gate_up[:, ff_width:]
    slope = jax.nn.sigmoid(gate)
    hidden = (gate * slope * up).astype(low)
    result = middle + dims(hidden, ffn_out_t, 1, 1)
    grad_low = out_grad.reshape(row_count * seq_len, model_width)
    hidden_grad = jnp.dot(grad_low, ffn_out_t, preferred_element_type=f32)
    gate_grad = (hidden_grad * up * slope * (1.0 + gate * (1.0 - slope))).astype(low)
    up_grad = (hidden_grad * gate * slope).astype(low)
    gate_up_grad = jnp.concatenate([gate_grad, up_grad], axis=1)
    rows_grad = dims(gate_up_grad, ffn_in_full, 1, 1)
    middle_norm_grad, ffn_gain_term = rms_back(ffn_normed, ffn_scale, ffn_row, rows_grad)
    middle_grad = grad_low.astype(f32) + middle_norm_grad
    branch_grad = middle_grad.astype(low)
    mixed_grad = jnp.dot(branch_grad, out_t, preferred_element_type=f32)
    factors = [(grad_low, hidden), (ffn_rows, gate_grad, up_grad), (branch_grad, mixed)]
    layout = (heads, channels, devices, line_width)
    ffn_gain_line = ffn_gain_term[None]
    if own:
        late = planned([ffn_out_t, ffn_in_full, out_t], SCATTER_ORDERS, BACKWARD_PLAN)
        grads, late_sums = mixer_backward(
            sizes,
            late,
            BACKWARD_CALLS,
            each[0],
            weights[0],
            mixed_grad,
            saves[0],
            middle_grad,
            ffn_gain_line,
            factors,
            layout,
            3,
        )
        grads = [grads]
    else:
        grads = []
        for index, entry in enumerate(each):
            rows = slice(index * seq_len, (index + 1) * seq_len)
            share = ffn_gain_line if index == 0 else jnp.zeros_like(ffn_gain_line)
            grads.append(
                mixer_backward(
                    sizes,
                    [],
                    (),
                    entry,
                    weights[index],
                    mixed_grad[rows],
                    saves[index],
                    middle_grad[rows],
                    share,
                    [],
                    layout,
                    3,
                )[0]
            )
        late_sums = [
            scattered(dims(left, jnp.concatenate(right, axis=1), 0, 0).astype(low)).astype(f32)
            for left, *right in factors
        ]
    in_term, lines_term, small_term, small = [
        functools.reduce(jnp.add, [entry[index] for entry in grads]) for index in range(4)
    ]
    input_grad = jnp.stack([entry[4] for entry in grads])
    lines_term = lines_term.reshape(devices * 16, line_width)
    early_terms = [in_term, small_term, lines_term]
    if own:
        early = planned(early_terms, SCATTER_ORDERS, ((8, 0, 2), (1, 0, 1), (1, 0, 1)), 0.7)
        in_sum, small_sum, lines_sum, small = scatter(
            sizes, early, early_terms, small, heads, 4
        )
    else:
        in_sum, small_sum, lines_sum = [scattered(term).astype(f32) for term in early_terms]
        small = lax.psum(small, AXES)
        in_sum = (
            in_sum.reshape(shard_rows, heads, 6, width)
            .transpose(0, 2, 1, 3)
            .reshape(shard_rows, -1)
        )
    ffn_out_sum, ffn_in_sum, out_sum = late_sums
    outputs = result.astype(low).reshape(row_count, seq_len, model_width)
    return (
        outputs,
        input_grad,
        lines_sum[4, :shard_rows],
        in_sum,
        small_sum[:, :small_cols],
        lines_sum[:4, :channels].T,
        small[0, :heads],
        small[1, :heads],
        small[2],
        out_sum.T,
        lines_sum[5, :shard_rows],
        ffn_in_sum,
        ffn_out_sum.T,
    )


def solution(mesh):
    both = P(AXES)
    line = P(None, AXES)
    in_specs = (both, both, both, both, both, both, P(), P(), P(), line, both, both, line, both)
    out_specs = (both, both, both, both, both, both, P(), P(), P(), line, both, both, line)
    sizes = grid_of(mesh.shape["wide"], mesh.shape["narrow"])
    return jax.shard_map(
        functools.partial(per_device, sizes),
        mesh=mesh, in_specs=in_specs, out_specs=out_specs, check_vma=False
    )
```
